32 devices in a mesh: groups: 1, rows: 32 (over z, y, x, core).
Axes of the slice: x: 2, y: 2, z: 4, core: 2. Of those that a mesh axis runs over, the one named last changes fastest.
Arguments:
- tokens: bfloat16 [384, 8192], P(('groups', 'rows')), may hold values from -6 to 6
- gate_weight: bfloat16 [8192, 14336], P('rows'), may hold values from -0.0625 to 0.0625
- up_weight: bfloat16 [8192, 14336], P('rows'), may hold values from -0.0625 to 0.0625
- skew_params: float32 [2, 2, 128, 64, 64], P(None, None, 'rows'), may hold values from -0.3125 to 0.3125
- section_bits: int32 [2, 13], replicated, may hold values from 0 to 12, each once within a row
- upstream: bfloat16 [384, 14336], P('groups', 'rows'), may hold values from -0.3125 to 0.3125
Outputs:
- activation: bfloat16 [384, 14336], P('groups', 'rows')
- skew_grad: float32 [2, 2, 128, 64, 64], P('groups', None, 'rows')
The draws below stay inside these ranges and needn't reach their ends.
Inputs may be any that keep to these rules, and one draw needn't show every extreme that they name: Each row of section_bits names every one of the 13 bit positions once.
All inputs are finite; a program needn't handle non-finite values.
Results may differ from the reference program's by a relative error of at most 0.0093.
Values may be sent and summed in bfloat16 or wider, within the bound.
A program may use at most 192 MiB of HBM per device.

```python
import jax
import jax.numpy as jnp
from jax import lax

D = 8192
FF = 14336
LOG_D = 13
BLOCK = 64
SECTIONS = 2
MATS = 2
TOKENS = 384
NB = 128


def block_levels(key, shape, shards, least, largest):
    factor_of = 1.0
    for position, parts in shards:
        draws = jax.random.uniform(jax.random.fold_in(jax.random.fold_in(key, 6), position), (parts,), jnp.float32, least / len(shards), largest / len(shards))
        factor_of = factor_of * jnp.repeat(jnp.exp(draws), shape[position] // parts).reshape((-1,) + (1,) * (len(shape) - 1 - position))
    return factor_of


def noise(rng, shape, width, most, split=(), held_as=jnp.bfloat16):
    level = block_levels(rng, shape, split, -0.22, 0.18) if split else 1.0
    drawn = jax.random.normal(rng, shape, jnp.float32) * width * level
    return jnp.minimum(jnp.maximum(drawn, -most), most).astype(held_as)


def setup_inputs(seed: int = 0, part: int = 0) -> dict:
    key_list = jax.random.split(jax.random.key(seed), 7)
    part_splits = jax.random.split(jax.random.fold_in(key_list[6], part), 7)
    tokens = noise(part_splits[0], (TOKENS, D), 1.0, 6.0, ((0, 32),))
    gate_weight = noise(key_list[1], (D, FF), D ** -0.5, 0.0625, ((0, 32),))
    up_weight = noise(key_list[2], (D, FF), D ** -0.5, 0.0625, ((0, 32),))
    skew_params = noise(key_list[3], (MATS, SECTIONS, NB, BLOCK, BLOCK), 0.05, 0.3125, ((2, 32),), jnp.float32)
    section_bits = jax.vmap(lambda own: jax.random.permutation(own, LOG_D))(jax.random.split(key_list[4], SECTIONS)).reshape((SECTIONS, LOG_D)).astype(jnp.int32)
    upstream = noise(part_splits[5], (TOKENS, FF), 0.05, 0.3125, ((1, 32),))
    return {"tokens": tokens, "gate_weight": gate_weight, "up_weight": up_weight, "skew_params": skew_params, "section_bits": section_bits, "upstream": upstream}


def cayley(skew_blocks):
    extent = skew_blocks.shape[-1]
    identity = jnp.eye(extent, dtype=skew_blocks.dtype)
    generator = skew_blocks - jnp.swapaxes(skew_blocks, -1, -2)
    minus_part = identity - generator
    squared = jnp.einsum('...ij,...jk->...ik', minus_part, minus_part, precision=lax.Precision.HIGHEST)
    normal = identity - jnp.einsum('...ij,...jk->...ik', generator, generator, precision=lax.Precision.HIGHEST)
    return jnp.linalg.solve(normal, squared)

def slot_order(section_row, extent):
    positions = jnp.arange(extent, dtype=jnp.int32)
    places = jnp.arange(section_row.shape[0], dtype=jnp.int32)
    digits = jnp.right_shift(positions[:, None], places[None, :]) & 1
    return lax.optimization_barrier(jnp.sum(jnp.left_shift(digits, section_row[None, :]), axis=1)).astype(jnp.int32)

def inverse_order(section_row, extent):
    positions = jnp.arange(extent, dtype=jnp.int32)
    places = jnp.arange(section_row.shape[0], dtype=jnp.int32)
    digits = jnp.right_shift(positions[:, None], section_row[None, :]) & 1
    return lax.optimization_barrier(jnp.sum(jnp.left_shift(digits, places[None, :]), axis=1)).astype(jnp.int32)

def rotate_columns(columns, rotation, orders, inverses):
    kept_inputs = []
    current = columns
    block_count = rotation.shape[1]
    col_count = columns.shape[1]
    for section_at in range(len(orders)):
        permuted = current[orders[section_at]].reshape(block_count, -1, col_count)
        mixed_rows = jnp.einsum('kji,kic->kjc', rotation[section_at].astype(jnp.float32), permuted.astype(jnp.float32)).astype(jnp.bfloat16)
        kept_inputs.append(permuted)
        current = mixed_rows.reshape(current.shape)[inverses[section_at]]
    return (current, kept_inputs)

def unrotate(grad_top, rotation, kept_inputs, orders, inverses):
    block_count = rotation.shape[1]
    col_count = grad_top.shape[1]
    factor_grads = [None] * len(orders)
    current = grad_top
    for section_at in reversed(range(len(orders))):
        permuted = current[orders[section_at]].reshape(block_count, -1, col_count)
        factor_grads[section_at] = jnp.einsum('kjc,kic->kji', permuted.astype(jnp.float32), kept_inputs[section_at].astype(jnp.float32))
        if section_at > 0:
            pulled = jnp.einsum('kji,kjc->kic', rotation[section_at].astype(jnp.float32), permuted.astype(jnp.float32)).astype(jnp.bfloat16)
            current = pulled.reshape(current.shape)[inverses[section_at]]
    return jnp.stack(factor_grads)

def reference(tokens, gate_weight, up_weight, skew_params, section_bits, upstream):
    rotation_f32, pullback = jax.vjp(cayley, skew_params)
    rotation = rotation_f32.astype(jnp.bfloat16)
    model_width = gate_weight.shape[0]
    orders = [slot_order(section_bits[section_at], model_width) for section_at in range(SECTIONS)]
    inverses = [inverse_order(section_bits[section_at], model_width) for section_at in range(SECTIONS)]
    piece_cols = upstream.shape[1] // 16

    def one_piece(factor_sum, piece_index):
        first_col = (piece_index * piece_cols).astype(jnp.int32)
        gate_cols = lax.dynamic_slice_in_dim(gate_weight, first_col, piece_cols, 1)
        up_cols = lax.dynamic_slice_in_dim(up_weight, first_col, piece_cols, 1)
        cotangent = lax.dynamic_slice_in_dim(upstream, first_col, piece_cols, 1).astype(jnp.float32)
        rotated_gate, gate_inputs = rotate_columns(gate_cols, rotation[0], orders, inverses)
        rotated_up, up_inputs = rotate_columns(up_cols, rotation[1], orders, inverses)
        gate_pre = jnp.dot(tokens.astype(jnp.float32), rotated_gate.astype(jnp.float32), preferred_element_type=jnp.float32)
        up_pre = jnp.dot(tokens.astype(jnp.float32), rotated_up.astype(jnp.float32), preferred_element_type=jnp.float32)
        sigmoid_val = jax.nn.sigmoid(gate_pre)
        silu_val = gate_pre * sigmoid_val
        activation = (silu_val * up_pre).astype(jnp.bfloat16)
        gate_grad = (cotangent * up_pre * sigmoid_val * (1.0 + gate_pre * (1.0 - sigmoid_val))).astype(jnp.bfloat16)
        up_grad = (cotangent * silu_val).astype(jnp.bfloat16)
        gate_top = jnp.dot(tokens.T.astype(jnp.float32), gate_grad.astype(jnp.float32), preferred_element_type=jnp.float32).astype(jnp.bfloat16)
        up_top = jnp.dot(tokens.T.astype(jnp.float32), up_grad.astype(jnp.float32), preferred_element_type=jnp.float32).astype(jnp.bfloat16)
        gate_factor = unrotate(gate_top, rotation[0], gate_inputs, orders, inverses)
        up_factor = unrotate(up_top, rotation[1], up_inputs, orders, inverses)
        return (factor_sum + jnp.stack((gate_factor, up_factor)), activation)
    start_sum = jnp.zeros(rotation.shape, jnp.float32)
    factor_sum, act_blocks = lax.scan(one_piece, start_sum, jnp.arange(16, dtype=jnp.int32))
    activation = jnp.transpose(act_blocks, (1, 0, 2)).reshape(tokens.shape[0], upstream.shape[1])
    skew_grad = pullback(factor_sum)[0]
    return (activation, skew_grad)
```

```python
import jax
import jax.numpy as jnp
from jax import lax
from jax.experimental import pallas as pl
from jax.experimental.pallas import tpu as pltpu
from jax.sharding import PartitionSpec as P


def inverse_kernel(skew_ref, out_ref):
    extent = skew_ref.shape[-1]
    shape = skew_ref.shape
    row_at = lax.broadcasted_iota(jnp.int32, shape, 1)
    col_at = lax.broadcasted_iota(jnp.int32, shape, 2)
    skew = skew_ref[...]
    generator = skew - jnp.swapaxes(skew, 1, 2)
    out_ref[...] = jnp.where(row_at == col_at, 1.0, 0.0) + generator
    lane = lax.broadcasted_iota(jnp.int32, (shape[0], 1, extent), 2)

    def step(at, carry):
        work = out_ref[...]
        pivot_row = out_ref[:, pl.ds(at, 1), :]
        at_col = col_at == at
        pivot_col = jnp.sum(jnp.where(at_col, work, 0.0), axis=2, keepdims=True)
        pivot = jnp.sum(jnp.where(lane == at, pivot_row, 0.0), axis=2, keepdims=True)
        scale = 1.0 / pivot
        scaled_row = jnp.where(lane == at, 1.0, pivot_row) * scale
        cleared = jnp.where(at_col, 0.0, work)
        out_ref[...] = cleared - pivot_col * scaled_row
        out_ref[:, pl.ds(at, 1), :] = scaled_row
        return carry

    lax.fori_loop(0, extent, step, 0)


def cayley_inverse(skew_blocks):
    extent = skew_blocks.shape[-1]
    flat = skew_blocks.reshape(-1, extent, extent)
    out = pl.pallas_call(
        inverse_kernel,
        out_shape=jax.ShapeDtypeStruct(flat.shape, jnp.float32),
        in_specs=[pl.BlockSpec(memory_space=pltpu.VMEM)],
        out_specs=pl.BlockSpec(memory_space=pltpu.VMEM),
        cost_estimate=pl.CostEstimate(
            flops=50_000_000, bytes_accessed=2 * 4 * flat.size, transcendentals=0
        ),
        name="cayley_inverse",
    )(flat)
    return out.reshape(skew_blocks.shape)


def estimate(flops, *arrays):
    moved = sum(array.size * array.dtype.itemsize for array in arrays)
    return pl.CostEstimate(flops=flops, bytes_accessed=moved, transcendentals=0)


def pack(weight, half, cols):
    rows, width = weight.shape
    step = min(rows, 32)

    def body(in_ref, out_ref):
        for at in range(half):
            left = in_ref[:, at * cols : (at + 1) * cols]
            right = in_ref[:, (half + at) * cols : (half + at + 1) * cols]
            out_ref[at] = jnp.concatenate([left, right], axis=1)

    out = jax.ShapeDtypeStruct((half, rows, 2 * cols), weight.dtype)
    return pl.pallas_call(
        body,
        out_shape=out,
        grid=(rows // step,),
        in_specs=[pl.BlockSpec((step, width), lambda at: (at, 0))],
        out_specs=pl.BlockSpec((half, step, 2 * cols), lambda at: (0, at, 0)),
        cost_estimate=estimate(0, weight, out),
        name="pack",
    )(weight)


def dot(left, right, left_dim, right_dim):
    contract = (((left_dim,), (right_dim,)), ((), ()))
    return lax.dot_general(left, right, contract, preferred_element_type=jnp.float32)


def routes(places):
    count, digits = places.shape
    low = GROUP_BITS
    at = jnp.arange(digits, dtype=jnp.int32)
    hit = places[:, :, None] == at[None, None, :]
    slot_of = jnp.sum(jnp.where(hit, at[None, :, None], 0), axis=1)
    is_low = at[None, :] < low
    crosses = is_low != (slot_of < low)
    before = at[:, None] < at[None, :]
    same = (at[:, None] < low) == (at[None, :] < low)
    rank_cross = jnp.sum((crosses[:, :, None] & (before & same)[None]).astype(jnp.int32), axis=1)
    rank_stay = jnp.sum((~crosses[:, :, None] & (before & same)[None]).astype(jnp.int32), axis=1)
    inside = jnp.where(crosses, low - 1 - rank_cross, rank_stay)
    first = jnp.where(is_low, inside, at[None, :])
    second = jnp.where(is_low & ~crosses, inside, slot_of)
    second = jnp.where(~is_low & crosses, low - 1 - rank_cross, second)
    after = jnp.sum(jnp.where(hit, second[:, None, :], 0), axis=2)

    def spread(index, sources, targets):
        bits = jnp.right_shift(index[None, :, None], sources[:, None, :]) & 1
        return jnp.sum(jnp.left_shift(bits, targets[:, None, :]), axis=2)

    group = jnp.arange(1 << low, dtype=jnp.int32)
    natural = jnp.broadcast_to(at[None, :], (count, digits))
    take_first = spread(group, first[:, :low], natural[:, :low])
    take_last = spread(group, natural[:, :low], after[:, :low])
    tiles = jnp.arange((1 << digits) // TILE, dtype=jnp.int32) * TILE
    moves = spread(tiles, second, first)
    heads = (take_first[:, :, None] == group[None, None, :]).astype(jnp.bfloat16)
    tails = (take_last[:, :, None] == group[None, None, :]).astype(jnp.bfloat16)
    return heads, tails, moves


GROUP_BITS = 8
GROUP = 1 << GROUP_BITS
TILE = 8
STEPS = 8


def moved(moves_ref, base, source_ref, slot_ref, tail):
    for pair in range(GROUP // (2 * TILE)):
        parts = []
        for half in range(2):
            start = pl.multiple_of(moves_ref[base + 2 * pair + half], TILE)
            parts.append(source_ref[pl.ds(start, TILE), :])
        rows = slice(2 * TILE * pair, 2 * TILE * (pair + 1))
        slot_ref[rows, :] = jnp.concatenate(parts, axis=0).astype(jnp.bfloat16)
    return dot(tail, slot_ref[...], 1, 0).astype(jnp.bfloat16)


def clamp(phase, wanted, at, last):
    return jnp.where(phase < wanted, 0, jnp.where(phase > wanted, last, at))


def rotate_tokens(all_tokens, rotation, heads, tails, moves, side, extent, mats):
    count, width = all_tokens.shape
    chunk = width // STEPS
    groups = chunk // GROUP
    tiles = GROUP // TILE
    all_tiles = width // TILE
    half_rows = width // 2
    half_chunk = half_rows // STEPS
    last = STEPS - 1

    def body(moves_ref, side_ref, tok_ref, rot_ref, heads_ref, tails_ref, top_ref, mid_ref, low_ref, za, zb, slot):
        m, phase, at = pl.program_id(0), pl.program_id(1), pl.program_id(2)

        def turned(block, value, section):
            parts = []
            for b in range(GROUP // extent):
                rows = slice(b * extent, (b + 1) * extent)
                both = rot_ref[pl.ds(block * GROUP + b * extent, extent), section * mats * extent : (section + 1) * mats * extent]
                own = jnp.where(m == 0, both[:, :extent], both[:, extent:])
                parts.append(dot(own, value[rows], 0, 0).astype(jnp.bfloat16))
            return jnp.concatenate(parts, axis=0)

        @pl.when(phase == 0)
        def _():
            for g in range(groups):
                piece = tok_ref[:, g * GROUP : (g + 1) * GROUP]
                za[pl.ds(at * chunk + g * GROUP, GROUP), :] = dot(heads_ref[0], piece, 1, 1)

        @pl.when(phase == 1)
        def _():
            for g in range(groups):
                value = moved(moves_ref, (at * groups + g) * tiles, za, slot.at[g], tails_ref[0])
                top_ref[g * GROUP : (g + 1) * GROUP, :] = value
                mixed = turned(g, value, 1)
                zb[pl.ds(at * chunk + g * GROUP, GROUP), :] = dot(heads_ref[1], mixed, 1, 0)

        @pl.when(phase == 2)
        def _():
            for g in range(groups):
                value = moved(moves_ref, all_tiles + (at * groups + g) * tiles, zb, slot.at[g], tails_ref[1])
                mid_ref[g * GROUP : (g + 1) * GROUP, :] = value
                mixed = turned(g, value, 0)
                za[pl.ds(at * chunk + g * GROUP, GROUP), :] = dot(heads_ref[2], mixed, 1, 0)

        @pl.when(phase == 3)
        def _():
            for g in range(half_chunk // GROUP):
                at_group = side_ref[0] * (half_rows // GROUP) + at * (half_chunk // GROUP) + g
                value = moved(moves_ref, 2 * all_tiles + at_group * tiles, za, slot.at[g], tails_ref[2])
                low_ref[g * GROUP : (g + 1) * GROUP, :] = value

    outs = (
        jax.ShapeDtypeStruct((width, count), jnp.bfloat16),
        jax.ShapeDtypeStruct((width, mats * count), jnp.bfloat16),
        jax.ShapeDtypeStruct((half_rows, mats * count), jnp.bfloat16),
    )
    whole = lambda m, phase, at: (0, 0, 0)
    return pl.pallas_call(
        body,
        out_shape=outs,
        grid=(mats, 4, STEPS),
        in_specs=[
            pl.BlockSpec(memory_space=pltpu.SMEM),
            pl.BlockSpec(memory_space=pltpu.SMEM),
            pl.BlockSpec((count, chunk), lambda m, phase, at: (0, jnp.where(phase == 0, at, last))),
            pl.BlockSpec(
                (chunk, rotation.shape[1]),
                lambda m, phase, at: (jnp.where(phase == 0, 0, jnp.where(phase == 3, last, at)), 0),
            ),
            pl.BlockSpec((3, GROUP, GROUP), whole),
            pl.BlockSpec((3, GROUP, GROUP), whole),
        ],
        out_specs=(
            pl.BlockSpec((chunk, count), lambda m, phase, at: (jnp.where(m == 0, clamp(phase, 1, at, last), clamp(phase, 1, at, last)), 0)),
            pl.BlockSpec((chunk, count), lambda m, phase, at: (clamp(phase, 2, at, last), m)),
            pl.BlockSpec((half_chunk, count), lambda m, phase, at: (clamp(phase, 3, at, last), m)),
        ),
        scratch_shapes=[
            pltpu.VMEM((width, count), jnp.float32),
            pltpu.VMEM((width, count), jnp.float32),
            pltpu.VMEM((groups, GROUP, count), jnp.bfloat16),
        ],
        compiler_params=pltpu.CompilerParams(vmem_limit_bytes=48 << 20),
        cost_estimate=estimate(14 * 2 * width * GROUP * count, all_tokens, rotation, *outs),
        name="rotate_tokens",
    )(moves, side, all_tokens, rotation, heads, tails)


def block_terms(pulled, mid, top, rotation, heads, tails, moves, side, extent, mats):
    half_rows = pulled.shape[0]
    width, count = top.shape
    chunk = width // STEPS
    groups = chunk // GROUP
    tiles = GROUP // TILE
    all_tiles = width // TILE
    half_chunk = half_rows // STEPS
    last = STEPS - 1

    def body(moves_ref, side_ref, pulled_ref, mid_ref, top_ref, rot_ref, heads_ref, tails_ref, terms_0_ref, terms_1_ref, za, zb, slot, kept_0, kept_1):
        m, phase, at = pl.program_id(0), pl.program_id(1), pl.program_id(2)
        chunk_rows = pl.ds(at * chunk, chunk)

        def emit(out_ref, kept, left_ref, g, value):
            for b in range(GROUP // extent):
                rows = slice(g * GROUP + b * extent, g * GROUP + (b + 1) * extent)
                term = dot(left_ref[rows, :], value[b * extent : (b + 1) * extent], 1, 1)
                at_rows = pl.ds(at * chunk + g * GROUP + b * extent, extent)

                @pl.when(m == 0)
                def _():
                    kept[at_rows, :] = term

                @pl.when(m == mats - 1)
                def _():
                    out_ref[rows, :] = jnp.concatenate([kept[at_rows, :], term], axis=1).astype(jnp.bfloat16)

        @pl.when(phase == 0)
        def _():
            own = side_ref[0] * half_rows + at * half_chunk
            other = (1 - side_ref[0]) * half_rows + at * half_chunk
            za[pl.ds(pl.multiple_of(other, half_chunk), half_chunk), :] = jnp.zeros((half_chunk, count), jnp.float32)
            for g in range(half_chunk // GROUP):
                piece = pulled_ref[g * GROUP : (g + 1) * GROUP, :]
                za[pl.ds(pl.multiple_of(own + g * GROUP, GROUP), GROUP), :] = dot(heads_ref[0], piece, 1, 0)

        @pl.when(phase == 1)
        def _():
            for g in range(groups):
                value = moved(moves_ref, (at * groups + g) * tiles, za, slot.at[g], tails_ref[0])
                emit(terms_0_ref, kept_0, mid_ref, g, value)
                parts = []
                for b in range(GROUP // extent):
                    both = rot_ref[pl.ds(g * GROUP + b * extent, extent), : mats * extent]
                    own = jnp.where(m == 0, both[:, :extent], both[:, extent:])
                    parts.append(dot(own, value[b * extent : (b + 1) * extent], 1, 0).astype(jnp.bfloat16))
                mixed = jnp.concatenate(parts, axis=0)
                zb[pl.ds(at * chunk + g * GROUP, GROUP), :] = dot(heads_ref[1], mixed, 1, 0)

        @pl.when(phase == 2)
        def _():
            for g in range(groups):
                value = moved(moves_ref, all_tiles + (at * groups + g) * tiles, zb, slot.at[g], tails_ref[1])
                emit(terms_1_ref, kept_1, top_ref, g, value)

    out = jax.ShapeDtypeStruct((width, mats * extent), jnp.bfloat16)
    whole = lambda m, phase, at: (0, 0, 0)
    return pl.pallas_call(
        body,
        out_shape=(out, out),
        grid=(mats, 3, STEPS),
        in_specs=[
            pl.BlockSpec(memory_space=pltpu.SMEM),
            pl.BlockSpec(memory_space=pltpu.SMEM),
            pl.BlockSpec((half_chunk, count), lambda m, phase, at: (clamp(phase, 0, at, last), m)),
            pl.BlockSpec((chunk, count), lambda m, phase, at: (clamp(phase, 1, at, last), m)),
            pl.BlockSpec((chunk, count), lambda m, phase, at: (clamp(phase, 2, at, last), 0)),
            pl.BlockSpec((chunk, rotation.shape[1]), lambda m, phase, at: (clamp(phase, 1, at, last), 0)),
            pl.BlockSpec((2, GROUP, GROUP), whole),
            pl.BlockSpec((2, GROUP, GROUP), whole),
        ],
        out_specs=(
            pl.BlockSpec((chunk, mats * extent), lambda m, phase, at: (jnp.where(m == mats - 1, clamp(phase, 1, at, last), 0), 0)),
            pl.BlockSpec((chunk, mats * extent), lambda m, phase, at: (jnp.where(m == mats - 1, clamp(phase, 2, at, last), 0), 0)),
        ),
        scratch_shapes=[
            pltpu.VMEM((width, count), jnp.float32),
            pltpu.VMEM((width, count), jnp.float32),
            pltpu.VMEM((groups, GROUP, count), jnp.bfloat16),
            pltpu.VMEM((width, extent), jnp.float32),
            pltpu.VMEM((width, extent), jnp.float32),
        ],
        compiler_params=pltpu.CompilerParams(vmem_limit_bytes=52 << 20),
        cost_estimate=estimate(14 * 2 * width * GROUP * count, pulled, mid, top, rotation, out, out),
        name="block_terms",
    )(moves, side, pulled, mid, top, rotation, heads, tails)


def pull(gate_cols, up_cols, gate_grad, up_grad):
    rows, width = gate_cols.shape
    count = gate_grad.shape[0]
    step = min(512, rows)

    def body(gate_ref, up_ref, gate_grad_ref, up_grad_ref, out_ref):
        out_ref[:, :count] = dot(gate_ref[...], gate_grad_ref[...], 1, 1).astype(jnp.bfloat16)
        out_ref[:, count:] = dot(up_ref[...], up_grad_ref[...], 1, 1).astype(jnp.bfloat16)

    out = jax.ShapeDtypeStruct((rows, 2 * count), jnp.bfloat16)
    weights = pl.BlockSpec((step, width), lambda at: (at, 0))
    grads = pl.BlockSpec((count, width), lambda at: (0, 0))
    return pl.pallas_call(
        body,
        out_shape=out,
        grid=(rows // step,),
        in_specs=[weights, weights, grads, grads],
        out_specs=pl.BlockSpec((step, 2 * count), lambda at: (at, 0)),
        cost_estimate=estimate(4 * rows * width * count, gate_cols, up_cols, out),
        name="pull",
    )(gate_cols, up_cols, gate_grad, up_grad)


def places_of(bits, section_row):
    places = jnp.arange(section_row.shape[0], dtype=jnp.int32)
    found = bits[:, None] == section_row[None, :]
    return jnp.sum(jnp.where(found, places[None, :], 0), axis=1)


def shards(tokens, gate_weight, up_weight, skew_params, section_bits, upstream):
    mats, _, own_blocks, extent, _ = skew_params.shape
    own_rows = gate_weight.shape[0]
    own_cols = upstream.shape[1]
    devices = gate_weight.shape[1] // own_cols
    half = devices // 2
    half_rows = half * own_rows
    side = lax.axis_index("rows") // half
    groups = [list(range(half)), list(range(half, devices))]
    swap = [(at, (at + half) % devices) for at in range(devices)]

    def move(parts):
        moved = lax.all_to_all(
            parts, "rows", split_axis=0, concat_axis=0, axis_index_groups=groups, tiled=True
        )
        return moved.reshape(half_rows, 2 * own_cols)

    bits_0, bits_1 = section_bits[0], section_bits[1]
    natural = jnp.arange(bits_0.shape[0], dtype=jnp.int32)
    inverse_0 = places_of(natural, bits_0)
    one_to_zero = places_of(bits_0, bits_1)
    zero_to_one = places_of(bits_1, bits_0)
    heads, tails, moves = routes(jnp.stack([bits_1, one_to_zero, inverse_0, bits_0, zero_to_one]))
    side_at = jnp.reshape(side, (1,)).astype(jnp.int32)

    all_tokens = lax.all_gather(tokens, "rows", axis=0, tiled=True)
    token_count = all_tokens.shape[0]
    gate_cols = move(pack(gate_weight, half, own_cols))
    inverse = cayley_inverse(skew_params)
    own_rotation = (2.0 * inverse - jnp.eye(extent, dtype=jnp.float32)).astype(jnp.bfloat16)
    packed = own_rotation.transpose(2, 3, 1, 0, 4).reshape(own_blocks * extent, -1)
    rotation = lax.all_gather(packed, "rows", axis=0, tiled=True)
    up_cols = move(pack(up_weight, half, own_cols))
    other_upstream = lax.ppermute(upstream, "rows", swap)
    top_tokens, mid, low = rotate_tokens(
        all_tokens, rotation, heads[:3], tails[:3], moves[:3].reshape(-1), side_at, extent, mats
    )

    def project(at, columns):
        part = dot(low[:, at * token_count : (at + 1) * token_count], columns, 0, 0)
        return part + lax.ppermute(part.astype(jnp.bfloat16), "rows", swap).astype(jnp.float32)

    gate_pre = project(0, gate_cols)
    up_pre = project(1, up_cols)
    sigmoid_val = jax.nn.sigmoid(gate_pre)
    silu_val = gate_pre * sigmoid_val
    activation = (silu_val * up_pre).astype(jnp.bfloat16)
    activation = jnp.where(side == 0, activation[:, :own_cols], activation[:, own_cols:])
    first = jnp.where(side == 0, upstream, other_upstream)
    second = jnp.where(side == 0, other_upstream, upstream)
    cotangent = jnp.concatenate([first, second], axis=1).astype(jnp.float32)
    gate_grad = (cotangent * up_pre * sigmoid_val * (1.0 + gate_pre * (1.0 - sigmoid_val))).astype(
        jnp.bfloat16
    )
    up_grad = (cotangent * silu_val).astype(jnp.bfloat16)

    pulled = pull(gate_cols, up_cols, gate_grad, up_grad)
    terms_0, terms_1 = block_terms(
        pulled, mid, top_tokens, rotation, heads[3:], tails[3:], moves[3:].reshape(-1), side_at, extent, mats
    )

    def send(terms):
        terms = terms.reshape(devices, own_blocks * extent, -1)
        return lax.all_to_all(terms, "rows", split_axis=0, concat_axis=0, tiled=True)

    def summed_of(terms):
        summed = jnp.sum(terms.astype(jnp.float32), axis=0)
        return summed.reshape(own_blocks, extent, mats, extent).transpose(2, 0, 1, 3)

    sent_0 = send(terms_0)
    sent_1 = send(terms_1)
    factor_grad = jnp.stack([summed_of(sent_0), summed_of(sent_1)], axis=1)

    left = jnp.einsum(
        "mskab,mskac->mskbc", inverse, factor_grad, precision=lax.Precision.HIGHEST
    )
    generator_grad = -2.0 * jnp.einsum(
        "mskbc,mskdc->mskbd", left, inverse, precision=lax.Precision.HIGHEST
    )
    skew_grad = generator_grad - jnp.swapaxes(generator_grad, -1, -2)
    return (activation, skew_grad)


def solution(mesh):
    placed = (
        P(("groups", "rows"), None),
        P("rows", None),
        P("rows", None),
        P(None, None, "rows", None, None),
        P(),
        P("groups", "rows"),
    )
    return jax.shard_map(
        shards,
        mesh=mesh,
        in_specs=placed,
        out_specs=(P("groups", "rows"), P("groups", None, "rows", None, None)),
        check_vma=False,
    )
```

```python
import jax
import jax.numpy as jnp
from jax import lax
from jax.experimental import pallas as pl
from jax.experimental.pallas import tpu as pltpu
from jax.sharding import PartitionSpec as P


def inverse_kernel(skew_ref, out_ref):
    extent = skew_ref.shape[-1]
    shape = skew_ref.shape
    row_at = lax.broadcasted_iota(jnp.int32, shape, 1)
    col_at = lax.broadcasted_iota(jnp.int32, shape, 2)
    skew = skew_ref[...]
    generator = skew - jnp.swapaxes(skew, 1, 2)
    out_ref[...] = jnp.where(row_at == col_at, 1.0, 0.0) + generator
    lane = lax.broadcasted_iota(jnp.int32, (shape[0], 1, extent), 2)

    def step(at, carry):
        work = out_ref[...]
        pivot_row = out_ref[:, pl.ds(at, 1), :]
        at_col = col_at == at
        pivot_col = jnp.sum(jnp.where(at_col, work, 0.0), axis=2, keepdims=True)
        pivot = jnp.sum(jnp.where(lane == at, pivot_row, 0.0), axis=2, keepdims=True)
        scale = 1.0 / pivot
        scaled_row = jnp.where(lane == at, 1.0, pivot_row) * scale
        cleared = jnp.where(at_col, 0.0, work)
        out_ref[...] = cleared - pivot_col * scaled_row
        out_ref[:, pl.ds(at, 1), :] = scaled_row
        return carry

    lax.fori_loop(0, extent, step, 0)


def cayley_inverse(skew_blocks):
    extent = skew_blocks.shape[-1]
    flat = skew_blocks.reshape(-1, extent, extent)
    out = pl.pallas_call(
        inverse_kernel,
        out_shape=jax.ShapeDtypeStruct(flat.shape, jnp.float32),
        in_specs=[pl.BlockSpec(memory_space=pltpu.VMEM)],
        out_specs=pl.BlockSpec(memory_space=pltpu.VMEM),
        cost_estimate=pl.CostEstimate(
            flops=50_000_000, bytes_accessed=2 * 4 * flat.size, transcendentals=0
        ),
        name="cayley_inverse",
    )(flat)
    return out.reshape(skew_blocks.shape)


def estimate(flops, *arrays):
    moved = sum(array.size * array.dtype.itemsize for array in arrays)
    return pl.CostEstimate(flops=flops, bytes_accessed=moved, transcendentals=0)


def pack(weight, half, cols):
    rows, width = weight.shape
    step = min(rows, 32)

    def body(in_ref, out_ref):
        for at in range(half):
            left = in_ref[:, at * cols : (at + 1) * cols]
            right = in_ref[:, (half + at) * cols : (half + at + 1) * cols]
            out_ref[at] = jnp.concatenate([left, right], axis=1)

    out = jax.ShapeDtypeStruct((half, rows, 2 * cols), weight.dtype)
    return pl.pallas_call(
        body,
        out_shape=out,
        grid=(rows // step,),
        in_specs=[pl.BlockSpec((step, width), lambda at: (at, 0))],
        out_specs=pl.BlockSpec((half, step, 2 * cols), lambda at: (0, at, 0)),
        cost_estimate=estimate(0, weight, out),
        name="pack",
    )(weight)


def dot(left, right, left_dim, right_dim):
    contract = (((left_dim,), (right_dim,)), ((), ()))
    return lax.dot_general(left, right, contract, preferred_element_type=jnp.float32)


def routes(places):
    count, digits = places.shape
    low = GROUP_BITS
    at = jnp.arange(digits, dtype=jnp.int32)
    hit = places[:, :, None] == at[None, None, :]
    slot_of = jnp.sum(jnp.where(hit, at[None, :, None], 0), axis=1)
    is_low = at[None, :] < low
    crosses = is_low != (slot_of < low)
    before = at[:, None] < at[None, :]
    same = (at[:, None] < low) == (at[None, :] < low)
    rank_cross = jnp.sum((crosses[:, :, None] & (before & same)[None]).astype(jnp.int32), axis=1)
    rank_stay = jnp.sum((~crosses[:, :, None] & (before & same)[None]).astype(jnp.int32), axis=1)
    inside = jnp.where(crosses, low - 1 - rank_cross, rank_stay)
    first = jnp.where(is_low, inside, at[None, :])
    second = jnp.where(is_low & ~crosses, inside, slot_of)
    second = jnp.where(~is_low & crosses, low - 1 - rank_cross, second)
    after = jnp.sum(jnp.where(hit, second[:, None, :], 0), axis=2)

    def spread(index, sources, targets):
        bits = jnp.right_shift(index[None, :, None], sources[:, None, :]) & 1
        return jnp.sum(jnp.left_shift(bits, targets[:, None, :]), axis=2)

    group = jnp.arange(1 << low, dtype=jnp.int32)
    natural = jnp.broadcast_to(at[None, :], (count, digits))
    take_first = spread(group, first[:, :low], natural[:, :low])
    take_last = spread(group, natural[:, :low], after[:, :low])
    tiles = jnp.arange((1 << digits) // TILE, dtype=jnp.int32) * TILE
    moves = spread(tiles, second, first)
    heads = (take_first[:, :, None] == group[None, None, :]).astype(jnp.bfloat16)
    tails = (take_last[:, :, None] == group[None, None, :]).astype(jnp.bfloat16)
    return heads, tails, moves


GROUP_BITS = 8
GROUP = 1 << GROUP_BITS
TILE = 8
STEPS = 8


def collect(moves_ref, base, source_ref, slot_ref):
    for pair in range(GROUP // (2 * TILE)):
        parts = []
        for half in range(2):
            start = pl.multiple_of(moves_ref[base + 2 * pair + half], TILE)
            parts.append(source_ref[pl.ds(start, TILE), :])
        rows = slice(2 * TILE * pair, 2 * TILE * (pair + 1))
        slot_ref[rows, :] = jnp.concatenate(parts, axis=0).astype(jnp.bfloat16)


def moved(moves_ref, base, source_ref, slot_ref, tail):
    collect(moves_ref, base, source_ref, slot_ref)
    return dot(tail, slot_ref[...], 1, 0).astype(jnp.bfloat16)


def gather_blocks(own, devices):
    rows, lanes = own.shape
    bits = devices.bit_length() - 1
    half = rows // 2
    down = list(reversed(range(bits)))
    orders = [down, down[:-3] + [down[-2], down[-3], down[-1]]]

    def kernel(own_ref, out_ref, send_sem, recv_sem, local_sem):
        me = lax.axis_index("rows")

        def flipped(index, bit):
            return index + (1 - 2 * ((index // (1 << bit)) % 2)) * (1 << bit)

        barrier = pltpu.get_barrier_semaphore()
        for bit in range(bits):
            pl.semaphore_signal(
                barrier, inc=1, device_id={"rows": flipped(me, bit)}, device_id_type=pl.DeviceIdType.MESH
            )
        pl.semaphore_wait(barrier, bits)
        local = pltpu.make_async_copy(own_ref, out_ref.at[me], local_sem)
        local.start()

        def copy(color, step, pattern):
            order = orders[color]
            block = me
            for at in range(step):
                if (pattern >> at) & 1:
                    block = flipped(block, order[at])
            lines = pl.ds(color * half, half)
            source = own_ref.at[lines] if pattern == 0 else out_ref.at[block, lines]
            slot = pattern + (1 << step) - 1
            return pltpu.make_async_remote_copy(
                src_ref=source,
                dst_ref=out_ref.at[block, lines],
                send_sem=send_sem.at[color, slot],
                recv_sem=recv_sem.at[color, slot],
                device_id={"rows": flipped(me, order[step])},
                device_id_type=pl.DeviceIdType.MESH,
            )

        copies = {}
        arrived = set()

        def arrive(color, pattern):
            if pattern and (color, pattern) not in arrived:
                arrived.add((color, pattern))
                copies[color, pattern].wait_recv()

        for step in range(bits):
            for pattern in range(1 << step):
                for color in range(2):
                    arrive(color, pattern)
                    made = copy(color, step, pattern)
                    made.start()
                    copies[color, pattern + (1 << step)] = made
        for pattern in range(1, devices):
            for color in range(2):
                arrive(color, pattern)
        for made in copies.values():
            made.wait_send()
        local.wait()

    return pl.pallas_call(
        kernel,
        out_shape=jax.ShapeDtypeStruct((devices, rows, lanes), own.dtype),
        in_specs=[pl.BlockSpec(memory_space=pl.ANY)],
        out_specs=pl.BlockSpec(memory_space=pl.ANY),
        scratch_shapes=[
            pltpu.SemaphoreType.DMA((2, devices - 1)),
            pltpu.SemaphoreType.DMA((2, devices - 1)),
            pltpu.SemaphoreType.DMA,
        ],
        compiler_params=pltpu.CompilerParams(collective_id=0, has_side_effects=True),
        cost_estimate=pl.CostEstimate(flops=0, bytes_accessed=64 * devices * rows * lanes, transcendentals=0),
        name="gather_blocks",
    )(own)


def clamp(phase, wanted, at, last):
    return jnp.where(phase < wanted, 0, jnp.where(phase > wanted, last, at))


def rotate_tokens(all_tokens, rotation, heads, tails, moves, side, extent, mats):
    count, width = all_tokens.shape
    chunk = width // STEPS
    groups = chunk // GROUP
    tiles = GROUP // TILE
    all_tiles = width // TILE
    half_rows = width // 2
    half_chunk = half_rows // STEPS
    last = STEPS - 1

    def body(moves_ref, side_ref, tok_ref, rot_ref, heads_ref, tails_ref, top_ref, mid_ref, low_ref, za, zb, slot):
        m, phase, at = pl.program_id(0), pl.program_id(1), pl.program_id(2)

        def turned(block, value, section):
            parts = []
            for b in range(GROUP // extent):
                rows = slice(b * extent, (b + 1) * extent)
                both = rot_ref[pl.ds(block * GROUP + b * extent, extent), section * mats * extent : (section + 1) * mats * extent]
                own = jnp.where(m == 0, both[:, :extent], both[:, extent:])
                parts.append(dot(own, value[rows], 0, 0).astype(jnp.bfloat16))
            return jnp.concatenate(parts, axis=0)

        @pl.when(phase == 0)
        def _():
            for g in range(groups):
                piece = tok_ref[:, g * GROUP : (g + 1) * GROUP]
                za[pl.ds(at * chunk + g * GROUP, GROUP), :] = dot(heads_ref[0], piece, 1, 1)

        @pl.when(phase == 1)
        def _():
            for g in range(groups):
                value = moved(moves_ref, (at * groups + g) * tiles, za, slot.at[g], tails_ref[0])
                top_ref[g * GROUP : (g + 1) * GROUP, :] = value
                mixed = turned(g, value, 1)
                zb[pl.ds(at * chunk + g * GROUP, GROUP), :] = dot(heads_ref[1], mixed, 1, 0)

        @pl.when(phase == 2)
        def _():
            for g in range(groups):
                value = moved(moves_ref, all_tiles + (at * groups + g) * tiles, zb, slot.at[g], tails_ref[1])
                mid_ref[g * GROUP : (g + 1) * GROUP, :] = value
                mixed = turned(g, value, 0)
                za[pl.ds(at * chunk + g * GROUP, GROUP), :] = dot(heads_ref[2], mixed, 1, 0)

        @pl.when(phase == 3)
        def _():
            for g in range(half_chunk // GROUP):
                at_group = side_ref[0] * (half_rows // GROUP) + at * (half_chunk // GROUP) + g
                value = moved(moves_ref, 2 * all_tiles + at_group * tiles, za, slot.at[g], tails_ref[2])
                low_ref[g * GROUP : (g + 1) * GROUP, :] = value

    outs = (
        jax.ShapeDtypeStruct((width, count), jnp.bfloat16),
        jax.ShapeDtypeStruct((width, mats * count), jnp.bfloat16),
        jax.ShapeDtypeStruct((half_rows, mats * count), jnp.bfloat16),
    )
    whole = lambda m, phase, at: (0, 0, 0)
    return pl.pallas_call(
        body,
        out_shape=outs,
        grid=(mats, 4, STEPS),
        in_specs=[
            pl.BlockSpec(memory_space=pltpu.SMEM),
            pl.BlockSpec(memory_space=pltpu.SMEM),
            pl.BlockSpec((count, chunk), lambda m, phase, at: (0, jnp.where(phase == 0, at, last))),
            pl.BlockSpec(
                (chunk, rotation.shape[1]),
                lambda m, phase, at: (jnp.where(phase == 0, 0, jnp.where(phase == 3, last, at)), 0),
            ),
            pl.BlockSpec((3, GROUP, GROUP), whole),
            pl.BlockSpec((3, GROUP, GROUP), whole),
        ],
        out_specs=(
            pl.BlockSpec((chunk, count), lambda m, phase, at: (jnp.where(m == 0, clamp(phase, 1, at, last), clamp(phase, 1, at, last)), 0)),
            pl.BlockSpec((chunk, count), lambda m, phase, at: (clamp(phase, 2, at, last), m)),
            pl.BlockSpec((half_chunk, count), lambda m, phase, at: (clamp(phase, 3, at, last), m)),
        ),
        scratch_shapes=[
            pltpu.VMEM((width, count), jnp.float32),
            pltpu.VMEM((width, count), jnp.float32),
            pltpu.VMEM((groups, GROUP, count), jnp.bfloat16),
        ],
        compiler_params=pltpu.CompilerParams(vmem_limit_bytes=48 << 20),
        cost_estimate=estimate(14 * 2 * width * GROUP * count, all_tokens, rotation, *outs),
        name="rotate_tokens",
    )(moves, side, all_tokens, rotation, heads, tails)


def block_terms(pulled, mid, top, rotation, heads, tails, moves, side, extent, mats):
    half_rows = pulled.shape[0]
    width, count = top.shape
    chunk = width // STEPS
    groups = chunk // GROUP
    tiles = GROUP // TILE
    all_tiles = width // TILE
    half_chunk = half_rows // STEPS
    last = STEPS - 1

    def body(moves_ref, side_ref, pulled_ref, mid_ref, top_ref, rot_ref, heads_ref, tails_ref, terms_0_ref, terms_1_ref, za, zb, slot, kept_0, kept_1):
        m, phase, at = pl.program_id(0), pl.program_id(1), pl.program_id(2)
        lane_mat = lax.broadcasted_iota(jnp.int32, (extent, mats * extent), 1) // extent

        def emit(out_ref, kept, left_ref, g, tail):
            gram = dot(left_ref[g * GROUP : (g + 1) * GROUP, :], slot[g], 1, 1).astype(jnp.bfloat16)
            terms = dot(gram, tail, 1, 1)
            for b in range(GROUP // extent):
                pair = b // mats * mats * extent
                piece = terms[b * extent : (b + 1) * extent, pair : pair + mats * extent]
                turned = pltpu.roll(piece, extent, 1)
                placed = jnp.where(m == b % mats, piece, turned)
                at_rows = pl.ds(at * chunk + g * GROUP + b * extent, extent)
                both = jnp.where(lane_mat == m, placed, kept[at_rows, :])
                kept[at_rows, :] = both
                out_ref[g * GROUP + b * extent : g * GROUP + (b + 1) * extent, :] = both.astype(jnp.bfloat16)

        @pl.when(phase == 0)
        def _():
            own = side_ref[0] * half_rows + at * half_chunk
            other = (1 - side_ref[0]) * half_rows + at * half_chunk
            za[pl.ds(pl.multiple_of(other, half_chunk), half_chunk), :] = jnp.zeros((half_chunk, count), jnp.float32)
            for g in range(half_chunk // GROUP):
                piece = pulled_ref[g * GROUP : (g + 1) * GROUP, :]
                za[pl.ds(pl.multiple_of(own + g * GROUP, GROUP), GROUP), :] = dot(heads_ref[0], piece, 1, 0)

        @pl.when(phase == 1)
        def _():
            for g in range(groups):
                collect(moves_ref, (at * groups + g) * tiles, za, slot.at[g])
                emit(terms_0_ref, kept_0, mid_ref, g, tails_ref[0])
                parts = []
                for b in range(GROUP // extent):
                    both = rot_ref[pl.ds(g * GROUP + b * extent, extent), : mats * extent]
                    own = jnp.where(m == 0, both[:, :extent], both[:, extent:])
                    tail = tails_ref[0, b * extent : (b + 1) * extent, :]
                    parts.append(dot(own, tail, 1, 0).astype(jnp.bfloat16))
                merged = dot(heads_ref[1], jnp.concatenate(parts, axis=0), 1, 0).astype(jnp.bfloat16)
                zb[pl.ds(at * chunk + g * GROUP, GROUP), :] = dot(merged, slot[g], 1, 0)

        @pl.when(phase == 2)
        def _():
            for g in range(groups):
                collect(moves_ref, all_tiles + (at * groups + g) * tiles, zb, slot.at[g])
                emit(terms_1_ref, kept_1, top_ref, g, tails_ref[1])

    out = jax.ShapeDtypeStruct((width, mats * extent), jnp.bfloat16)
    whole = lambda m, phase, at: (0, 0, 0)
    return pl.pallas_call(
        body,
        out_shape=(out, out),
        grid=(mats, 3, STEPS),
        in_specs=[
            pl.BlockSpec(memory_space=pltpu.SMEM),
            pl.BlockSpec(memory_space=pltpu.SMEM),
            pl.BlockSpec((half_chunk, count), lambda m, phase, at: (clamp(phase, 0, at, last), m)),
            pl.BlockSpec((chunk, count), lambda m, phase, at: (clamp(phase, 1, at, last), m)),
            pl.BlockSpec((chunk, count), lambda m, phase, at: (clamp(phase, 2, at, last), 0)),
            pl.BlockSpec((chunk, rotation.shape[1]), lambda m, phase, at: (clamp(phase, 1, at, last), 0)),
            pl.BlockSpec((2, GROUP, GROUP), whole),
            pl.BlockSpec((2, GROUP, GROUP), whole),
        ],
        out_specs=(
            pl.BlockSpec((chunk, mats * extent), lambda m, phase, at: (jnp.where(m == mats - 1, clamp(phase, 1, at, last), 0), 0)),
            pl.BlockSpec((chunk, mats * extent), lambda m, phase, at: (jnp.where(m == mats - 1, clamp(phase, 2, at, last), 0), 0)),
        ),
        scratch_shapes=[
            pltpu.VMEM((width, count), jnp.float32),
            pltpu.VMEM((width, count), jnp.float32),
            pltpu.VMEM((groups, GROUP, count), jnp.bfloat16),
            pltpu.VMEM((width, mats * extent), jnp.float32),
            pltpu.VMEM((width, mats * extent), jnp.float32),
        ],
        compiler_params=pltpu.CompilerParams(vmem_limit_bytes=52 << 20),
        cost_estimate=estimate(14 * 2 * width * GROUP * count, pulled, mid, top, rotation, out, out),
        name="block_terms",
    )(moves, side, pulled, mid, top, rotation, heads, tails)


def pull(gate_cols, up_cols, gate_grad, up_grad):
    rows, width = gate_cols.shape
    count = gate_grad.shape[0]
    step = min(512, rows)

    def body(gate_ref, up_ref, gate_grad_ref, up_grad_ref, out_ref):
        out_ref[:, :count] = dot(gate_ref[...], gate_grad_ref[...], 1, 1).astype(jnp.bfloat16)
        out_ref[:, count:] = dot(up_ref[...], up_grad_ref[...], 1, 1).astype(jnp.bfloat16)

    out = jax.ShapeDtypeStruct((rows, 2 * count), jnp.bfloat16)
    weights = pl.BlockSpec((step, width), lambda at: (at, 0))
    grads = pl.BlockSpec((count, width), lambda at: (0, 0))
    return pl.pallas_call(
        body,
        out_shape=out,
        grid=(rows // step,),
        in_specs=[weights, weights, grads, grads],
        out_specs=pl.BlockSpec((step, 2 * count), lambda at: (at, 0)),
        cost_estimate=estimate(4 * rows * width * count, gate_cols, up_cols, out),
        name="pull",
    )(gate_cols, up_cols, gate_grad, up_grad)


def places_of(bits, section_row):
    places = jnp.arange(section_row.shape[0], dtype=jnp.int32)
    found = bits[:, None] == section_row[None, :]
    return jnp.sum(jnp.where(found, places[None, :], 0), axis=1)


def shards(tokens, gate_weight, up_weight, skew_params, section_bits, upstream):
    mats, _, own_blocks, extent, _ = skew_params.shape
    own_rows = gate_weight.shape[0]
    own_cols = upstream.shape[1]
    devices = gate_weight.shape[1] // own_cols
    half = devices // 2
    half_rows = half * own_rows
    side = lax.axis_index("rows") // half
    groups = [list(range(half)), list(range(half, devices))]
    swap = [(at, (at + half) % devices) for at in range(devices)]

    def move(parts):
        moved = lax.all_to_all(
            parts, "rows", split_axis=0, concat_axis=0, axis_index_groups=groups, tiled=True
        )
        return moved.reshape(half_rows, 2 * own_cols)

    bits_0, bits_1 = section_bits[0], section_bits[1]
    natural = jnp.arange(bits_0.shape[0], dtype=jnp.int32)
    inverse_0 = places_of(natural, bits_0)
    one_to_zero = places_of(bits_0, bits_1)
    zero_to_one = places_of(bits_1, bits_0)
    heads, tails, moves = routes(jnp.stack([bits_1, one_to_zero, inverse_0, bits_0, zero_to_one]))
    side_at = jnp.reshape(side, (1,)).astype(jnp.int32)

    all_tokens = lax.all_gather(tokens, "rows", axis=0, tiled=True)
    token_count = all_tokens.shape[0]
    skew_params, gate_parts = lax.optimization_barrier((skew_params, pack(gate_weight, half, own_cols)))
    gate_cols = move(gate_parts)
    inverse = cayley_inverse(skew_params)
    own_rotation = (2.0 * inverse - jnp.eye(extent, dtype=jnp.float32)).astype(jnp.bfloat16)
    packed = own_rotation.transpose(2, 3, 1, 0, 4).reshape(own_blocks * extent, -1)
    rotation = gather_blocks(packed, devices).reshape(devices * own_blocks * extent, -1)
    rotation, up_weight = lax.optimization_barrier((rotation, up_weight))
    up_parts = pack(up_weight, half, own_cols)
    all_tokens, gate_cols, up_parts = lax.optimization_barrier((all_tokens, gate_cols, up_parts))
    up_cols = move(up_parts)
    other_upstream = lax.ppermute(upstream, "rows", swap)
    top_tokens, mid, low = rotate_tokens(
        all_tokens, rotation, heads[:3], tails[:3], moves[:3].reshape(-1), side_at, extent, mats
    )

    def project(at, columns):
        part = dot(low[:, at * token_count : (at + 1) * token_count], columns, 0, 0)
        return part + lax.ppermute(part.astype(jnp.bfloat16), "rows", swap).astype(jnp.float32)

    gate_pre = project(0, gate_cols)
    up_pre = project(1, up_cols)
    sigmoid_val = jax.nn.sigmoid(gate_pre)
    silu_val = gate_pre * sigmoid_val
    activation = (silu_val * up_pre).astype(jnp.bfloat16)
    activation = jnp.where(side == 0, activation[:, :own_cols], activation[:, own_cols:])
    first = jnp.where(side == 0, upstream, other_upstream)
    second = jnp.where(side == 0, other_upstream, upstream)
    cotangent = jnp.concatenate([first, second], axis=1).astype(jnp.float32)
    gate_grad = (cotangent * up_pre * sigmoid_val * (1.0 + gate_pre * (1.0 - sigmoid_val))).astype(
        jnp.bfloat16
    )
    up_grad = (cotangent * silu_val).astype(jnp.bfloat16)

    pulled = pull(gate_cols, up_cols, gate_grad, up_grad)
    terms_0, terms_1 = block_terms(
        pulled, mid, top_tokens, rotation, heads[3:], tails[3:], moves[3:].reshape(-1), side_at, extent, mats
    )

    def send(terms):
        terms = terms.reshape(devices, own_blocks * extent, -1)
        return lax.all_to_all(terms, "rows", split_axis=0, concat_axis=0, tiled=True)

    def summed_of(terms):
        summed = jnp.sum(terms.astype(jnp.float32), axis=0)
        return summed.reshape(own_blocks, extent, mats, extent).transpose(2, 0, 1, 3)

    sent_0 = send(terms_0)
    sent_1 = send(terms_1)
    factor_grad = jnp.stack([summed_of(sent_0), summed_of(sent_1)], axis=1)

    left = jnp.einsum(
        "mskab,mskac->mskbc", inverse, factor_grad, precision=lax.Precision.HIGHEST
    )
    generator_grad = -2.0 * jnp.einsum(
        "mskbc,mskdc->mskbd", left, inverse, precision=lax.Precision.HIGHEST
    )
    skew_grad = generator_grad - jnp.swapaxes(generator_grad, -1, -2)
    return (activation, skew_grad)


def solution(mesh):
    placed = (
        P(("groups", "rows"), None),
        P("rows", None),
        P("rows", None),
        P(None, None, "rows", None, None),
        P(),
        P("groups", "rows"),
    )
    return jax.shard_map(
        shards,
        mesh=mesh,
        in_specs=placed,
        out_specs=(P("groups", "rows"), P("groups", None, "rows", None, None)),
        check_vma=False,
    )
```

```python
import jax
import jax.numpy as jnp
from jax import lax
from jax.experimental import pallas as pl
from jax.experimental.pallas import tpu as pltpu
from jax.sharding import PartitionSpec as P


def inverse_kernel(skew_ref, out_ref):
    extent = skew_ref.shape[-1]
    shape = skew_ref.shape
    row_at = lax.broadcasted_iota(jnp.int32, shape, 1)
    col_at = lax.broadcasted_iota(jnp.int32, shape, 2)
    skew = skew_ref[...]
    generator = skew - jnp.swapaxes(skew, 1, 2)
    out_ref[...] = jnp.where(row_at == col_at, 1.0, 0.0) + generator
    lane = lax.broadcasted_iota(jnp.int32, (shape[0], 1, extent), 2)

    def step(at, carry):
        work = out_ref[...]
        pivot_row = out_ref[:, pl.ds(at, 1), :]
        at_col = col_at == at
        pivot_col = jnp.sum(jnp.where(at_col, work, 0.0), axis=2, keepdims=True)
        pivot = jnp.sum(jnp.where(lane == at, pivot_row, 0.0), axis=2, keepdims=True)
        scale = 1.0 / pivot
        scaled_row = jnp.where(lane == at, 1.0, pivot_row) * scale
        cleared = jnp.where(at_col, 0.0, work)
        out_ref[...] = cleared - pivot_col * scaled_row
        out_ref[:, pl.ds(at, 1), :] = scaled_row
        return carry

    lax.fori_loop(0, extent, step, 0)


def cayley_inverse(skew_blocks):
    extent = skew_blocks.shape[-1]
    flat = skew_blocks.reshape(-1, extent, extent)
    out = pl.pallas_call(
        inverse_kernel,
        out_shape=jax.ShapeDtypeStruct(flat.shape, jnp.float32),
        in_specs=[pl.BlockSpec(memory_space=pltpu.VMEM)],
        out_specs=pl.BlockSpec(memory_space=pltpu.VMEM),
        cost_estimate=pl.CostEstimate(
            flops=50_000_000, bytes_accessed=2 * 4 * flat.size, transcendentals=0
        ),
        name="cayley_inverse",
    )(flat)
    return out.reshape(skew_blocks.shape)


def estimate(flops, *arrays):
    moved = sum(array.size * array.dtype.itemsize for array in arrays)
    return pl.CostEstimate(flops=flops, bytes_accessed=moved, transcendentals=0)


def pack(weight, half, cols):
    rows, width = weight.shape
    step = min(rows, 32)

    def body(in_ref, out_ref):
        for at in range(half):
            left = in_ref[:, at * cols : (at + 1) * cols]
            right = in_ref[:, (half + at) * cols : (half + at + 1) * cols]
            out_ref[at] = jnp.concatenate([left, right], axis=1)

    out = jax.ShapeDtypeStruct((half, rows, 2 * cols), weight.dtype)
    return pl.pallas_call(
        body,
        out_shape=out,
        grid=(rows // step,),
        in_specs=[pl.BlockSpec((step, width), lambda at: (at, 0))],
        out_specs=pl.BlockSpec((half, step, 2 * cols), lambda at: (0, at, 0)),
        cost_estimate=estimate(0, weight, out),
        name="pack",
    )(weight)


def dot(left, right, left_dim, right_dim):
    contract = (((left_dim,), (right_dim,)), ((), ()))
    return lax.dot_general(left, right, contract, preferred_element_type=jnp.float32)


def routes(places):
    count, digits = places.shape
    low = GROUP_BITS
    at = jnp.arange(digits, dtype=jnp.int32)
    hit = places[:, :, None] == at[None, None, :]
    slot_of = jnp.sum(jnp.where(hit, at[None, :, None], 0), axis=1)
    is_low = at[None, :] < low
    crosses = is_low != (slot_of < low)
    before = at[:, None] < at[None, :]
    same = (at[:, None] < low) == (at[None, :] < low)
    rank_cross = jnp.sum((crosses[:, :, None] & (before & same)[None]).astype(jnp.int32), axis=1)
    rank_stay = jnp.sum((~crosses[:, :, None] & (before & same)[None]).astype(jnp.int32), axis=1)
    inside = jnp.where(crosses, low - 1 - rank_cross, rank_stay)
    first = jnp.where(is_low, inside, at[None, :])
    second = jnp.where(is_low & ~crosses, inside, slot_of)
    second = jnp.where(~is_low & crosses, low - 1 - rank_cross, second)
    after = jnp.sum(jnp.where(hit, second[:, None, :], 0), axis=2)

    def spread(index, sources, targets):
        bits = jnp.right_shift(index[None, :, None], sources[:, None, :]) & 1
        return jnp.sum(jnp.left_shift(bits, targets[:, None, :]), axis=2)

    group = jnp.arange(1 << low, dtype=jnp.int32)
    natural = jnp.broadcast_to(at[None, :], (count, digits))
    take_first = spread(group, first[:, :low], natural[:, :low])
    take_last = spread(group, natural[:, :low], after[:, :low])
    tiles = jnp.arange((1 << digits) // TILE, dtype=jnp.int32) * TILE
    moves = spread(tiles, second, first)
    heads = (take_first[:, :, None] == group[None, None, :]).astype(jnp.bfloat16)
    tails = (take_last[:, :, None] == group[None, None, :]).astype(jnp.bfloat16)
    return heads, tails, moves


GROUP_BITS = 8
GROUP = 1 << GROUP_BITS
TILE = 8
STEPS = 8


def collect(moves_ref, base, source_ref, slot_ref):
    for pair in range(GROUP // (2 * TILE)):
        parts = []
        for half in range(2):
            start = pl.multiple_of(moves_ref[base + 2 * pair + half], TILE)
            parts.append(source_ref[pl.ds(start, TILE), :])
        rows = slice(2 * TILE * pair, 2 * TILE * (pair + 1))
        slot_ref[rows, :] = jnp.concatenate(parts, axis=0).astype(jnp.bfloat16)


def moved(moves_ref, base, source_ref, slot_ref, tail):
    collect(moves_ref, base, source_ref, slot_ref)
    return dot(tail, slot_ref[...], 1, 0).astype(jnp.bfloat16)


def flipped(index, bit):
    return index + (1 - 2 * ((index // (1 << bit)) % 2)) * (1 << bit)


def greet(bits):
    me = lax.axis_index("rows")
    barrier = pltpu.get_barrier_semaphore()
    for bit in range(bits):
        pl.semaphore_signal(
            barrier, inc=1, device_id={"rows": flipped(me, bit)}, device_id_type=pl.DeviceIdType.MESH
        )
    pl.semaphore_wait(barrier, bits)
    return me


def bit_orders(devices):
    down = list(reversed(range(devices.bit_length() - 1)))
    return [down, down[:-3] + [down[-2], down[-3], down[-1]]]


def gather_blocks(arrays, devices):
    bits = devices.bit_length() - 1
    orders = bit_orders(devices)
    count = len(arrays)
    streams = [(at, color) for at in range(count) for color in range(2)]

    def kernel(*refs):
        own_refs, out_refs = refs[:count], refs[count : 2 * count]
        send_sem, recv_sem, local_sem = refs[2 * count :]
        me = greet(bits)
        locals_ = []
        for at in range(count):
            local = pltpu.make_async_copy(own_refs[at], out_refs[at].at[me], local_sem.at[at])
            local.start()
            locals_.append(local)

        def part(at, color):
            rows, lanes = arrays[at].shape
            if rows % 32:
                return (slice(None), pl.ds(color * (lanes // 2), lanes // 2))
            return (pl.ds(color * (rows // 2), rows // 2), slice(None))

        def copy(stream, step, pattern):
            at, color = streams[stream]
            order = orders[color]
            block = me
            for level in range(step):
                if (pattern >> level) & 1:
                    block = flipped(block, order[level])
            piece = part(at, color)
            source = own_refs[at].at[piece] if pattern == 0 else out_refs[at].at[(block,) + piece]
            slot = pattern + (1 << step) - 1
            return pltpu.make_async_remote_copy(
                src_ref=source,
                dst_ref=out_refs[at].at[(block,) + piece],
                send_sem=send_sem.at[stream, slot],
                recv_sem=recv_sem.at[stream, slot],
                device_id={"rows": flipped(me, order[step])},
                device_id_type=pl.DeviceIdType.MESH,
            )

        copies = {}
        arrived = set()

        def arrive(stream, pattern):
            if pattern and (stream, pattern) not in arrived:
                arrived.add((stream, pattern))
                copies[stream, pattern].wait_recv()

        for step in range(bits):
            for pattern in range(1 << step):
                for stream in range(len(streams)):
                    arrive(stream, pattern)
                    made = copy(stream, step, pattern)
                    made.start()
                    copies[stream, pattern + (1 << step)] = made
        for pattern in range(1, devices):
            for stream in range(len(streams)):
                arrive(stream, pattern)
        for made in copies.values():
            made.wait_send()
        for local in locals_:
            local.wait()

    outs = tuple(jax.ShapeDtypeStruct((devices,) + own.shape, own.dtype) for own in arrays)
    anywhere = pl.BlockSpec(memory_space=pl.ANY)
    return pl.pallas_call(
        kernel,
        out_shape=outs,
        in_specs=[anywhere] * count,
        out_specs=(anywhere,) * count,
        scratch_shapes=[
            pltpu.SemaphoreType.DMA((2 * count, devices - 1)),
            pltpu.SemaphoreType.DMA((2 * count, devices - 1)),
            pltpu.SemaphoreType.DMA((count,)),
        ],
        compiler_params=pltpu.CompilerParams(collective_id=0, has_side_effects=True),
        cost_estimate=pl.CostEstimate(
            flops=0, bytes_accessed=32 * sum(2 * out.size for out in outs), transcendentals=0
        ),
        name="gather_blocks",
    )(*arrays)


def reduce_blocks(arrays, devices):
    _, rows, lanes = arrays[0].shape
    bits = devices.bit_length() - 1
    count = len(arrays)
    orders = [list(reversed(order)) for order in bit_orders(devices)]

    def kernel(*refs):
        in_refs = refs[:count]
        out_ref, acc, landed, send_sem, recv_sem = refs[count:]
        me = greet(bits)
        copies = {}

        def block_of(at, step, pattern, index):
            order = orders[at % 2]
            for level in range(step + 1, bits):
                if (pattern >> (level - step - 1)) & 1:
                    index = flipped(index, order[level])
            return index

        def send(at, step, pattern):
            other = flipped(me, orders[at % 2][step])
            if step == 0:
                source = in_refs[at].at[block_of(at, 0, pattern, other)]
            else:
                source = acc.at[at, (2 * pattern + 1) << (step - 1)]
            slot = (devices >> (step + 1)) + pattern - 1
            made = pltpu.make_async_remote_copy(
                src_ref=source,
                dst_ref=landed.at[at, slot],
                send_sem=send_sem.at[at, slot],
                recv_sem=recv_sem.at[at, slot],
                device_id={"rows": other},
                device_id_type=pl.DeviceIdType.MESH,
            )
            made.start()
            copies[at, step, pattern] = made

        def arrive(at, step, pattern):
            copies[at, step, pattern].wait_recv()
            slot = (devices >> (step + 1)) + pattern - 1
            if step == 0:
                kept = in_refs[at][block_of(at, 0, pattern, me)]
            else:
                kept = acc[at, (2 * pattern) << (step - 1)]
            total = kept.astype(jnp.float32) + landed[at, slot].astype(jnp.float32)
            if step == bits - 1:
                out_ref[at] = total
            else:
                acc[at, pattern << step] = total.astype(jnp.bfloat16)

        for pattern in [p for odd in (1, 0) for p in range(devices // 2) if p % 2 == odd]:
            for at in range(count):
                send(at, 0, pattern)
        for step in range(1, bits + 1):
            patterns = devices >> step
            for pattern in [p for odd in (1, 0) for p in range(patterns) if p % 2 == odd]:
                for at in range(count):
                    arrive(at, step - 1, pattern)
                    if step < bits and pattern % 2:
                        send(at, step, pattern // 2)
        for made in copies.values():
            made.wait_send()

    return pl.pallas_call(
        kernel,
        out_shape=jax.ShapeDtypeStruct((count, rows, lanes), jnp.float32),
        in_specs=[pl.BlockSpec(memory_space=pltpu.VMEM)] * count,
        out_specs=pl.BlockSpec(memory_space=pltpu.VMEM),
        scratch_shapes=[
            pltpu.VMEM((count, devices // 2, rows, lanes), jnp.bfloat16),
            pltpu.VMEM((count, devices - 1, rows, lanes), jnp.bfloat16),
            pltpu.SemaphoreType.DMA((count, devices - 1)),
            pltpu.SemaphoreType.DMA((count, devices - 1)),
        ],
        compiler_params=pltpu.CompilerParams(
            collective_id=1, has_side_effects=True, vmem_limit_bytes=32 << 20
        ),
        cost_estimate=pl.CostEstimate(flops=0, bytes_accessed=64 * arrays[0].size, transcendentals=0),
        name="reduce_blocks",
    )(*arrays)


def clamp(phase, wanted, at, last):
    return jnp.where(phase < wanted, 0, jnp.where(phase > wanted, last, at))


def rotate_tokens(all_tokens, rotation, heads, tails, moves, side, extent, mats):
    count, width = all_tokens.shape
    chunk = width // STEPS
    groups = chunk // GROUP
    tiles = GROUP // TILE
    all_tiles = width // TILE
    half_rows = width // 2
    half_chunk = half_rows // STEPS
    last = STEPS - 1

    def body(moves_ref, side_ref, tok_ref, rot_ref, heads_ref, tails_ref, top_ref, mid_ref, low_ref, za, zb, slot):
        m, phase, at = pl.program_id(0), pl.program_id(1), pl.program_id(2)

        def turned(block, value, section):
            parts = []
            for b in range(GROUP // extent):
                rows = slice(b * extent, (b + 1) * extent)
                both = rot_ref[pl.ds(block * GROUP + b * extent, extent), section * mats * extent : (section + 1) * mats * extent]
                own = jnp.where(m == 0, both[:, :extent], both[:, extent:])
                parts.append(dot(own, value[rows], 0, 0).astype(jnp.bfloat16))
            return jnp.concatenate(parts, axis=0)

        @pl.when(phase == 0)
        def _():
            for g in range(groups):
                piece = tok_ref[:, g * GROUP : (g + 1) * GROUP]
                za[pl.ds(at * chunk + g * GROUP, GROUP), :] = dot(heads_ref[0], piece, 1, 1)

        @pl.when(phase == 1)
        def _():
            for g in range(groups):
                value = moved(moves_ref, (at * groups + g) * tiles, za, slot.at[g], tails_ref[0])
                top_ref[g * GROUP : (g + 1) * GROUP, :] = value
                mixed = turned(g, value, 1)
                zb[pl.ds(at * chunk + g * GROUP, GROUP), :] = dot(heads_ref[1], mixed, 1, 0)

        @pl.when(phase == 2)
        def _():
            for g in range(groups):
                value = moved(moves_ref, all_tiles + (at * groups + g) * tiles, zb, slot.at[g], tails_ref[1])
                mid_ref[g * GROUP : (g + 1) * GROUP, :] = value
                mixed = turned(g, value, 0)
                za[pl.ds(at * chunk + g * GROUP, GROUP), :] = dot(heads_ref[2], mixed, 1, 0)

        @pl.when(phase == 3)
        def _():
            for g in range(half_chunk // GROUP):
                at_group = side_ref[0] * (half_rows // GROUP) + at * (half_chunk // GROUP) + g
                value = moved(moves_ref, 2 * all_tiles + at_group * tiles, za, slot.at[g], tails_ref[2])
                low_ref[g * GROUP : (g + 1) * GROUP, :] = value

    outs = (
        jax.ShapeDtypeStruct((width, count), jnp.bfloat16),
        jax.ShapeDtypeStruct((width, mats * count), jnp.bfloat16),
        jax.ShapeDtypeStruct((half_rows, mats * count), jnp.bfloat16),
    )
    whole = lambda m, phase, at: (0, 0, 0)
    return pl.pallas_call(
        body,
        out_shape=outs,
        grid=(mats, 4, STEPS),
        in_specs=[
            pl.BlockSpec(memory_space=pltpu.SMEM),
            pl.BlockSpec(memory_space=pltpu.SMEM),
            pl.BlockSpec((count, chunk), lambda m, phase, at: (0, jnp.where(phase == 0, at, last))),
            pl.BlockSpec(
                (chunk, rotation.shape[1]),
                lambda m, phase, at: (jnp.where(phase == 0, 0, jnp.where(phase == 3, last, at)), 0),
            ),
            pl.BlockSpec((3, GROUP, GROUP), whole),
            pl.BlockSpec((3, GROUP, GROUP), whole),
        ],
        out_specs=(
            pl.BlockSpec((chunk, count), lambda m, phase, at: (jnp.where(m == 0, clamp(phase, 1, at, last), clamp(phase, 1, at, last)), 0)),
            pl.BlockSpec((chunk, count), lambda m, phase, at: (clamp(phase, 2, at, last), m)),
            pl.BlockSpec((half_chunk, count), lambda m, phase, at: (clamp(phase, 3, at, last), m)),
        ),
        scratch_shapes=[
            pltpu.VMEM((width, count), jnp.float32),
            pltpu.VMEM((width, count), jnp.float32),
            pltpu.VMEM((groups, GROUP, count), jnp.bfloat16),
        ],
        compiler_params=pltpu.CompilerParams(vmem_limit_bytes=48 << 20),
        cost_estimate=estimate(14 * 2 * width * GROUP * count, all_tokens, rotation, *outs),
        name="rotate_tokens",
    )(moves, side, all_tokens, rotation, heads, tails)


def block_terms(pulled, mid, top, rotation, heads, tails, moves, side, extent, mats):
    half_rows = pulled.shape[0]
    width, count = top.shape
    chunk = width // STEPS
    groups = chunk // GROUP
    tiles = GROUP // TILE
    all_tiles = width // TILE
    half_chunk = half_rows // STEPS
    last = STEPS - 1

    def body(moves_ref, side_ref, pulled_ref, mid_ref, top_ref, rot_ref, heads_ref, tails_ref, terms_0_ref, terms_1_ref, za, zb, slot, kept_0, kept_1):
        m, phase, at = pl.program_id(0), pl.program_id(1), pl.program_id(2)
        lane_mat = lax.broadcasted_iota(jnp.int32, (chunk, mats * extent), 1) // extent
        chunk_rows = pl.ds(pl.multiple_of(at * chunk, chunk), chunk)
        block_row = lax.broadcasted_iota(jnp.int32, (GROUP, GROUP), 0) // extent
        block_col = lax.broadcasted_iota(jnp.int32, (GROUP, GROUP), 1) // extent
        same_block = block_row == block_col

        def emit(out_ref, kept, left_ref, tail):
            grams = [
                dot(left_ref[g * GROUP : (g + 1) * GROUP, :], slot[g], 1, 1).astype(jnp.bfloat16)
                for g in range(groups)
            ]
            terms = [dot(gram, tail, 1, 1) for gram in grams]
            parts = []
            for g in range(groups):
                for b in range(GROUP // extent):
                    pair = b // mats * mats * extent
                    piece = terms[g][b * extent : (b + 1) * extent, pair : pair + mats * extent]
                    parts.append(jnp.where(m == b % mats, piece, pltpu.roll(piece, extent, 1)))
            placed = jnp.concatenate(parts, axis=0)
            both = jnp.where(lane_mat == m, placed, kept[chunk_rows, :])
            kept[chunk_rows, :] = both
            out_ref[...] = both.astype(jnp.bfloat16)

        @pl.when(phase == 0)
        def _():
            own = side_ref[0] * half_rows + at * half_chunk
            other = (1 - side_ref[0]) * half_rows + at * half_chunk
            za[pl.ds(pl.multiple_of(other, half_chunk), half_chunk), :] = jnp.zeros((half_chunk, count), jnp.float32)
            for g in range(half_chunk // GROUP):
                piece = pulled_ref[g * GROUP : (g + 1) * GROUP, :]
                za[pl.ds(pl.multiple_of(own + g * GROUP, GROUP), GROUP), :] = dot(heads_ref[0], piece, 1, 0)

        @pl.when(phase == 1)
        def _():
            for g in range(groups):
                collect(moves_ref, (at * groups + g) * tiles, za, slot.at[g])
            merged = []
            for g in range(groups):
                both = rot_ref[g * GROUP : (g + 1) * GROUP, : mats * extent]
                own = jnp.where(m == 0, both[:, :extent], both[:, extent:])
                tiled = jnp.concatenate([own] * (GROUP // extent), axis=1)
                block = jnp.where(same_block, tiled, jnp.zeros_like(tiled))
                merged.append(dot(block, tails_ref[0], 1, 0).astype(jnp.bfloat16))
            merged = [dot(heads_ref[1], value, 1, 0).astype(jnp.bfloat16) for value in merged]
            emit(terms_0_ref, kept_0, mid_ref, tails_ref[0])
            for g in range(groups):
                zb[pl.ds(at * chunk + g * GROUP, GROUP), :] = dot(merged[g], slot[g], 1, 0)

        @pl.when(phase == 2)
        def _():
            for g in range(groups):
                collect(moves_ref, all_tiles + (at * groups + g) * tiles, zb, slot.at[g])
            emit(terms_1_ref, kept_1, top_ref, tails_ref[1])

    out = jax.ShapeDtypeStruct((width, mats * extent), jnp.bfloat16)
    whole = lambda m, phase, at: (0, 0, 0)
    return pl.pallas_call(
        body,
        out_shape=(out, out),
        grid=(mats, 3, STEPS),
        in_specs=[
            pl.BlockSpec(memory_space=pltpu.SMEM),
            pl.BlockSpec(memory_space=pltpu.SMEM),
            pl.BlockSpec((half_chunk, count), lambda m, phase, at: (clamp(phase, 0, at, last), m)),
            pl.BlockSpec((chunk, count), lambda m, phase, at: (clamp(phase, 1, at, last), m)),
            pl.BlockSpec((chunk, count), lambda m, phase, at: (clamp(phase, 2, at, last), 0)),
            pl.BlockSpec((chunk, rotation.shape[1]), lambda m, phase, at: (clamp(phase, 1, at, last), 0)),
            pl.BlockSpec((2, GROUP, GROUP), whole),
            pl.BlockSpec((2, GROUP, GROUP), whole),
        ],
        out_specs=(
            pl.BlockSpec((chunk, mats * extent), lambda m, phase, at: (jnp.where(m == mats - 1, clamp(phase, 1, at, last), 0), 0)),
            pl.BlockSpec((chunk, mats * extent), lambda m, phase, at: (jnp.where(m == mats - 1, clamp(phase, 2, at, last), 0), 0)),
        ),
        scratch_shapes=[
            pltpu.VMEM((width, count), jnp.float32),
            pltpu.VMEM((width, count), jnp.float32),
            pltpu.VMEM((groups, GROUP, count), jnp.bfloat16),
            pltpu.VMEM((width, mats * extent), jnp.float32),
            pltpu.VMEM((width, mats * extent), jnp.float32),
        ],
        compiler_params=pltpu.CompilerParams(vmem_limit_bytes=52 << 20),
        cost_estimate=estimate(14 * 2 * width * GROUP * count, pulled, mid, top, rotation, out, out),
        name="block_terms",
    )(moves, side, pulled, mid, top, rotation, heads, tails)


def pull(gate_cols, up_cols, gate_grad, up_grad):
    rows, width = gate_cols.shape
    count = gate_grad.shape[0]
    step = min(512, rows)

    def body(gate_ref, up_ref, gate_grad_ref, up_grad_ref, out_ref):
        out_ref[:, :count] = dot(gate_ref[...], gate_grad_ref[...], 1, 1).astype(jnp.bfloat16)
        out_ref[:, count:] = dot(up_ref[...], up_grad_ref[...], 1, 1).astype(jnp.bfloat16)

    out = jax.ShapeDtypeStruct((rows, 2 * count), jnp.bfloat16)
    weights = pl.BlockSpec((step, width), lambda at: (at, 0))
    grads = pl.BlockSpec((count, width), lambda at: (0, 0))
    return pl.pallas_call(
        body,
        out_shape=out,
        grid=(rows // step,),
        in_specs=[weights, weights, grads, grads],
        out_specs=pl.BlockSpec((step, 2 * count), lambda at: (at, 0)),
        cost_estimate=estimate(4 * rows * width * count, gate_cols, up_cols, out),
        name="pull",
    )(gate_cols, up_cols, gate_grad, up_grad)


def places_of(bits, section_row):
    places = jnp.arange(section_row.shape[0], dtype=jnp.int32)
    found = bits[:, None] == section_row[None, :]
    return jnp.sum(jnp.where(found, places[None, :], 0), axis=1)


def shards(tokens, gate_weight, up_weight, skew_params, section_bits, upstream):
    mats, _, own_blocks, extent, _ = skew_params.shape
    own_rows = gate_weight.shape[0]
    own_cols = upstream.shape[1]
    devices = gate_weight.shape[1] // own_cols
    half = devices // 2
    half_rows = half * own_rows
    side = lax.axis_index("rows") // half
    groups = [list(range(half)), list(range(half, devices))]
    swap = [(at, (at + half) % devices) for at in range(devices)]

    def move(parts):
        moved = lax.all_to_all(
            parts, "rows", split_axis=0, concat_axis=0, axis_index_groups=groups, tiled=True
        )
        return moved.reshape(half_rows, 2 * own_cols)

    bits_0, bits_1 = section_bits[0], section_bits[1]
    natural = jnp.arange(bits_0.shape[0], dtype=jnp.int32)
    inverse_0 = places_of(natural, bits_0)
    one_to_zero = places_of(bits_0, bits_1)
    zero_to_one = places_of(bits_1, bits_0)
    heads, tails, moves = routes(jnp.stack([bits_1, one_to_zero, inverse_0, bits_0, zero_to_one]))
    side_at = jnp.reshape(side, (1,)).astype(jnp.int32)

    skew_params, gate_parts = lax.optimization_barrier((skew_params, pack(gate_weight, half, own_cols)))
    gate_cols = move(gate_parts)
    other_upstream = lax.ppermute(upstream, "rows", swap)
    inverse = cayley_inverse(skew_params)
    own_rotation = (2.0 * inverse - jnp.eye(extent, dtype=jnp.float32)).astype(jnp.bfloat16)
    packed = own_rotation.transpose(2, 3, 1, 0, 4).reshape(own_blocks * extent, -1)
    up_weight, packed = lax.optimization_barrier((up_weight, packed))
    packed, up_parts = lax.optimization_barrier((packed, pack(up_weight, half, own_cols)))
    all_tokens, rotation = gather_blocks((tokens, packed), devices)
    all_tokens = all_tokens.reshape(-1, tokens.shape[1])
    rotation = rotation.reshape(devices * own_blocks * extent, -1)
    token_count = all_tokens.shape[0]
    all_tokens, gate_cols, up_parts, other_upstream = lax.optimization_barrier(
        (all_tokens, gate_cols, up_parts, other_upstream)
    )
    up_cols = move(up_parts)
    top_tokens, mid, low = rotate_tokens(
        all_tokens, rotation, heads[:3], tails[:3], moves[:3].reshape(-1), side_at, extent, mats
    )

    def project(at, columns):
        part = dot(low[:, at * token_count : (at + 1) * token_count], columns, 0, 0)
        return part + lax.ppermute(part.astype(jnp.bfloat16), "rows", swap).astype(jnp.float32)

    gate_pre = project(0, gate_cols)
    up_pre = project(1, up_cols)
    sigmoid_val = jax.nn.sigmoid(gate_pre)
    silu_val = gate_pre * sigmoid_val
    activation = (silu_val * up_pre).astype(jnp.bfloat16)
    activation = jnp.where(side == 0, activation[:, :own_cols], activation[:, own_cols:])
    first = jnp.where(side == 0, upstream, other_upstream)
    second = jnp.where(side == 0, other_upstream, upstream)
    cotangent = jnp.concatenate([first, second], axis=1).astype(jnp.float32)
    gate_grad = (cotangent * up_pre * sigmoid_val * (1.0 + gate_pre * (1.0 - sigmoid_val))).astype(
        jnp.bfloat16
    )
    up_grad = (cotangent * silu_val).astype(jnp.bfloat16)

    pulled = pull(gate_cols, up_cols, gate_grad, up_grad)
    terms_0, terms_1 = block_terms(
        pulled, mid, top_tokens, rotation, heads[3:], tails[3:], moves[3:].reshape(-1), side_at, extent, mats
    )

    def ordered(summed):
        return summed.reshape(own_blocks, extent, mats, extent).transpose(2, 0, 1, 3)

    by_owner = (devices, own_blocks * extent, mats * extent)
    summed = reduce_blocks((terms_0.reshape(by_owner), terms_1.reshape(by_owner)), devices)
    factor_grad = jnp.stack([ordered(summed[0]), ordered(summed[1])], axis=1)

    left = jnp.einsum(
        "mskab,mskac->mskbc", inverse, factor_grad, precision=lax.Precision.HIGHEST
    )
    generator_grad = -2.0 * jnp.einsum(
        "mskbc,mskdc->mskbd", left, inverse, precision=lax.Precision.HIGHEST
    )
    skew_grad = generator_grad - jnp.swapaxes(generator_grad, -1, -2)
    return (activation, skew_grad)


def solution(mesh):
    placed = (
        P(("groups", "rows"), None),
        P("rows", None),
        P("rows", None),
        P(None, None, "rows", None, None),
        P(),
        P("groups", "rows"),
    )
    return jax.shard_map(
        shards,
        mesh=mesh,
        in_specs=placed,
        out_specs=(P("groups", "rows"), P("groups", None, "rows", None, None)),
        check_vma=False,
    )
```

```python
import jax
import jax.numpy as jnp
from jax import lax
from jax.experimental import pallas as pl
from jax.experimental.pallas import tpu as pltpu
from jax.sharding import PartitionSpec as P


def inverse_kernel(skew_ref, out_ref):
    extent = skew_ref.shape[-1]
    shape = skew_ref.shape
    row_at = lax.broadcasted_iota(jnp.int32, shape, 1)
    col_at = lax.broadcasted_iota(jnp.int32, shape, 2)
    skew = skew_ref[...]
    generator = skew - jnp.swapaxes(skew, 1, 2)
    out_ref[...] = jnp.where(row_at == col_at, 1.0, 0.0) + generator
    lane = lax.broadcasted_iota(jnp.int32, (shape[0], 1, extent), 2)

    def step(at, carry):
        work = out_ref[...]
        pivot_row = out_ref[:, pl.ds(at, 1), :]
        at_col = col_at == at
        pivot_col = jnp.sum(jnp.where(at_col, work, 0.0), axis=2, keepdims=True)
        pivot = jnp.sum(jnp.where(lane == at, pivot_row, 0.0), axis=2, keepdims=True)
        scale = 1.0 / pivot
        scaled_row = jnp.where(lane == at, 1.0, pivot_row) * scale
        cleared = jnp.where(at_col, 0.0, work)
        out_ref[...] = cleared - pivot_col * scaled_row
        out_ref[:, pl.ds(at, 1), :] = scaled_row
        return carry

    lax.fori_loop(0, extent, step, 0)


def cayley_inverse(skew_blocks):
    extent = skew_blocks.shape[-1]
    flat = skew_blocks.reshape(-1, extent, extent)
    out = pl.pallas_call(
        inverse_kernel,
        out_shape=jax.ShapeDtypeStruct(flat.shape, jnp.float32),
        in_specs=[pl.BlockSpec(memory_space=pltpu.VMEM)],
        out_specs=pl.BlockSpec(memory_space=pltpu.VMEM),
        cost_estimate=pl.CostEstimate(
            flops=50_000_000, bytes_accessed=2 * 4 * flat.size, transcendentals=0
        ),
        name="cayley_inverse",
    )(flat)
    return out.reshape(skew_blocks.shape)


def estimate(flops, *arrays):
    moved = sum(array.size * array.dtype.itemsize for array in arrays)
    return pl.CostEstimate(flops=flops, bytes_accessed=moved, transcendentals=0)


def pack(weight, half, cols):
    rows, width = weight.shape
    step = min(rows, 32)

    def body(in_ref, out_ref):
        for at in range(half):
            left = in_ref[:, at * cols : (at + 1) * cols]
            right = in_ref[:, (half + at) * cols : (half + at + 1) * cols]
            out_ref[at] = jnp.concatenate([left, right], axis=1)

    out = jax.ShapeDtypeStruct((half, rows, 2 * cols), weight.dtype)
    return pl.pallas_call(
        body,
        out_shape=out,
        grid=(rows // step,),
        in_specs=[pl.BlockSpec((step, width), lambda at: (at, 0))],
        out_specs=pl.BlockSpec((half, step, 2 * cols), lambda at: (0, at, 0)),
        cost_estimate=estimate(0, weight, out),
        name="pack",
    )(weight)


def dot(left, right, left_dim, right_dim):
    contract = (((left_dim,), (right_dim,)), ((), ()))
    return lax.dot_general(left, right, contract, preferred_element_type=jnp.float32)


def routes(places):
    count, digits = places.shape
    low = GROUP_BITS
    at = jnp.arange(digits, dtype=jnp.int32)
    hit = places[:, :, None] == at[None, None, :]
    slot_of = jnp.sum(jnp.where(hit, at[None, :, None], 0), axis=1)
    is_low = at[None, :] < low
    crosses = is_low != (slot_of < low)
    before = at[:, None] < at[None, :]
    same = (at[:, None] < low) == (at[None, :] < low)
    rank_cross = jnp.sum((crosses[:, :, None] & (before & same)[None]).astype(jnp.int32), axis=1)
    rank_stay = jnp.sum((~crosses[:, :, None] & (before & same)[None]).astype(jnp.int32), axis=1)
    inside = jnp.where(crosses, low - 1 - rank_cross, rank_stay)
    first = jnp.where(is_low, inside, at[None, :])
    second = jnp.where(is_low & ~crosses, inside, slot_of)
    second = jnp.where(~is_low & crosses, low - 1 - rank_cross, second)
    after = jnp.sum(jnp.where(hit, second[:, None, :], 0), axis=2)

    def spread(index, sources, targets):
        bits = jnp.right_shift(index[None, :, None], sources[:, None, :]) & 1
        return jnp.sum(jnp.left_shift(bits, targets[:, None, :]), axis=2)

    group = jnp.arange(1 << low, dtype=jnp.int32)
    natural = jnp.broadcast_to(at[None, :], (count, digits))
    take_first = spread(group, first[:, :low], natural[:, :low])
    take_last = spread(group, natural[:, :low], after[:, :low])
    tiles = jnp.arange((1 << digits) // TILE, dtype=jnp.int32) * TILE
    moves = spread(tiles, second, first)
    heads = (take_first[:, :, None] == group[None, None, :]).astype(jnp.bfloat16)
    tails = (take_last[:, :, None] == group[None, None, :]).astype(jnp.bfloat16)
    return heads, tails, moves


GROUP_BITS = 8
GROUP = 1 << GROUP_BITS
TILE = 8
STEPS = 8


def collect(moves_ref, base, source_ref, slot_ref):
    for pair in range(GROUP // (2 * TILE)):
        parts = []
        for half in range(2):
            start = pl.multiple_of(moves_ref[base + 2 * pair + half], TILE)
            parts.append(source_ref[pl.ds(start, TILE), :])
        rows = slice(2 * TILE * pair, 2 * TILE * (pair + 1))
        slot_ref[rows, :] = jnp.concatenate(parts, axis=0).astype(jnp.bfloat16)


def flipped(index, bit):
    return index + (1 - 2 * ((index // (1 << bit)) % 2)) * (1 << bit)


def greet(bits):
    me = lax.axis_index("rows")
    barrier = pltpu.get_barrier_semaphore()
    for bit in range(bits):
        pl.semaphore_signal(
            barrier, inc=1, device_id={"rows": flipped(me, bit)}, device_id_type=pl.DeviceIdType.MESH
        )
    pl.semaphore_wait(barrier, bits)
    return me


def bit_orders(devices):
    down = list(reversed(range(devices.bit_length() - 1)))
    return [down, down[:-3] + [down[-2], down[-3], down[-1]]]


def gather_blocks(arrays, devices):
    bits = devices.bit_length() - 1
    down = list(reversed(range(bits)))
    high, (far, near, core) = down[:-3], down[-3:]
    orders = [high + [far, near, core], high + [near, far, core], [near, far] + high + [core], [far, near] + high + [core]]
    count = len(arrays)
    streams = [(at, color) for color in range(4) for at in range(count)]

    def kernel(*refs):
        own_refs, out_refs = refs[:count], refs[count : 2 * count]
        send_sem, recv_sem, local_sem = refs[2 * count :]
        me = greet(bits)
        locals_ = []
        for at in range(count):
            local = pltpu.make_async_copy(own_refs[at], out_refs[at].at[me], local_sem.at[at])
            local.start()
            locals_.append(local)

        def part(at, color):
            rows, lanes = arrays[at].shape
            extent = rows if rows % 64 == 0 else lanes
            eighths = (0, 3, 6, 7, 8) if extent % 128 == 0 else (0, 2, 4, 6, 8)
            begin, end = (extent * eighths[color + at] // 8 for at in range(2))
            if extent == rows:
                return (pl.ds(begin, end - begin), slice(None))
            return (slice(None), pl.ds(begin, end - begin))

        def copy(stream, step, pattern):
            at, color = streams[stream]
            order = orders[color]
            block = me
            for level in range(step):
                if (pattern >> level) & 1:
                    block = flipped(block, order[level])
            piece = part(at, color)
            source = own_refs[at].at[piece] if pattern == 0 else out_refs[at].at[(block,) + piece]
            slot = pattern + (1 << step) - 1
            return pltpu.make_async_remote_copy(
                src_ref=source,
                dst_ref=out_refs[at].at[(block,) + piece],
                send_sem=send_sem.at[stream, slot],
                recv_sem=recv_sem.at[stream, slot],
                device_id={"rows": flipped(me, order[step])},
                device_id_type=pl.DeviceIdType.MESH,
            )

        copies = {}
        arrived = set()

        def arrive(stream, pattern):
            if pattern and (stream, pattern) not in arrived:
                arrived.add((stream, pattern))
                copies[stream, pattern].wait_recv()

        for step in range(bits):
            for pattern in range(1 << step):
                for stream in range(len(streams)):
                    arrive(stream, pattern)
                    made = copy(stream, step, pattern)
                    made.start()
                    copies[stream, pattern + (1 << step)] = made
        for pattern in range(1, devices):
            for stream in range(len(streams)):
                arrive(stream, pattern)
        for made in copies.values():
            made.wait_send()
        for local in locals_:
            local.wait()

    outs = tuple(jax.ShapeDtypeStruct((devices,) + own.shape, own.dtype) for own in arrays)
    anywhere = pl.BlockSpec(memory_space=pl.ANY)
    return pl.pallas_call(
        kernel,
        out_shape=outs,
        in_specs=[anywhere] * count,
        out_specs=(anywhere,) * count,
        scratch_shapes=[
            pltpu.SemaphoreType.DMA((4 * count, devices - 1)),
            pltpu.SemaphoreType.DMA((4 * count, devices - 1)),
            pltpu.SemaphoreType.DMA((count,)),
        ],
        compiler_params=pltpu.CompilerParams(collective_id=0, has_side_effects=True),
        cost_estimate=pl.CostEstimate(
            flops=0, bytes_accessed=32 * sum(2 * out.size for out in outs), transcendentals=0
        ),
        name="gather_blocks",
    )(*arrays)


def reduce_blocks(arrays, devices):
    _, rows, lanes = arrays[0].shape
    bits = devices.bit_length() - 1
    count = len(arrays)
    orders = [list(reversed(order)) for order in bit_orders(devices)]

    def kernel(*refs):
        in_refs = refs[:count]
        out_ref, acc, landed, send_sem, recv_sem = refs[count:]
        me = greet(bits)
        copies = {}

        def block_of(at, step, pattern, index):
            order = orders[at % 2]
            for level in range(step + 1, bits):
                if (pattern >> (level - step - 1)) & 1:
                    index = flipped(index, order[level])
            return index

        def send(at, step, pattern):
            other = flipped(me, orders[at % 2][step])
            if step == 0:
                source = in_refs[at].at[block_of(at, 0, pattern, other)]
            else:
                source = acc.at[at, (2 * pattern + 1) << (step - 1)]
            slot = (devices >> (step + 1)) + pattern - 1
            made = pltpu.make_async_remote_copy(
                src_ref=source,
                dst_ref=landed.at[at, slot],
                send_sem=send_sem.at[at, slot],
                recv_sem=recv_sem.at[at, slot],
                device_id={"rows": other},
                device_id_type=pl.DeviceIdType.MESH,
            )
            made.start()
            copies[at, step, pattern] = made

        def arrive(at, step, pattern):
            copies[at, step, pattern].wait_recv()
            slot = (devices >> (step + 1)) + pattern - 1
            if step == 0:
                kept = in_refs[at][block_of(at, 0, pattern, me)]
            else:
                kept = acc[at, (2 * pattern) << (step - 1)]
            total = kept.astype(jnp.float32) + landed[at, slot].astype(jnp.float32)
            if step == bits - 1:
                out_ref[at] = total
            else:
                acc[at, pattern << step] = total.astype(jnp.bfloat16)

        for pattern in [p for odd in (1, 0) for p in range(devices // 2) if p % 2 == odd]:
            for at in range(count):
                send(at, 0, pattern)
        for step in range(1, bits + 1):
            patterns = devices >> step
            for pattern in [p for odd in (1, 0) for p in range(patterns) if p % 2 == odd]:
                for at in range(count):
                    arrive(at, step - 1, pattern)
                    if step < bits and pattern % 2:
                        send(at, step, pattern // 2)
        for made in copies.values():
            made.wait_send()

    return pl.pallas_call(
        kernel,
        out_shape=jax.ShapeDtypeStruct((count, rows, lanes), jnp.float32),
        in_specs=[pl.BlockSpec(memory_space=pltpu.VMEM)] * count,
        out_specs=pl.BlockSpec(memory_space=pltpu.VMEM),
        scratch_shapes=[
            pltpu.VMEM((count, devices // 2, rows, lanes), jnp.bfloat16),
            pltpu.VMEM((count, devices - 1, rows, lanes), jnp.bfloat16),
            pltpu.SemaphoreType.DMA((count, devices - 1)),
            pltpu.SemaphoreType.DMA((count, devices - 1)),
        ],
        compiler_params=pltpu.CompilerParams(
            collective_id=1, has_side_effects=True, vmem_limit_bytes=32 << 20
        ),
        cost_estimate=pl.CostEstimate(flops=0, bytes_accessed=64 * arrays[0].size, transcendentals=0),
        name="reduce_blocks",
    )(*arrays)


def clamp(phase, wanted, at, last):
    return jnp.where(phase < wanted, 0, jnp.where(phase > wanted, last, at))


def rotate_tokens(all_tokens, rotation, heads, tails, moves, side, extent, mats):
    count, width = all_tokens.shape
    chunk = width // STEPS
    groups = chunk // GROUP
    tiles = GROUP // TILE
    all_tiles = width // TILE
    half_rows = width // 2
    half_chunk = half_rows // STEPS
    last = STEPS - 1

    def body(moves_ref, side_ref, tok_ref, rot_ref, heads_ref, tails_ref, top_ref, mid_ref, low_ref, za, zb, slot):
        m, phase, at = pl.program_id(0), pl.program_id(1), pl.program_id(2)

        block_row = lax.broadcasted_iota(jnp.int32, (GROUP, GROUP), 0) // extent
        block_col = lax.broadcasted_iota(jnp.int32, (GROUP, GROUP), 1) // extent
        same_block = block_row == block_col

        def turned(values, section):
            blocks = []
            for g in range(groups):
                both = rot_ref[g * GROUP : (g + 1) * GROUP, section * mats * extent : (section + 1) * mats * extent]
                own = jnp.where(m == 0, both[:, :extent], both[:, extent:])
                tiled = jnp.concatenate([own] * (GROUP // extent), axis=1)
                blocks.append(jnp.where(same_block, tiled, jnp.zeros_like(tiled)))
            return [dot(block, value, 0, 0).astype(jnp.bfloat16) for block, value in zip(blocks, values)]

        def stage(base, source, out_ref, perm, section, target):
            for g in range(groups):
                collect(moves_ref, base + (at * groups + g) * tiles, source, slot.at[g])
            values = [dot(tails_ref[perm], slot[g], 1, 0).astype(jnp.bfloat16) for g in range(groups)]
            for g in range(groups):
                out_ref[g * GROUP : (g + 1) * GROUP, :] = values[g]
            mixed = turned(values, section)
            for g in range(groups):
                target[pl.ds(at * chunk + g * GROUP, GROUP), :] = dot(heads_ref[perm + 1], mixed[g], 1, 0)

        @pl.when(phase == 0)
        def _():
            for g in range(groups):
                piece = tok_ref[:, g * GROUP : (g + 1) * GROUP]
                za[pl.ds(at * chunk + g * GROUP, GROUP), :] = dot(heads_ref[0], piece, 1, 1)

        @pl.when(phase == 1)
        def _():
            stage(0, za, top_ref, 0, 1, zb)

        @pl.when(phase == 2)
        def _():
            stage(all_tiles, zb, mid_ref, 1, 0, za)

        @pl.when(phase == 3)
        def _():
            low_groups = half_chunk // GROUP
            for g in range(low_groups):
                at_group = side_ref[0] * (half_rows // GROUP) + at * low_groups + g
                collect(moves_ref, 2 * all_tiles + at_group * tiles, za, slot.at[g])
            for g in range(low_groups):
                value = dot(tails_ref[2], slot[g], 1, 0)
                low_ref[g * GROUP : (g + 1) * GROUP, :] = value.astype(jnp.bfloat16)

    outs = (
        jax.ShapeDtypeStruct((width, count), jnp.bfloat16),
        jax.ShapeDtypeStruct((width, mats * count), jnp.bfloat16),
        jax.ShapeDtypeStruct((half_rows, mats * count), jnp.bfloat16),
    )
    whole = lambda m, phase, at: (0, 0, 0)
    return pl.pallas_call(
        body,
        out_shape=outs,
        grid=(mats, 4, STEPS),
        in_specs=[
            pl.BlockSpec(memory_space=pltpu.SMEM),
            pl.BlockSpec(memory_space=pltpu.SMEM),
            pl.BlockSpec((count, chunk), lambda m, phase, at: (0, jnp.where(phase == 0, at, last))),
            pl.BlockSpec(
                (chunk, rotation.shape[1]),
                lambda m, phase, at: (jnp.where(phase == 0, 0, jnp.where(phase == 3, last, at)), 0),
            ),
            pl.BlockSpec((3, GROUP, GROUP), whole),
            pl.BlockSpec((3, GROUP, GROUP), whole),
        ],
        out_specs=(
            pl.BlockSpec((chunk, count), lambda m, phase, at: (jnp.where(m == 0, clamp(phase, 1, at, last), clamp(phase, 1, at, last)), 0)),
            pl.BlockSpec((chunk, count), lambda m, phase, at: (clamp(phase, 2, at, last), m)),
            pl.BlockSpec((half_chunk, count), lambda m, phase, at: (clamp(phase, 3, at, last), m)),
        ),
        scratch_shapes=[
            pltpu.VMEM((width, count), jnp.float32),
            pltpu.VMEM((width, count), jnp.float32),
            pltpu.VMEM((groups, GROUP, count), jnp.bfloat16),
        ],
        compiler_params=pltpu.CompilerParams(vmem_limit_bytes=48 << 20),
        cost_estimate=estimate(14 * 2 * width * GROUP * count, all_tokens, rotation, *outs),
        name="rotate_tokens",
    )(moves, side, all_tokens, rotation, heads, tails)


def block_terms(pulled, mid, top, rotation, heads, tails, moves, side, extent, mats):
    half_rows = pulled.shape[0]
    width, count = top.shape
    chunk = width // STEPS
    groups = chunk // GROUP
    tiles = GROUP // TILE
    all_tiles = width // TILE
    half_chunk = half_rows // STEPS
    last = STEPS - 1

    def body(moves_ref, side_ref, pulled_ref, mid_ref, top_ref, rot_ref, heads_ref, tails_ref, terms_0_ref, terms_1_ref, za, zb, slot, kept_0, kept_1):
        m, phase, at = pl.program_id(0), pl.program_id(1), pl.program_id(2)
        lane_mat = lax.broadcasted_iota(jnp.int32, (chunk, mats * extent), 1) // extent
        chunk_rows = pl.ds(pl.multiple_of(at * chunk, chunk), chunk)
        block_row = lax.broadcasted_iota(jnp.int32, (GROUP, GROUP), 0) // extent
        block_col = lax.broadcasted_iota(jnp.int32, (GROUP, GROUP), 1) // extent
        same_block = block_row == block_col

        def emit(out_ref, kept, left_ref, tail):
            grams = [
                dot(left_ref[g * GROUP : (g + 1) * GROUP, :], slot[g], 1, 1).astype(jnp.bfloat16)
                for g in range(groups)
            ]
            terms = [dot(gram, tail, 1, 1) for gram in grams]
            parts = []
            for g in range(groups):
                for b in range(GROUP // extent):
                    pair = b // mats * mats * extent
                    piece = terms[g][b * extent : (b + 1) * extent, pair : pair + mats * extent]
                    parts.append(jnp.where(m == b % mats, piece, pltpu.roll(piece, extent, 1)))
            placed = jnp.concatenate(parts, axis=0)
            both = jnp.where(lane_mat == m, placed, kept[chunk_rows, :])
            kept[chunk_rows, :] = both
            out_ref[...] = both.astype(jnp.bfloat16)

        @pl.when(phase == 0)
        def _():
            own = side_ref[0] * half_rows + at * half_chunk
            other = (1 - side_ref[0]) * half_rows + at * half_chunk
            za[pl.ds(pl.multiple_of(other, half_chunk), half_chunk), :] = jnp.zeros((half_chunk, count), jnp.float32)
            for g in range(half_chunk // GROUP):
                piece = pulled_ref[g * GROUP : (g + 1) * GROUP, :]
                za[pl.ds(pl.multiple_of(own + g * GROUP, GROUP), GROUP), :] = dot(heads_ref[0], piece, 1, 0)

        @pl.when(phase == 1)
        def _():
            for g in range(groups):
                collect(moves_ref, (at * groups + g) * tiles, za, slot.at[g])
            merged = []
            for g in range(groups):
                both = rot_ref[g * GROUP : (g + 1) * GROUP, : mats * extent]
                own = jnp.where(m == 0, both[:, :extent], both[:, extent:])
                tiled = jnp.concatenate([own] * (GROUP // extent), axis=1)
                block = jnp.where(same_block, tiled, jnp.zeros_like(tiled))
                merged.append(dot(block, tails_ref[0], 1, 0).astype(jnp.bfloat16))
            merged = [dot(heads_ref[1], value, 1, 0).astype(jnp.bfloat16) for value in merged]
            emit(terms_0_ref, kept_0, mid_ref, tails_ref[0])
            for g in range(groups):
                zb[pl.ds(at * chunk + g * GROUP, GROUP), :] = dot(merged[g], slot[g], 1, 0)

        @pl.when(phase == 2)
        def _():
            for g in range(groups):
                collect(moves_ref, all_tiles + (at * groups + g) * tiles, zb, slot.at[g])
            emit(terms_1_ref, kept_1, top_ref, tails_ref[1])

    out = jax.ShapeDtypeStruct((width, mats * extent), jnp.bfloat16)
    whole = lambda m, phase, at: (0, 0, 0)
    return pl.pallas_call(
        body,
        out_shape=(out, out),
        grid=(mats, 3, STEPS),
        in_specs=[
            pl.BlockSpec(memory_space=pltpu.SMEM),
            pl.BlockSpec(memory_space=pltpu.SMEM),
            pl.BlockSpec((half_chunk, count), lambda m, phase, at: (clamp(phase, 0, at, last), m)),
            pl.BlockSpec((chunk, count), lambda m, phase, at: (clamp(phase, 1, at, last), m)),
            pl.BlockSpec((chunk, count), lambda m, phase, at: (clamp(phase, 2, at, last), 0)),
            pl.BlockSpec((chunk, rotation.shape[1]), lambda m, phase, at: (clamp(phase, 1, at, last), 0)),
            pl.BlockSpec((2, GROUP, GROUP), whole),
            pl.BlockSpec((2, GROUP, GROUP), whole),
        ],
        out_specs=(
            pl.BlockSpec((chunk, mats * extent), lambda m, phase, at: (jnp.where(m == mats - 1, clamp(phase, 1, at, last), 0), 0)),
            pl.BlockSpec((chunk, mats * extent), lambda m, phase, at: (jnp.where(m == mats - 1, clamp(phase, 2, at, last), 0), 0)),
        ),
        scratch_shapes=[
            pltpu.VMEM((width, count), jnp.float32),
            pltpu.VMEM((width, count), jnp.float32),
            pltpu.VMEM((groups, GROUP, count), jnp.bfloat16),
            pltpu.VMEM((width, mats * extent), jnp.float32),
            pltpu.VMEM((width, mats * extent), jnp.float32),
        ],
        compiler_params=pltpu.CompilerParams(vmem_limit_bytes=52 << 20),
        cost_estimate=estimate(14 * 2 * width * GROUP * count, pulled, mid, top, rotation, out, out),
        name="block_terms",
    )(moves, side, pulled, mid, top, rotation, heads, tails)


def pull(gate_cols, up_cols, gate_grad, up_grad):
    rows, width = gate_cols.shape
    count = gate_grad.shape[0]
    step = min(512, rows)

    def body(gate_ref, up_ref, gate_grad_ref, up_grad_ref, out_ref):
        out_ref[:, :count] = dot(gate_ref[...], gate_grad_ref[...], 1, 1).astype(jnp.bfloat16)
        out_ref[:, count:] = dot(up_ref[...], up_grad_ref[...], 1, 1).astype(jnp.bfloat16)

    out = jax.ShapeDtypeStruct((rows, 2 * count), jnp.bfloat16)
    weights = pl.BlockSpec((step, width), lambda at: (at, 0))
    grads = pl.BlockSpec((count, width), lambda at: (0, 0))
    return pl.pallas_call(
        body,
        out_shape=out,
        grid=(rows // step,),
        in_specs=[weights, weights, grads, grads],
        out_specs=pl.BlockSpec((step, 2 * count), lambda at: (at, 0)),
        cost_estimate=estimate(4 * rows * width * count, gate_cols, up_cols, out),
        name="pull",
    )(gate_cols, up_cols, gate_grad, up_grad)


def places_of(bits, section_row):
    places = jnp.arange(section_row.shape[0], dtype=jnp.int32)
    found = bits[:, None] == section_row[None, :]
    return jnp.sum(jnp.where(found, places[None, :], 0), axis=1)


def shards(tokens, gate_weight, up_weight, skew_params, section_bits, upstream):
    mats, _, own_blocks, extent, _ = skew_params.shape
    own_rows = gate_weight.shape[0]
    own_cols = upstream.shape[1]
    devices = gate_weight.shape[1] // own_cols
    half = devices // 2
    half_rows = half * own_rows
    side = lax.axis_index("rows") // half
    groups = [list(range(half)), list(range(half, devices))]
    swap = [(at, (at + half) % devices) for at in range(devices)]

    def move(parts):
        moved = lax.all_to_all(
            parts, "rows", split_axis=0, concat_axis=0, axis_index_groups=groups, tiled=True
        )
        return moved.reshape(half_rows, 2 * own_cols)

    bits_0, bits_1 = section_bits[0], section_bits[1]
    natural = jnp.arange(bits_0.shape[0], dtype=jnp.int32)
    inverse_0 = places_of(natural, bits_0)
    one_to_zero = places_of(bits_0, bits_1)
    zero_to_one = places_of(bits_1, bits_0)
    heads, tails, moves = routes(jnp.stack([bits_1, one_to_zero, inverse_0, bits_0, zero_to_one]))
    side_at = jnp.reshape(side, (1,)).astype(jnp.int32)

    skew_params, gate_parts = lax.optimization_barrier((skew_params, pack(gate_weight, half, own_cols)))
    gate_cols = move(gate_parts)
    other_upstream = lax.ppermute(upstream, "rows", swap)
    inverse = cayley_inverse(skew_params)
    own_rotation = (2.0 * inverse - jnp.eye(extent, dtype=jnp.float32)).astype(jnp.bfloat16)
    packed = own_rotation.transpose(2, 3, 1, 0, 4).reshape(own_blocks * extent, -1)
    up_weight, packed = lax.optimization_barrier((up_weight, packed))
    packed, up_parts = lax.optimization_barrier((packed, pack(up_weight, half, own_cols)))
    all_tokens, rotation = gather_blocks((tokens, packed), devices)
    all_tokens = all_tokens.reshape(-1, tokens.shape[1])
    rotation = rotation.reshape(devices * own_blocks * extent, -1)
    token_count = all_tokens.shape[0]
    all_tokens, gate_cols, up_parts, other_upstream = lax.optimization_barrier(
        (all_tokens, gate_cols, up_parts, other_upstream)
    )
    up_cols = move(up_parts)
    top_tokens, mid, low = rotate_tokens(
        all_tokens, rotation, heads[:3], tails[:3], moves[:3].reshape(-1), side_at, extent, mats
    )

    def project(at, columns):
        part = dot(low[:, at * token_count : (at + 1) * token_count], columns, 0, 0)
        return part + lax.ppermute(part.astype(jnp.bfloat16), "rows", swap).astype(jnp.float32)

    gate_pre = project(0, gate_cols)
    up_pre = project(1, up_cols)
    sigmoid_val = jax.nn.sigmoid(gate_pre)
    silu_val = gate_pre * sigmoid_val
    activation = (silu_val * up_pre).astype(jnp.bfloat16)
    activation = jnp.where(side == 0, activation[:, :own_cols], activation[:, own_cols:])
    first = jnp.where(side == 0, upstream, other_upstream)
    second = jnp.where(side == 0, other_upstream, upstream)
    cotangent = jnp.concatenate([first, second], axis=1).astype(jnp.float32)
    gate_grad = (cotangent * up_pre * sigmoid_val * (1.0 + gate_pre * (1.0 - sigmoid_val))).astype(
        jnp.bfloat16
    )
    up_grad = (cotangent * silu_val).astype(jnp.bfloat16)

    pulled = pull(gate_cols, up_cols, gate_grad, up_grad)
    terms_0, terms_1 = block_terms(
        pulled, mid, top_tokens, rotation, heads[3:], tails[3:], moves[3:].reshape(-1), side_at, extent, mats
    )

    def ordered(summed):
        return summed.reshape(own_blocks, extent, mats, extent).transpose(2, 0, 1, 3)

    by_owner = (devices, own_blocks * extent, mats * extent)
    summed = reduce_blocks((terms_0.reshape(by_owner), terms_1.reshape(by_owner)), devices)
    factor_grad = jnp.stack([ordered(summed[0]), ordered(summed[1])], axis=1)

    left = jnp.einsum(
        "mskab,mskac->mskbc", inverse, factor_grad, precision=lax.Precision.HIGHEST
    )
    generator_grad = -2.0 * jnp.einsum(
        "mskbc,mskdc->mskbd", left, inverse, precision=lax.Precision.HIGHEST
    )
    skew_grad = generator_grad - jnp.swapaxes(generator_grad, -1, -2)
    return (activation, skew_grad)


def solution(mesh):
    placed = (
        P(("groups", "rows"), None),
        P("rows", None),
        P("rows", None),
        P(None, None, "rows", None, None),
        P(),
        P("groups", "rows"),
    )
    return jax.shard_map(
        shards,
        mesh=mesh,
        in_specs=placed,
        out_specs=(P("groups", "rows"), P("groups", None, "rows", None, None)),
        check_vma=False,
    )
```

```python
import jax
import jax.numpy as jnp
from jax import lax
from jax.experimental import pallas as pl
from jax.experimental.pallas import tpu as pltpu
from jax.sharding import PartitionSpec as P


def inverse_kernel(skew_ref, out_ref):
    extent = skew_ref.shape[-1]
    shape = skew_ref.shape
    row_at = lax.broadcasted_iota(jnp.int32, shape, 1)
    col_at = lax.broadcasted_iota(jnp.int32, shape, 2)
    skew = skew_ref[...]
    generator = skew - jnp.swapaxes(skew, 1, 2)
    out_ref[...] = jnp.where(row_at == col_at, 1.0, 0.0) + generator
    lane = lax.broadcasted_iota(jnp.int32, (shape[0], 1, extent), 2)

    def step(at, carry):
        work = out_ref[...]
        pivot_row = out_ref[:, pl.ds(at, 1), :]
        at_col = col_at == at
        pivot_col = jnp.sum(jnp.where(at_col, work, 0.0), axis=2, keepdims=True)
        pivot = jnp.sum(jnp.where(lane == at, pivot_row, 0.0), axis=2, keepdims=True)
        scale = 1.0 / pivot
        scaled_row = jnp.where(lane == at, 1.0, pivot_row) * scale
        cleared = jnp.where(at_col, 0.0, work)
        out_ref[...] = cleared - pivot_col * scaled_row
        out_ref[:, pl.ds(at, 1), :] = scaled_row
        return carry

    lax.fori_loop(0, extent, step, 0)


def cayley_inverse(skew_blocks):
    extent = skew_blocks.shape[-1]
    flat = skew_blocks.reshape(-1, extent, extent)
    out = pl.pallas_call(
        inverse_kernel,
        out_shape=jax.ShapeDtypeStruct(flat.shape, jnp.float32),
        in_specs=[pl.BlockSpec(memory_space=pltpu.VMEM)],
        out_specs=pl.BlockSpec(memory_space=pltpu.VMEM),
        cost_estimate=pl.CostEstimate(
            flops=50_000_000, bytes_accessed=2 * 4 * flat.size, transcendentals=0
        ),
        name="cayley_inverse",
    )(flat)
    return out.reshape(skew_blocks.shape)


def estimate(flops, *arrays):
    moved = sum(array.size * array.dtype.itemsize for array in arrays)
    return pl.CostEstimate(flops=flops, bytes_accessed=moved, transcendentals=0)


def pack(weight, half, cols):
    rows, width = weight.shape
    step = min(rows, 32)

    def body(in_ref, out_ref):
        for at in range(half):
            left = in_ref[:, at * cols : (at + 1) * cols]
            right = in_ref[:, (half + at) * cols : (half + at + 1) * cols]
            out_ref[at] = jnp.concatenate([left, right], axis=1)

    out = jax.ShapeDtypeStruct((half, rows, 2 * cols), weight.dtype)
    return pl.pallas_call(
        body,
        out_shape=out,
        grid=(rows // step,),
        in_specs=[pl.BlockSpec((step, width), lambda at: (at, 0))],
        out_specs=pl.BlockSpec((half, step, 2 * cols), lambda at: (0, at, 0)),
        cost_estimate=estimate(0, weight, out),
        name="pack",
    )(weight)


def dot(left, right, left_dim, right_dim):
    contract = (((left_dim,), (right_dim,)), ((), ()))
    return lax.dot_general(left, right, contract, preferred_element_type=jnp.float32)


def routes(places):
    count, digits = places.shape
    low = GROUP_BITS
    at = jnp.arange(digits, dtype=jnp.int32)
    hit = places[:, :, None] == at[None, None, :]
    slot_of = jnp.sum(jnp.where(hit, at[None, :, None], 0), axis=1)
    is_low = at[None, :] < low
    crosses = is_low != (slot_of < low)
    before = at[:, None] < at[None, :]
    same = (at[:, None] < low) == (at[None, :] < low)
    rank_cross = jnp.sum((crosses[:, :, None] & (before & same)[None]).astype(jnp.int32), axis=1)
    rank_stay = jnp.sum((~crosses[:, :, None] & (before & same)[None]).astype(jnp.int32), axis=1)
    inside = jnp.where(crosses, low - 1 - rank_cross, rank_stay)
    first = jnp.where(is_low, inside, at[None, :])
    second = jnp.where(is_low & ~crosses, inside, slot_of)
    second = jnp.where(~is_low & crosses, low - 1 - rank_cross, second)
    after = jnp.sum(jnp.where(hit, second[:, None, :], 0), axis=2)

    def spread(index, sources, targets):
        bits = jnp.right_shift(index[None, :, None], sources[:, None, :]) & 1
        return jnp.sum(jnp.left_shift(bits, targets[:, None, :]), axis=2)

    group = jnp.arange(1 << low, dtype=jnp.int32)
    natural = jnp.broadcast_to(at[None, :], (count, digits))
    take_first = spread(group, first[:, :low], natural[:, :low])
    take_last = spread(group, natural[:, :low], after[:, :low])
    tiles = jnp.arange((1 << digits) // TILE, dtype=jnp.int32) * TILE
    moves = spread(tiles, second, first)
    heads = (take_first[:, :, None] == group[None, None, :]).astype(jnp.bfloat16)
    tails = (take_last[:, :, None] == group[None, None, :]).astype(jnp.bfloat16)
    return heads, tails, moves


GROUP_BITS = 8
GROUP = 1 << GROUP_BITS
TILE = 8
STEPS = 8


def collect(moves_ref, base, source_ref, slot_ref):
    for pair in range(GROUP // (2 * TILE)):
        parts = []
        for half in range(2):
            start = pl.multiple_of(moves_ref[base + 2 * pair + half], TILE)
            parts.append(source_ref[pl.ds(start, TILE), :])
        rows = slice(2 * TILE * pair, 2 * TILE * (pair + 1))
        slot_ref[rows, :] = jnp.concatenate(parts, axis=0).astype(jnp.bfloat16)


def flipped(index, bit):
    return index + (1 - 2 * ((index // (1 << bit)) % 2)) * (1 << bit)


def greet(bits):
    me = lax.axis_index("rows")
    barrier = pltpu.get_barrier_semaphore()
    for bit in range(bits):
        pl.semaphore_signal(
            barrier, inc=1, device_id={"rows": flipped(me, bit)}, device_id_type=pl.DeviceIdType.MESH
        )
    pl.semaphore_wait(barrier, bits)
    return me


def bit_orders(devices):
    down = list(reversed(range(devices.bit_length() - 1)))
    return [down, down[:-3] + [down[-2], down[-3], down[-1]]]


def gather_blocks(arrays, devices):
    bits = devices.bit_length() - 1
    down = list(reversed(range(bits)))
    high, (far, near, core) = down[:-3], down[-3:]
    orders = [high + [far, near, core], high + [near, far, core], [near, far] + high + [core], [far, near] + high + [core]]
    count = len(arrays)
    streams = [(at, color) for color in range(4) for at in range(count)]

    def kernel(*refs):
        own_refs, out_refs = refs[:count], refs[count : 2 * count]
        send_sem, recv_sem, local_sem = refs[2 * count :]
        me = greet(bits)
        locals_ = []
        for at in range(count):
            local = pltpu.make_async_copy(own_refs[at], out_refs[at].at[me], local_sem.at[at])
            local.start()
            locals_.append(local)

        def part(at, color):
            rows, lanes = arrays[at].shape
            extent = rows if rows % 64 == 0 else lanes
            eighths = (0, 3, 6, 7, 8) if extent % 128 == 0 else (0, 2, 4, 6, 8)
            begin, end = (extent * eighths[color + at] // 8 for at in range(2))
            if extent == rows:
                return (pl.ds(begin, end - begin), slice(None))
            return (slice(None), pl.ds(begin, end - begin))

        def copy(stream, step, pattern):
            at, color = streams[stream]
            order = orders[color]
            block = me
            for level in range(step):
                if (pattern >> level) & 1:
                    block = flipped(block, order[level])
            piece = part(at, color)
            source = own_refs[at].at[piece] if pattern == 0 else out_refs[at].at[(block,) + piece]
            slot = pattern + (1 << step) - 1
            return pltpu.make_async_remote_copy(
                src_ref=source,
                dst_ref=out_refs[at].at[(block,) + piece],
                send_sem=send_sem.at[stream, slot],
                recv_sem=recv_sem.at[stream, slot],
                device_id={"rows": flipped(me, order[step])},
                device_id_type=pl.DeviceIdType.MESH,
            )

        copies = {}
        arrived = set()

        def arrive(stream, pattern):
            if pattern and (stream, pattern) not in arrived:
                arrived.add((stream, pattern))
                copies[stream, pattern].wait_recv()

        for step in range(bits):
            for pattern in range(1 << step):
                for stream in range(len(streams)):
                    arrive(stream, pattern)
                    made = copy(stream, step, pattern)
                    made.start()
                    copies[stream, pattern + (1 << step)] = made
        for pattern in range(1, devices):
            for stream in range(len(streams)):
                arrive(stream, pattern)
        for made in copies.values():
            made.wait_send()
        for local in locals_:
            local.wait()

    outs = tuple(jax.ShapeDtypeStruct((devices,) + own.shape, own.dtype) for own in arrays)
    anywhere = pl.BlockSpec(memory_space=pl.ANY)
    return pl.pallas_call(
        kernel,
        out_shape=outs,
        in_specs=[anywhere] * count,
        out_specs=(anywhere,) * count,
        scratch_shapes=[
            pltpu.SemaphoreType.DMA((4 * count, devices - 1)),
            pltpu.SemaphoreType.DMA((4 * count, devices - 1)),
            pltpu.SemaphoreType.DMA((count,)),
        ],
        compiler_params=pltpu.CompilerParams(collective_id=0, has_side_effects=True),
        cost_estimate=pl.CostEstimate(
            flops=0, bytes_accessed=32 * sum(2 * out.size for out in outs), transcendentals=0
        ),
        name="gather_blocks",
    )(*arrays)


def with_sibling(name, collective_id, out_shape, plan, array, cuts):
    def kernel(in_ref, out_ref, local_sem, send_sem, recv_sem):
        me = greet(1)
        moving = []
        for cut in range(cuts):
            here, kept, there, sent = plan(in_ref, out_ref, me % 2, cut)
            far = pltpu.make_async_remote_copy(
                src_ref=there,
                dst_ref=sent,
                send_sem=send_sem.at[cut],
                recv_sem=recv_sem.at[cut],
                device_id={"rows": flipped(me, 0)},
                device_id_type=pl.DeviceIdType.MESH,
            )
            far.start()
            near = pltpu.make_async_copy(here, kept, local_sem.at[cut])
            near.start()
            moving += [far, near]
        for made in moving:
            made.wait()

    anywhere = pl.BlockSpec(memory_space=pl.ANY)
    return pl.pallas_call(
        kernel,
        out_shape=jax.ShapeDtypeStruct(out_shape, array.dtype),
        in_specs=[anywhere],
        out_specs=anywhere,
        scratch_shapes=[pltpu.SemaphoreType.DMA((cuts,))] * 3,
        compiler_params=pltpu.CompilerParams(collective_id=collective_id, has_side_effects=True),
        cost_estimate=estimate(0, array, array, array),
        name=name,
    )(array)


def join_low(low):
    mats, share, rows = low.shape
    cuts = 2 if share % 64 == 0 else 1
    step = share // cuts

    def plan(in_ref, out_ref, parity, cut):
        m, at = cut // cuts, cut % cuts
        source = in_ref.at[m, pl.ds(at * step, step)]
        place = out_ref.at[m, pl.ds(parity * share + at * step, step)]
        return source, place, source, place

    return with_sibling("join_low", 2, (mats, 2 * share, rows), plan, low, mats * cuts)


def swap_pulled(pulled):
    _, mats, rows, share = pulled.shape
    cuts = 4
    step = rows // cuts

    def plan(in_ref, out_ref, parity, cut):
        m, lines = cut // cuts, pl.ds(cut % cuts * step, step)
        return (
            in_ref.at[parity, m, lines],
            out_ref.at[0, m, lines],
            in_ref.at[1 - parity, m, lines],
            out_ref.at[1, m, lines],
        )

    return with_sibling("swap_pulled", 3, pulled.shape, plan, pulled, mats * cuts)


def reduce_blocks(arrays, devices):
    _, rows, lanes = arrays[0].shape
    bits = devices.bit_length() - 1
    count = len(arrays)
    orders = [list(reversed(order)) for order in bit_orders(devices)]

    def kernel(*refs):
        in_refs = refs[:count]
        out_ref, acc, landed, send_sem, recv_sem = refs[count:]
        me = greet(bits)
        copies = {}

        def block_of(at, step, pattern, index):
            order = orders[at % 2]
            for level in range(step + 1, bits):
                if (pattern >> (level - step - 1)) & 1:
                    index = flipped(index, order[level])
            return index

        def send(at, step, pattern):
            other = flipped(me, orders[at % 2][step])
            if step == 0:
                source = in_refs[at].at[block_of(at, 0, pattern, other)]
            else:
                source = acc.at[at, (2 * pattern + 1) << (step - 1)]
            slot = (devices >> (step + 1)) + pattern - 1
            made = pltpu.make_async_remote_copy(
                src_ref=source,
                dst_ref=landed.at[at, slot],
                send_sem=send_sem.at[at, slot],
                recv_sem=recv_sem.at[at, slot],
                device_id={"rows": other},
                device_id_type=pl.DeviceIdType.MESH,
            )
            made.start()
            copies[at, step, pattern] = made

        def arrive(at, step, pattern):
            copies[at, step, pattern].wait_recv()
            slot = (devices >> (step + 1)) + pattern - 1
            if step == 0:
                kept = in_refs[at][block_of(at, 0, pattern, me)]
            else:
                kept = acc[at, (2 * pattern) << (step - 1)]
            total = kept.astype(jnp.float32) + landed[at, slot].astype(jnp.float32)
            if step == bits - 1:
                out_ref[at] = total
            else:
                acc[at, pattern << step] = total.astype(jnp.bfloat16)

        for pattern in [p for odd in (1, 0) for p in range(devices // 2) if p % 2 == odd]:
            for at in range(count):
                send(at, 0, pattern)
        for step in range(1, bits + 1):
            patterns = devices >> step
            for pattern in [p for odd in (1, 0) for p in range(patterns) if p % 2 == odd]:
                for at in range(count):
                    arrive(at, step - 1, pattern)
                    if step < bits and pattern % 2:
                        send(at, step, pattern // 2)
        for made in copies.values():
            made.wait_send()

    return pl.pallas_call(
        kernel,
        out_shape=jax.ShapeDtypeStruct((count, rows, lanes), jnp.float32),
        in_specs=[pl.BlockSpec(memory_space=pltpu.VMEM)] * count,
        out_specs=pl.BlockSpec(memory_space=pltpu.VMEM),
        scratch_shapes=[
            pltpu.VMEM((count, devices // 2, rows, lanes), jnp.bfloat16),
            pltpu.VMEM((count, devices - 1, rows, lanes), jnp.bfloat16),
            pltpu.SemaphoreType.DMA((count, devices - 1)),
            pltpu.SemaphoreType.DMA((count, devices - 1)),
        ],
        compiler_params=pltpu.CompilerParams(
            collective_id=1, has_side_effects=True, vmem_limit_bytes=32 << 20
        ),
        cost_estimate=pl.CostEstimate(flops=0, bytes_accessed=64 * arrays[0].size, transcendentals=0),
        name="reduce_blocks",
    )(*arrays)


def clamp(phase, wanted, at, last):
    return jnp.where(phase < wanted, 0, jnp.where(phase > wanted, last, at))


def rotate_tokens(all_tokens, rotation, heads, tails, moves, side, extent, mats):
    count, width = all_tokens.shape
    chunk = width // STEPS
    groups = chunk // GROUP
    tiles = GROUP // TILE
    all_tiles = width // TILE
    half_rows = width // 2
    half_chunk = half_rows // STEPS
    last = STEPS - 1

    def body(moves_ref, side_ref, tok_ref, rot_ref, heads_ref, tails_ref, top_ref, mid_ref, low_ref, za, zb, slot):
        m, phase, at = pl.program_id(0), pl.program_id(1), pl.program_id(2)

        block_row = lax.broadcasted_iota(jnp.int32, (GROUP, GROUP), 0) // extent
        block_col = lax.broadcasted_iota(jnp.int32, (GROUP, GROUP), 1) // extent
        same_block = block_row == block_col

        def turned(values, section):
            blocks = []
            for g in range(groups):
                both = rot_ref[g * GROUP : (g + 1) * GROUP, section * mats * extent : (section + 1) * mats * extent]
                own = jnp.where(m == 0, both[:, :extent], both[:, extent:])
                tiled = jnp.concatenate([own] * (GROUP // extent), axis=1)
                blocks.append(jnp.where(same_block, tiled, jnp.zeros_like(tiled)))
            return [dot(block, value, 0, 0).astype(jnp.bfloat16) for block, value in zip(blocks, values)]

        def stage(base, source, out_ref, perm, section, target):
            for g in range(groups):
                collect(moves_ref, base + (at * groups + g) * tiles, source, slot.at[g])
            values = [dot(tails_ref[perm], slot[g], 1, 0).astype(jnp.bfloat16) for g in range(groups)]
            for g in range(groups):
                out_ref[g * GROUP : (g + 1) * GROUP, :] = values[g]
            mixed = turned(values, section)
            for g in range(groups):
                target[pl.ds(at * chunk + g * GROUP, GROUP), :] = dot(heads_ref[perm + 1], mixed[g], 1, 0)

        @pl.when(phase == 0)
        def _():
            for g in range(groups):
                piece = tok_ref[:, g * GROUP : (g + 1) * GROUP]
                za[pl.ds(at * chunk + g * GROUP, GROUP), :] = dot(heads_ref[0], piece, 1, 1)

        @pl.when(phase == 1)
        def _():
            stage(0, za, top_ref, 0, 1, zb)

        @pl.when(phase == 2)
        def _():
            stage(all_tiles, zb, mid_ref, 1, 0, za)

        @pl.when(phase == 3)
        def _():
            low_groups = half_chunk // GROUP
            for g in range(low_groups):
                at_group = side_ref[0] * (half_rows // GROUP) + at * low_groups + g
                collect(moves_ref, 2 * all_tiles + at_group * tiles, za, slot.at[g])
            for g in range(low_groups):
                value = dot(slot[g], tails_ref[2], 0, 1)
                low_ref[:, g * GROUP : (g + 1) * GROUP] = value.astype(jnp.bfloat16)

    outs = (
        jax.ShapeDtypeStruct((width, count), jnp.bfloat16),
        jax.ShapeDtypeStruct((mats, width, count), jnp.bfloat16),
        jax.ShapeDtypeStruct((mats, count, half_rows), jnp.bfloat16),
    )
    whole = lambda m, phase, at: (0, 0, 0)
    return pl.pallas_call(
        body,
        out_shape=outs,
        grid=(mats, 4, STEPS),
        in_specs=[
            pl.BlockSpec(memory_space=pltpu.SMEM),
            pl.BlockSpec(memory_space=pltpu.SMEM),
            pl.BlockSpec((count, chunk), lambda m, phase, at: (0, jnp.where(phase == 0, at, last))),
            pl.BlockSpec(
                (chunk, rotation.shape[1]),
                lambda m, phase, at: (jnp.where(phase == 0, 0, jnp.where(phase == 3, last, at)), 0),
            ),
            pl.BlockSpec((3, GROUP, GROUP), whole),
            pl.BlockSpec((3, GROUP, GROUP), whole),
        ],
        out_specs=(
            pl.BlockSpec((chunk, count), lambda m, phase, at: (clamp(phase, 1, at, last), 0)),
            pl.BlockSpec((None, chunk, count), lambda m, phase, at: (m, clamp(phase, 2, at, last), 0)),
            pl.BlockSpec((None, count, half_chunk), lambda m, phase, at: (m, 0, clamp(phase, 3, at, last))),
        ),
        scratch_shapes=[
            pltpu.VMEM((width, count), jnp.float32),
            pltpu.VMEM((width, count), jnp.float32),
            pltpu.VMEM((groups, GROUP, count), jnp.bfloat16),
        ],
        compiler_params=pltpu.CompilerParams(vmem_limit_bytes=48 << 20),
        cost_estimate=estimate(14 * 2 * width * GROUP * count, all_tokens, rotation, *outs),
        name="rotate_tokens",
    )(moves, side, all_tokens, rotation, heads, tails)


def block_terms(pulled, mid, top, rotation, heads, tails, moves, side, extent, mats):
    half_rows = pulled.shape[2]
    width, count = top.shape
    chunk = width // STEPS
    groups = chunk // GROUP
    tiles = GROUP // TILE
    all_tiles = width // TILE
    half_chunk = half_rows // STEPS
    last = STEPS - 1

    def body(moves_ref, side_ref, pulled_ref, mid_ref, top_ref, rot_ref, heads_ref, tails_ref, terms_0_ref, terms_1_ref, za, zb, slot, kept_0, kept_1):
        m, phase, at = pl.program_id(0), pl.program_id(1), pl.program_id(2)
        lane_mat = lax.broadcasted_iota(jnp.int32, (chunk, mats * extent), 1) // extent
        chunk_rows = pl.ds(pl.multiple_of(at * chunk, chunk), chunk)
        block_row = lax.broadcasted_iota(jnp.int32, (GROUP, GROUP), 0) // extent
        block_col = lax.broadcasted_iota(jnp.int32, (GROUP, GROUP), 1) // extent
        same_block = block_row == block_col

        def emit(out_ref, kept, left_ref, tail):
            grams = [
                dot(left_ref[g * GROUP : (g + 1) * GROUP, :], slot[g], 1, 1).astype(jnp.bfloat16)
                for g in range(groups)
            ]
            terms = [dot(gram, tail, 1, 1) for gram in grams]
            parts = []
            for g in range(groups):
                for b in range(GROUP // extent):
                    pair = b // mats * mats * extent
                    piece = terms[g][b * extent : (b + 1) * extent, pair : pair + mats * extent]
                    parts.append(jnp.where(m == b % mats, piece, pltpu.roll(piece, extent, 1)))
            placed = jnp.concatenate(parts, axis=0)
            both = jnp.where(lane_mat == m, placed, kept[chunk_rows, :])
            kept[chunk_rows, :] = both
            out_ref[...] = both.astype(jnp.bfloat16)

        @pl.when(phase == 0)
        def _():
            own = side_ref[0] * half_rows + at * half_chunk
            other = (1 - side_ref[0]) * half_rows + at * half_chunk
            za[pl.ds(pl.multiple_of(other, half_chunk), half_chunk), :] = jnp.zeros((half_chunk, count), jnp.float32)
            for g in range(half_chunk // GROUP):
                lines = slice(g * GROUP, (g + 1) * GROUP)
                piece = pulled_ref[0, lines].astype(jnp.float32) + pulled_ref[1, lines].astype(jnp.float32)
                piece = piece.astype(jnp.bfloat16)
                za[pl.ds(pl.multiple_of(own + g * GROUP, GROUP), GROUP), :] = dot(heads_ref[0], piece, 1, 0)

        @pl.when(phase == 1)
        def _():
            for g in range(groups):
                collect(moves_ref, (at * groups + g) * tiles, za, slot.at[g])
            merged = []
            for g in range(groups):
                both = rot_ref[g * GROUP : (g + 1) * GROUP, : mats * extent]
                own = jnp.where(m == 0, both[:, :extent], both[:, extent:])
                tiled = jnp.concatenate([own] * (GROUP // extent), axis=1)
                block = jnp.where(same_block, tiled, jnp.zeros_like(tiled))
                merged.append(dot(block, tails_ref[0], 1, 0).astype(jnp.bfloat16))
            merged = [dot(heads_ref[1], value, 1, 0).astype(jnp.bfloat16) for value in merged]
            emit(terms_0_ref, kept_0, mid_ref, tails_ref[0])
            for g in range(groups):
                zb[pl.ds(at * chunk + g * GROUP, GROUP), :] = dot(merged[g], slot[g], 1, 0)

        @pl.when(phase == 2)
        def _():
            for g in range(groups):
                collect(moves_ref, all_tiles + (at * groups + g) * tiles, zb, slot.at[g])
            emit(terms_1_ref, kept_1, top_ref, tails_ref[1])

    out = jax.ShapeDtypeStruct((width, mats * extent), jnp.bfloat16)
    whole = lambda m, phase, at: (0, 0, 0)
    return pl.pallas_call(
        body,
        out_shape=(out, out),
        grid=(mats, 3, STEPS),
        in_specs=[
            pl.BlockSpec(memory_space=pltpu.SMEM),
            pl.BlockSpec(memory_space=pltpu.SMEM),
            pl.BlockSpec((2, None, half_chunk, count), lambda m, phase, at: (0, m, clamp(phase, 0, at, last), 0)),
            pl.BlockSpec((None, chunk, count), lambda m, phase, at: (m, clamp(phase, 1, at, last), 0)),
            pl.BlockSpec((chunk, count), lambda m, phase, at: (clamp(phase, 2, at, last), 0)),
            pl.BlockSpec((chunk, rotation.shape[1]), lambda m, phase, at: (clamp(phase, 1, at, last), 0)),
            pl.BlockSpec((2, GROUP, GROUP), whole),
            pl.BlockSpec((2, GROUP, GROUP), whole),
        ],
        out_specs=(
            pl.BlockSpec((chunk, mats * extent), lambda m, phase, at: (jnp.where(m == mats - 1, clamp(phase, 1, at, last), 0), 0)),
            pl.BlockSpec((chunk, mats * extent), lambda m, phase, at: (jnp.where(m == mats - 1, clamp(phase, 2, at, last), 0), 0)),
        ),
        scratch_shapes=[
            pltpu.VMEM((width, count), jnp.float32),
            pltpu.VMEM((width, count), jnp.float32),
            pltpu.VMEM((groups, GROUP, count), jnp.bfloat16),
            pltpu.VMEM((width, mats * extent), jnp.float32),
            pltpu.VMEM((width, mats * extent), jnp.float32),
        ],
        compiler_params=pltpu.CompilerParams(vmem_limit_bytes=52 << 20),
        cost_estimate=estimate(14 * 2 * width * GROUP * count, pulled, mid, top, rotation, out, out),
        name="block_terms",
    )(moves, side, pulled, mid, top, rotation, heads, tails)


def pull(gate_cols, up_cols, gate_grad, up_grad):
    rows, width = gate_cols.shape
    count = gate_grad.shape[0]
    step = min(512, rows)

    def body(gate_ref, up_ref, gate_grad_ref, up_grad_ref, out_ref):
        for parity in range(2):
            own = slice(parity * share, (parity + 1) * share)
            out_ref[parity, 0] = dot(gate_ref[...], gate_grad_ref[own, :], 1, 1).astype(jnp.bfloat16)
            out_ref[parity, 1] = dot(up_ref[...], up_grad_ref[own, :], 1, 1).astype(jnp.bfloat16)

    share = count // 2
    out = jax.ShapeDtypeStruct((2, 2, rows, share), jnp.bfloat16)
    weights = pl.BlockSpec((step, width), lambda at: (at, 0))
    grads = pl.BlockSpec((count, width), lambda at: (0, 0))
    return pl.pallas_call(
        body,
        out_shape=out,
        grid=(rows // step,),
        in_specs=[weights, weights, grads, grads],
        out_specs=pl.BlockSpec((2, 2, step, share), lambda at: (0, 0, at, 0)),
        cost_estimate=estimate(4 * rows * width * count, gate_cols, up_cols, out),
        name="pull",
    )(gate_cols, up_cols, gate_grad, up_grad)


def places_of(bits, section_row):
    places = jnp.arange(section_row.shape[0], dtype=jnp.int32)
    found = bits[:, None] == section_row[None, :]
    return jnp.sum(jnp.where(found, places[None, :], 0), axis=1)


def shards(tokens, gate_weight, up_weight, skew_params, section_bits, upstream):
    mats, _, own_blocks, extent, _ = skew_params.shape
    own_rows = gate_weight.shape[0]
    own_cols = upstream.shape[1]
    devices = gate_weight.shape[1] // own_cols
    half = devices // 2
    half_rows = half * own_rows
    side = lax.axis_index("rows") // half
    groups = [list(range(half)), list(range(half, devices))]
    swap = [(at, (at + half) % devices) for at in range(devices)]

    def move(parts):
        moved = lax.all_to_all(
            parts, "rows", split_axis=0, concat_axis=0, axis_index_groups=groups, tiled=True
        )
        return moved.reshape(half_rows, 2 * own_cols)

    bits_0, bits_1 = section_bits[0], section_bits[1]
    natural = jnp.arange(bits_0.shape[0], dtype=jnp.int32)
    inverse_0 = places_of(natural, bits_0)
    one_to_zero = places_of(bits_0, bits_1)
    zero_to_one = places_of(bits_1, bits_0)
    heads, tails, moves = routes(jnp.stack([bits_1, one_to_zero, inverse_0, bits_0, zero_to_one]))
    side_at = jnp.reshape(side, (1,)).astype(jnp.int32)

    pairs = [list(range(parity, devices, 2)) for parity in range(2)]
    all_tokens = lax.all_gather(tokens, "rows", axis=0, axis_index_groups=pairs, tiled=True)
    own_count = tokens.shape[0]
    token_count = 2 * all_tokens.shape[0]

    skew_params, gate_parts = lax.optimization_barrier((skew_params, pack(gate_weight, half, own_cols)))
    gate_cols = move(gate_parts)
    upstream = upstream.reshape(half, 2, own_count, own_cols).transpose(1, 0, 2, 3).reshape(token_count, own_cols)
    other_upstream = lax.ppermute(upstream, "rows", swap)
    inverse = cayley_inverse(skew_params)
    own_rotation = (2.0 * inverse - jnp.eye(extent, dtype=jnp.float32)).astype(jnp.bfloat16)
    packed = own_rotation.transpose(2, 3, 1, 0, 4).reshape(own_blocks * extent, -1)
    up_weight, packed = lax.optimization_barrier((up_weight, packed))
    packed, up_parts = lax.optimization_barrier((packed, pack(up_weight, half, own_cols)))
    (rotation,) = gather_blocks((packed,), devices)
    rotation = rotation.reshape(devices * own_blocks * extent, -1)
    rotation, gate_cols, up_parts, other_upstream, all_tokens = lax.optimization_barrier(
        (rotation, gate_cols, up_parts, other_upstream, all_tokens)
    )
    up_cols = move(up_parts)
    top_tokens, mid, low = rotate_tokens(
        all_tokens, rotation, heads[:3], tails[:3], moves[:3].reshape(-1), side_at, extent, mats
    )
    low = join_low(low)

    def project(at, columns):
        part = dot(low[at], columns, 1, 0)
        return part + lax.ppermute(part.astype(jnp.bfloat16), "rows", swap).astype(jnp.float32)

    gate_pre = project(0, gate_cols)
    up_pre = project(1, up_cols)
    sigmoid_val = jax.nn.sigmoid(gate_pre)
    silu_val = gate_pre * sigmoid_val
    activation = (silu_val * up_pre).astype(jnp.bfloat16)
    activation = jnp.where(side == 0, activation[:, :own_cols], activation[:, own_cols:])
    activation = activation.reshape(2, half, own_count, own_cols).transpose(1, 0, 2, 3).reshape(token_count, own_cols)
    first = jnp.where(side == 0, upstream, other_upstream)
    second = jnp.where(side == 0, other_upstream, upstream)
    cotangent = jnp.concatenate([first, second], axis=1).astype(jnp.float32)
    gate_grad = (cotangent * up_pre * sigmoid_val * (1.0 + gate_pre * (1.0 - sigmoid_val))).astype(
        jnp.bfloat16
    )
    up_grad = (cotangent * silu_val).astype(jnp.bfloat16)

    pulled = swap_pulled(pull(gate_cols, up_cols, gate_grad, up_grad))
    terms_0, terms_1 = block_terms(
        pulled, mid, top_tokens, rotation, heads[3:], tails[3:], moves[3:].reshape(-1), side_at, extent, mats
    )

    def ordered(summed):
        return summed.reshape(own_blocks, extent, mats, extent).transpose(2, 0, 1, 3)

    by_owner = (devices, own_blocks * extent, mats * extent)
    summed = reduce_blocks((terms_0.reshape(by_owner), terms_1.reshape(by_owner)), devices)
    factor_grad = jnp.stack([ordered(summed[0]), ordered(summed[1])], axis=1)

    left = jnp.einsum(
        "mskab,mskac->mskbc", inverse, factor_grad, precision=lax.Precision.HIGHEST
    )
    generator_grad = -2.0 * jnp.einsum(
        "mskbc,mskdc->mskbd", left, inverse, precision=lax.Precision.HIGHEST
    )
    skew_grad = generator_grad - jnp.swapaxes(generator_grad, -1, -2)
    return (activation, skew_grad)


def solution(mesh):
    placed = (
        P(("groups", "rows"), None),
        P("rows", None),
        P("rows", None),
        P(None, None, "rows", None, None),
        P(),
        P("groups", "rows"),
    )
    return jax.shard_map(
        shards,
        mesh=mesh,
        in_specs=placed,
        out_specs=(P("groups", "rows"), P("groups", None, "rows", None, None)),
        check_vma=False,
    )
```

```python
import jax
import jax.numpy as jnp
from jax import lax
from jax.experimental import pallas as pl
from jax.experimental.pallas import tpu as pltpu
from jax.sharding import PartitionSpec as P


def inverse_kernel(skew_ref, out_ref):
    extent = skew_ref.shape[-1]
    shape = skew_ref.shape
    row_at = lax.broadcasted_iota(jnp.int32, shape, 1)
    col_at = lax.broadcasted_iota(jnp.int32, shape, 2)
    skew = skew_ref[...]
    generator = skew - jnp.swapaxes(skew, 1, 2)
    out_ref[...] = jnp.where(row_at == col_at, 1.0, 0.0) + generator
    lane = lax.broadcasted_iota(jnp.int32, (shape[0], 1, extent), 2)

    def step(at, carry):
        work = out_ref[...]
        pivot_row = out_ref[:, pl.ds(at, 1), :]
        at_col = col_at == at
        pivot_col = jnp.sum(jnp.where(at_col, work, 0.0), axis=2, keepdims=True)
        pivot = jnp.sum(jnp.where(lane == at, pivot_row, 0.0), axis=2, keepdims=True)
        scale = 1.0 / pivot
        scaled_row = jnp.where(lane == at, 1.0, pivot_row) * scale
        cleared = jnp.where(at_col, 0.0, work)
        out_ref[...] = cleared - pivot_col * scaled_row
        out_ref[:, pl.ds(at, 1), :] = scaled_row
        return carry

    lax.fori_loop(0, extent, step, 0)


def cayley_inverse(skew_blocks):
    extent = skew_blocks.shape[-1]
    flat = skew_blocks.reshape(-1, extent, extent)
    out = pl.pallas_call(
        inverse_kernel,
        out_shape=jax.ShapeDtypeStruct(flat.shape, jnp.float32),
        in_specs=[pl.BlockSpec(memory_space=pltpu.VMEM)],
        out_specs=pl.BlockSpec(memory_space=pltpu.VMEM),
        cost_estimate=pl.CostEstimate(
            flops=50_000_000, bytes_accessed=2 * 4 * flat.size, transcendentals=0
        ),
        name="cayley_inverse",
    )(flat)
    return out.reshape(skew_blocks.shape)


def estimate(flops, *arrays):
    moved = sum(array.size * array.dtype.itemsize for array in arrays)
    return pl.CostEstimate(flops=flops, bytes_accessed=moved, transcendentals=0)


def pack(weight, half, cols):
    rows, width = weight.shape
    step = min(rows, 32)

    def body(in_ref, out_ref):
        for at in range(half):
            left = in_ref[:, at * cols : (at + 1) * cols]
            right = in_ref[:, (half + at) * cols : (half + at + 1) * cols]
            out_ref[at] = jnp.concatenate([left, right], axis=1)

    out = jax.ShapeDtypeStruct((half, rows, 2 * cols), weight.dtype)
    return pl.pallas_call(
        body,
        out_shape=out,
        grid=(rows // step,),
        in_specs=[pl.BlockSpec((step, width), lambda at: (at, 0))],
        out_specs=pl.BlockSpec((half, step, 2 * cols), lambda at: (0, at, 0)),
        cost_estimate=estimate(0, weight, out),
        name="pack",
    )(weight)


def dot(left, right, left_dim, right_dim):
    contract = (((left_dim,), (right_dim,)), ((), ()))
    return lax.dot_general(left, right, contract, preferred_element_type=jnp.float32)


def routes(places):
    count, digits = places.shape
    low = GROUP_BITS
    at = jnp.arange(digits, dtype=jnp.int32)
    hit = places[:, :, None] == at[None, None, :]
    slot_of = jnp.sum(jnp.where(hit, at[None, :, None], 0), axis=1)
    is_low = at[None, :] < low
    crosses = is_low != (slot_of < low)
    before = at[:, None] < at[None, :]
    same = (at[:, None] < low) == (at[None, :] < low)
    rank_cross = jnp.sum((crosses[:, :, None] & (before & same)[None]).astype(jnp.int32), axis=1)
    rank_stay = jnp.sum((~crosses[:, :, None] & (before & same)[None]).astype(jnp.int32), axis=1)
    inside = jnp.where(crosses, low - 1 - rank_cross, rank_stay)
    first = jnp.where(is_low, inside, at[None, :])
    second = jnp.where(is_low & ~crosses, inside, slot_of)
    second = jnp.where(~is_low & crosses, low - 1 - rank_cross, second)
    after = jnp.sum(jnp.where(hit, second[:, None, :], 0), axis=2)

    def spread(index, sources, targets):
        bits = jnp.right_shift(index[None, :, None], sources[:, None, :]) & 1
        return jnp.sum(jnp.left_shift(bits, targets[:, None, :]), axis=2)

    group = jnp.arange(1 << low, dtype=jnp.int32)
    natural = jnp.broadcast_to(at[None, :], (count, digits))
    take_first = spread(group, first[:, :low], natural[:, :low])
    take_last = spread(group, natural[:, :low], after[:, :low])
    tiles = jnp.arange((1 << digits) // TILE, dtype=jnp.int32) * TILE
    moves = spread(tiles, second, first)
    heads = (take_first[:, :, None] == group[None, None, :]).astype(jnp.bfloat16)
    tails = (take_last[:, :, None] == group[None, None, :]).astype(jnp.bfloat16)
    return heads, tails, moves


GROUP_BITS = 8
GROUP = 1 << GROUP_BITS
TILE = 8
STEPS = 8


def collect(moves_ref, base, source_ref, slot_ref):
    for pair in range(GROUP // (2 * TILE)):
        parts = []
        for half in range(2):
            start = pl.multiple_of(moves_ref[base + 2 * pair + half], TILE)
            parts.append(source_ref[pl.ds(start, TILE), :])
        rows = slice(2 * TILE * pair, 2 * TILE * (pair + 1))
        slot_ref[rows, :] = jnp.concatenate(parts, axis=0).astype(jnp.bfloat16)


def flipped(index, bit):
    return index + (1 - 2 * ((index // (1 << bit)) % 2)) * (1 << bit)


def greet(bits):
    me = lax.axis_index("rows")
    barrier = pltpu.get_barrier_semaphore()
    for bit in range(bits):
        pl.semaphore_signal(
            barrier, inc=1, device_id={"rows": flipped(me, bit)}, device_id_type=pl.DeviceIdType.MESH
        )
    pl.semaphore_wait(barrier, bits)
    return me


def bit_orders(devices):
    down = list(reversed(range(devices.bit_length() - 1)))
    return [down, down[:-3] + [down[-2], down[-3], down[-1]]]


def gather_blocks(arrays, devices):
    bits = devices.bit_length() - 1
    down = list(reversed(range(bits)))
    high, (far, near, core) = down[:-3], down[-3:]
    orders = [high + [far, near, core], high + [near, far, core], [near, far] + high + [core], [far, near] + high + [core]]
    count = len(arrays)
    streams = [(at, color) for color in range(4) for at in range(count)]

    def kernel(*refs):
        own_refs, out_refs = refs[:count], refs[count : 2 * count]
        send_sem, recv_sem, local_sem = refs[2 * count :]
        me = greet(bits)
        locals_ = []
        for at in range(count):
            local = pltpu.make_async_copy(own_refs[at], out_refs[at].at[me], local_sem.at[at])
            local.start()
            locals_.append(local)

        def part(at, color):
            rows, lanes = arrays[at].shape
            extent = rows if rows % 64 == 0 else lanes
            eighths = (0, 3, 6, 7, 8) if extent % 128 == 0 else (0, 2, 4, 6, 8)
            begin, end = (extent * eighths[color + at] // 8 for at in range(2))
            if extent == rows:
                return (pl.ds(begin, end - begin), slice(None))
            return (slice(None), pl.ds(begin, end - begin))

        def copy(stream, step, pattern):
            at, color = streams[stream]
            order = orders[color]
            block = me
            for level in range(step):
                if (pattern >> level) & 1:
                    block = flipped(block, order[level])
            piece = part(at, color)
            source = own_refs[at].at[piece] if pattern == 0 else out_refs[at].at[(block,) + piece]
            slot = pattern + (1 << step) - 1
            return pltpu.make_async_remote_copy(
                src_ref=source,
                dst_ref=out_refs[at].at[(block,) + piece],
                send_sem=send_sem.at[stream, slot],
                recv_sem=recv_sem.at[stream, slot],
                device_id={"rows": flipped(me, order[step])},
                device_id_type=pl.DeviceIdType.MESH,
            )

        copies = {}
        arrived = set()

        def arrive(stream, pattern):
            if pattern and (stream, pattern) not in arrived:
                arrived.add((stream, pattern))
                copies[stream, pattern].wait_recv()

        for step in range(bits):
            for pattern in range(1 << step):
                for stream in range(len(streams)):
                    arrive(stream, pattern)
                    made = copy(stream, step, pattern)
                    made.start()
                    copies[stream, pattern + (1 << step)] = made
        for pattern in range(1, devices):
            for stream in range(len(streams)):
                arrive(stream, pattern)
        for made in copies.values():
            made.wait_send()
        for local in locals_:
            local.wait()

    outs = tuple(jax.ShapeDtypeStruct((devices,) + own.shape, own.dtype) for own in arrays)
    anywhere = pl.BlockSpec(memory_space=pl.ANY)
    return pl.pallas_call(
        kernel,
        out_shape=outs,
        in_specs=[anywhere] * count,
        out_specs=(anywhere,) * count,
        scratch_shapes=[
            pltpu.SemaphoreType.DMA((4 * count, devices - 1)),
            pltpu.SemaphoreType.DMA((4 * count, devices - 1)),
            pltpu.SemaphoreType.DMA((count,)),
        ],
        compiler_params=pltpu.CompilerParams(collective_id=0, has_side_effects=True),
        cost_estimate=pl.CostEstimate(
            flops=0, bytes_accessed=32 * sum(2 * out.size for out in outs), transcendentals=0
        ),
        name="gather_blocks",
    )(*arrays)


def reduce_blocks(arrays, devices):
    _, rows, lanes = arrays[0].shape
    bits = devices.bit_length() - 1
    count = len(arrays)
    orders = [list(reversed(order)) for order in bit_orders(devices)]

    def kernel(*refs):
        in_refs = refs[:count]
        out_ref, acc, landed, send_sem, recv_sem = refs[count:]
        me = greet(bits)
        copies = {}

        def block_of(at, step, pattern, index):
            order = orders[at % 2]
            for level in range(step + 1, bits):
                if (pattern >> (level - step - 1)) & 1:
                    index = flipped(index, order[level])
            return index

        def send(at, step, pattern):
            other = flipped(me, orders[at % 2][step])
            if step == 0:
                source = in_refs[at].at[block_of(at, 0, pattern, other)]
            else:
                source = acc.at[at, (2 * pattern + 1) << (step - 1)]
            slot = (devices >> (step + 1)) + pattern - 1
            made = pltpu.make_async_remote_copy(
                src_ref=source,
                dst_ref=landed.at[at, slot],
                send_sem=send_sem.at[at, slot],
                recv_sem=recv_sem.at[at, slot],
                device_id={"rows": other},
                device_id_type=pl.DeviceIdType.MESH,
            )
            made.start()
            copies[at, step, pattern] = made

        def arrive(at, step, pattern):
            copies[at, step, pattern].wait_recv()
            slot = (devices >> (step + 1)) + pattern - 1
            if step == 0:
                kept = in_refs[at][block_of(at, 0, pattern, me)]
            else:
                kept = acc[at, (2 * pattern) << (step - 1)]
            total = kept.astype(jnp.float32) + landed[at, slot].astype(jnp.float32)
            if step == bits - 1:
                out_ref[at] = total
            else:
                acc[at, pattern << step] = total.astype(jnp.bfloat16)

        for pattern in [p for odd in (1, 0) for p in range(devices // 2) if p % 2 == odd]:
            for at in range(count):
                send(at, 0, pattern)
        for step in range(1, bits + 1):
            patterns = devices >> step
            for pattern in [p for odd in (1, 0) for p in range(patterns) if p % 2 == odd]:
                for at in range(count):
                    arrive(at, step - 1, pattern)
                    if step < bits and pattern % 2:
                        send(at, step, pattern // 2)
        for made in copies.values():
            made.wait_send()

    return pl.pallas_call(
        kernel,
        out_shape=jax.ShapeDtypeStruct((count, rows, lanes), jnp.float32),
        in_specs=[pl.BlockSpec(memory_space=pltpu.VMEM)] * count,
        out_specs=pl.BlockSpec(memory_space=pltpu.VMEM),
        scratch_shapes=[
            pltpu.VMEM((count, devices // 2, rows, lanes), jnp.bfloat16),
            pltpu.VMEM((count, devices - 1, rows, lanes), jnp.bfloat16),
            pltpu.SemaphoreType.DMA((count, devices - 1)),
            pltpu.SemaphoreType.DMA((count, devices - 1)),
        ],
        compiler_params=pltpu.CompilerParams(
            collective_id=1, has_side_effects=True, vmem_limit_bytes=32 << 20
        ),
        cost_estimate=pl.CostEstimate(flops=0, bytes_accessed=64 * arrays[0].size, transcendentals=0),
        name="reduce_blocks",
    )(*arrays)


def clamp(phase, wanted, at, last):
    return jnp.where(phase < wanted, 0, jnp.where(phase > wanted, last, at))


def rotate_tokens(all_tokens, rotation, heads, tails, moves, side, extent, mats):
    count, width = all_tokens.shape
    chunk = width // STEPS
    groups = chunk // GROUP
    tiles = GROUP // TILE
    all_tiles = width // TILE
    half_rows = width // 2
    half_chunk = half_rows // STEPS
    last = STEPS - 1

    def body(moves_ref, side_ref, tok_ref, rot_ref, heads_ref, tails_ref, top_ref, mid_ref, low_ref, za, zb, slot):
        m, phase, at = pl.program_id(0), pl.program_id(1), pl.program_id(2)

        block_row = lax.broadcasted_iota(jnp.int32, (GROUP, GROUP), 0) // extent
        block_col = lax.broadcasted_iota(jnp.int32, (GROUP, GROUP), 1) // extent
        same_block = block_row == block_col

        def turned(values, section):
            blocks = []
            for g in range(groups):
                both = rot_ref[g * GROUP : (g + 1) * GROUP, section * mats * extent : (section + 1) * mats * extent]
                own = jnp.where(m == 0, both[:, :extent], both[:, extent:])
                tiled = jnp.concatenate([own] * (GROUP // extent), axis=1)
                blocks.append(jnp.where(same_block, tiled, jnp.zeros_like(tiled)))
            return [dot(block, value, 0, 0).astype(jnp.bfloat16) for block, value in zip(blocks, values)]

        def stage(base, source, out_ref, perm, section, target):
            for g in range(groups):
                collect(moves_ref, base + (at * groups + g) * tiles, source, slot.at[g])
            values = [dot(tails_ref[perm], slot[g], 1, 0).astype(jnp.bfloat16) for g in range(groups)]
            for g in range(groups):
                out_ref[g * GROUP : (g + 1) * GROUP, :] = values[g]
            mixed = turned(values, section)
            for g in range(groups):
                target[pl.ds(at * chunk + g * GROUP, GROUP), :] = dot(heads_ref[perm + 1], mixed[g], 1, 0)

        @pl.when(phase == 0)
        def _():
            for g in range(groups):
                piece = tok_ref[:, g * GROUP : (g + 1) * GROUP]
                za[pl.ds(at * chunk + g * GROUP, GROUP), :] = dot(heads_ref[0], piece, 1, 1)

        @pl.when(phase == 1)
        def _():
            stage(0, za, top_ref, 0, 1, zb)

        @pl.when(phase == 2)
        def _():
            stage(all_tiles, zb, mid_ref, 1, 0, za)

        @pl.when(phase == 3)
        def _():
            low_groups = half_chunk // GROUP
            for g in range(low_groups):
                at_group = side_ref[0] * (half_rows // GROUP) + at * low_groups + g
                collect(moves_ref, 2 * all_tiles + at_group * tiles, za, slot.at[g])
            for g in range(low_groups):
                value = dot(tails_ref[2], slot[g], 1, 0)
                low_ref[g * GROUP : (g + 1) * GROUP, :] = value.astype(jnp.bfloat16)

    outs = (
        jax.ShapeDtypeStruct((width, count), jnp.bfloat16),
        jax.ShapeDtypeStruct((width, mats * count), jnp.bfloat16),
        jax.ShapeDtypeStruct((half_rows, mats * count), jnp.bfloat16),
    )
    whole = lambda m, phase, at: (0, 0, 0)
    return pl.pallas_call(
        body,
        out_shape=outs,
        grid=(mats, 4, STEPS),
        in_specs=[
            pl.BlockSpec(memory_space=pltpu.SMEM),
            pl.BlockSpec(memory_space=pltpu.SMEM),
            pl.BlockSpec((count, chunk), lambda m, phase, at: (0, jnp.where(phase == 0, at, last))),
            pl.BlockSpec(
                (chunk, rotation.shape[1]),
                lambda m, phase, at: (jnp.where(phase == 0, 0, jnp.where(phase == 3, last, at)), 0),
            ),
            pl.BlockSpec((3, GROUP, GROUP), whole),
            pl.BlockSpec((3, GROUP, GROUP), whole),
        ],
        out_specs=(
            pl.BlockSpec((chunk, count), lambda m, phase, at: (jnp.where(m == 0, clamp(phase, 1, at, last), clamp(phase, 1, at, last)), 0)),
            pl.BlockSpec((chunk, count), lambda m, phase, at: (clamp(phase, 2, at, last), m)),
            pl.BlockSpec((half_chunk, count), lambda m, phase, at: (clamp(phase, 3, at, last), m)),
        ),
        scratch_shapes=[
            pltpu.VMEM((width, count), jnp.float32),
            pltpu.VMEM((width, count), jnp.float32),
            pltpu.VMEM((groups, GROUP, count), jnp.bfloat16),
        ],
        compiler_params=pltpu.CompilerParams(vmem_limit_bytes=48 << 20),
        cost_estimate=estimate(14 * 2 * width * GROUP * count, all_tokens, rotation, *outs),
        name="rotate_tokens",
    )(moves, side, all_tokens, rotation, heads, tails)


def merge_blocks(rotation, head, tail, extent, mats):
    width = rotation.shape[0]
    chunk = width // STEPS

    def body(rot_ref, head_ref, tail_ref, out_ref):
        m = pl.program_id(1)
        block_row = lax.broadcasted_iota(jnp.int32, (GROUP, GROUP), 0) // extent
        block_col = lax.broadcasted_iota(jnp.int32, (GROUP, GROUP), 1) // extent
        same_block = block_row == block_col
        merged = []
        for g in range(chunk // GROUP):
            both = rot_ref[g * GROUP : (g + 1) * GROUP, : mats * extent]
            own = jnp.where(m == 0, both[:, :extent], both[:, extent:])
            tiled = jnp.concatenate([own] * (GROUP // extent), axis=1)
            block = jnp.where(same_block, tiled, jnp.zeros_like(tiled))
            merged.append(dot(block, tail_ref[...], 1, 0).astype(jnp.bfloat16))
        for g, value in enumerate(merged):
            out_ref[g * GROUP : (g + 1) * GROUP, :] = dot(head_ref[...], value, 1, 0).astype(jnp.bfloat16)

    out = jax.ShapeDtypeStruct((mats, width, GROUP), jnp.bfloat16)
    whole = pl.BlockSpec((GROUP, GROUP), lambda at, m: (0, 0))
    return pl.pallas_call(
        body,
        out_shape=out,
        grid=(STEPS, mats),
        in_specs=[pl.BlockSpec((chunk, rotation.shape[1]), lambda at, m: (at, 0)), whole, whole],
        out_specs=pl.BlockSpec((None, chunk, GROUP), lambda at, m: (m, at, 0)),
        compiler_params=pltpu.CompilerParams(vmem_limit_bytes=16 << 20),
        cost_estimate=estimate(8 * width * GROUP * GROUP, rotation, out),
        name="merge_blocks",
    )(rotation, head, tail)


def block_terms(pulled, mid, top, merged, heads, tails, moves, side, extent, mats):
    half_rows = pulled.shape[0]
    width, count = top.shape
    chunk = width // STEPS
    groups = chunk // GROUP
    tiles = GROUP // TILE
    all_tiles = width // TILE
    half_chunk = half_rows // STEPS
    last = STEPS - 1

    def body(moves_ref, side_ref, pulled_ref, mid_ref, top_ref, merged_ref, heads_ref, tails_ref, terms_0_ref, terms_1_ref, za, zb, slot, kept_0, kept_1):
        m, phase, at = pl.program_id(0), pl.program_id(1), pl.program_id(2)
        lane_mat = lax.broadcasted_iota(jnp.int32, (chunk, mats * extent), 1) // extent
        chunk_rows = pl.ds(pl.multiple_of(at * chunk, chunk), chunk)

        def emit(out_ref, kept, left_ref, tail):
            grams = [
                dot(left_ref[g * GROUP : (g + 1) * GROUP, :], slot[g], 1, 1).astype(jnp.bfloat16)
                for g in range(groups)
            ]
            terms = [dot(gram, tail, 1, 1) for gram in grams]
            parts = []
            for g in range(groups):
                for b in range(GROUP // extent):
                    pair = b // mats * mats * extent
                    piece = terms[g][b * extent : (b + 1) * extent, pair : pair + mats * extent]
                    parts.append(jnp.where(m == b % mats, piece, pltpu.roll(piece, extent, 1)))
            placed = jnp.concatenate(parts, axis=0)
            both = jnp.where(lane_mat == m, placed, kept[chunk_rows, :])
            kept[chunk_rows, :] = both
            out_ref[...] = both.astype(jnp.bfloat16)

        @pl.when(phase == 0)
        def _():
            own = side_ref[0] * half_rows + at * half_chunk
            other = (1 - side_ref[0]) * half_rows + at * half_chunk
            za[pl.ds(pl.multiple_of(other, half_chunk), half_chunk), :] = jnp.zeros((half_chunk, count), jnp.float32)
            for g in range(half_chunk // GROUP):
                piece = pulled_ref[g * GROUP : (g + 1) * GROUP, :]
                za[pl.ds(pl.multiple_of(own + g * GROUP, GROUP), GROUP), :] = dot(heads_ref[0], piece, 1, 0)

        @pl.when(phase == 1)
        def _():
            for g in range(groups):
                collect(moves_ref, (at * groups + g) * tiles, za, slot.at[g])
            emit(terms_0_ref, kept_0, mid_ref, tails_ref[0])
            for g in range(groups):
                merged = merged_ref[g * GROUP : (g + 1) * GROUP, :]
                zb[pl.ds(at * chunk + g * GROUP, GROUP), :] = dot(merged, slot[g], 1, 0)

        @pl.when(phase == 2)
        def _():
            for g in range(groups):
                collect(moves_ref, all_tiles + (at * groups + g) * tiles, zb, slot.at[g])
            emit(terms_1_ref, kept_1, top_ref, tails_ref[1])

    out = jax.ShapeDtypeStruct((width, mats * extent), jnp.bfloat16)
    whole = lambda m, phase, at: (0, 0, 0)
    return pl.pallas_call(
        body,
        out_shape=(out, out),
        grid=(mats, 3, STEPS),
        in_specs=[
            pl.BlockSpec(memory_space=pltpu.SMEM),
            pl.BlockSpec(memory_space=pltpu.SMEM),
            pl.BlockSpec((half_chunk, count), lambda m, phase, at: (clamp(phase, 0, at, last), m)),
            pl.BlockSpec((chunk, count), lambda m, phase, at: (clamp(phase, 1, at, last), m)),
            pl.BlockSpec((chunk, count), lambda m, phase, at: (clamp(phase, 2, at, last), 0)),
            pl.BlockSpec((None, chunk, GROUP), lambda m, phase, at: (m, clamp(phase, 1, at, last), 0)),
            pl.BlockSpec((1, GROUP, GROUP), whole),
            pl.BlockSpec((2, GROUP, GROUP), whole),
        ],
        out_specs=(
            pl.BlockSpec((chunk, mats * extent), lambda m, phase, at: (jnp.where(m == mats - 1, clamp(phase, 1, at, last), 0), 0)),
            pl.BlockSpec((chunk, mats * extent), lambda m, phase, at: (jnp.where(m == mats - 1, clamp(phase, 2, at, last), 0), 0)),
        ),
        scratch_shapes=[
            pltpu.VMEM((width, count), jnp.float32),
            pltpu.VMEM((width, count), jnp.float32),
            pltpu.VMEM((groups, GROUP, count), jnp.bfloat16),
            pltpu.VMEM((width, mats * extent), jnp.float32),
            pltpu.VMEM((width, mats * extent), jnp.float32),
        ],
        compiler_params=pltpu.CompilerParams(vmem_limit_bytes=52 << 20),
        cost_estimate=estimate(14 * 2 * width * GROUP * count, pulled, mid, top, merged, out, out),
        name="block_terms",
    )(moves, side, pulled, mid, top, merged, heads, tails)


def pull(gate_cols, up_cols, gate_grad, up_grad):
    rows, width = gate_cols.shape
    count = gate_grad.shape[0]
    step = min(512, rows)

    def body(gate_ref, up_ref, gate_grad_ref, up_grad_ref, out_ref):
        out_ref[:, :count] = dot(gate_ref[...], gate_grad_ref[...], 1, 1).astype(jnp.bfloat16)
        out_ref[:, count:] = dot(up_ref[...], up_grad_ref[...], 1, 1).astype(jnp.bfloat16)

    out = jax.ShapeDtypeStruct((rows, 2 * count), jnp.bfloat16)
    weights = pl.BlockSpec((step, width), lambda at: (at, 0))
    grads = pl.BlockSpec((count, width), lambda at: (0, 0))
    return pl.pallas_call(
        body,
        out_shape=out,
        grid=(rows // step,),
        in_specs=[weights, weights, grads, grads],
        out_specs=pl.BlockSpec((step, 2 * count), lambda at: (at, 0)),
        cost_estimate=estimate(4 * rows * width * count, gate_cols, up_cols, out),
        name="pull",
    )(gate_cols, up_cols, gate_grad, up_grad)


def places_of(bits, section_row):
    places = jnp.arange(section_row.shape[0], dtype=jnp.int32)
    found = bits[:, None] == section_row[None, :]
    return jnp.sum(jnp.where(found, places[None, :], 0), axis=1)


def shards(tokens, gate_weight, up_weight, skew_params, section_bits, upstream):
    mats, _, own_blocks, extent, _ = skew_params.shape
    own_rows = gate_weight.shape[0]
    own_cols = upstream.shape[1]
    devices = gate_weight.shape[1] // own_cols
    half = devices // 2
    half_rows = half * own_rows
    side = lax.axis_index("rows") // half
    groups = [list(range(half)), list(range(half, devices))]
    swap = [(at, (at + half) % devices) for at in range(devices)]

    def move(parts):
        moved = lax.all_to_all(
            parts, "rows", split_axis=0, concat_axis=0, axis_index_groups=groups, tiled=True
        )
        return moved.reshape(half_rows, 2 * own_cols)

    bits_0, bits_1 = section_bits[0], section_bits[1]
    natural = jnp.arange(bits_0.shape[0], dtype=jnp.int32)
    inverse_0 = places_of(natural, bits_0)
    one_to_zero = places_of(bits_0, bits_1)
    zero_to_one = places_of(bits_1, bits_0)
    heads, tails, moves = routes(jnp.stack([bits_1, one_to_zero, inverse_0, bits_0, zero_to_one]))
    side_at = jnp.reshape(side, (1,)).astype(jnp.int32)

    skew_params, gate_parts = lax.optimization_barrier((skew_params, pack(gate_weight, half, own_cols)))
    gate_cols = move(gate_parts)
    other_upstream = lax.ppermute(upstream, "rows", swap)
    inverse = cayley_inverse(skew_params)
    own_rotation = (2.0 * inverse - jnp.eye(extent, dtype=jnp.float32)).astype(jnp.bfloat16)
    packed = own_rotation.transpose(2, 3, 1, 0, 4).reshape(own_blocks * extent, -1)
    up_weight, packed = lax.optimization_barrier((up_weight, packed))
    packed, up_parts = lax.optimization_barrier((packed, pack(up_weight, half, own_cols)))
    all_tokens, rotation = gather_blocks((tokens, packed), devices)
    all_tokens, gate_cols, up_parts, other_upstream = lax.optimization_barrier(
        (all_tokens, gate_cols, up_parts, other_upstream)
    )
    up_cols = move(up_parts)
    all_tokens = all_tokens.reshape(-1, tokens.shape[1])
    rotation = rotation.reshape(devices * own_blocks * extent, -1)
    token_count = all_tokens.shape[0]
    top_tokens, mid, low = rotate_tokens(
        all_tokens, rotation, heads[:3], tails[:3], moves[:3].reshape(-1), side_at, extent, mats
    )
    rotation, low = lax.optimization_barrier((rotation, low))
    merged = merge_blocks(rotation, heads[4], tails[3], extent, mats)

    def project(at, columns):
        part = dot(low[:, at * token_count : (at + 1) * token_count], columns, 0, 0)
        return part + lax.ppermute(part.astype(jnp.bfloat16), "rows", swap).astype(jnp.float32)

    gate_pre = project(0, gate_cols)
    up_pre = project(1, up_cols)
    sigmoid_val = jax.nn.sigmoid(gate_pre)
    silu_val = gate_pre * sigmoid_val
    activation = (silu_val * up_pre).astype(jnp.bfloat16)
    activation = jnp.where(side == 0, activation[:, :own_cols], activation[:, own_cols:])
    first = jnp.where(side == 0, upstream, other_upstream)
    second = jnp.where(side == 0, other_upstream, upstream)
    cotangent = jnp.concatenate([first, second], axis=1).astype(jnp.float32)
    gate_grad = (cotangent * up_pre * sigmoid_val * (1.0 + gate_pre * (1.0 - sigmoid_val))).astype(
        jnp.bfloat16
    )
    up_grad = (cotangent * silu_val).astype(jnp.bfloat16)

    pulled = pull(gate_cols, up_cols, gate_grad, up_grad)
    terms_0, terms_1 = block_terms(
        pulled, mid, top_tokens, merged, heads[3:4], tails[3:], moves[3:].reshape(-1), side_at, extent, mats
    )

    def ordered(summed):
        return summed.reshape(own_blocks, extent, mats, extent).transpose(2, 0, 1, 3)

    by_owner = (devices, own_blocks * extent, mats * extent)
    summed = reduce_blocks((terms_0.reshape(by_owner), terms_1.reshape(by_owner)), devices)
    factor_grad = jnp.stack([ordered(summed[0]), ordered(summed[1])], axis=1)

    left = jnp.einsum(
        "mskab,mskac->mskbc", inverse, factor_grad, precision=lax.Precision.HIGHEST
    )
    generator_grad = -2.0 * jnp.einsum(
        "mskbc,mskdc->mskbd", left, inverse, precision=lax.Precision.HIGHEST
    )
    skew_grad = generator_grad - jnp.swapaxes(generator_grad, -1, -2)
    return (activation, skew_grad)


def solution(mesh):
    placed = (
        P(("groups", "rows"), None),
        P("rows", None),
        P("rows", None),
        P(None, None, "rows", None, None),
        P(),
        P("groups", "rows"),
    )
    return jax.shard_map(
        shards,
        mesh=mesh,
        in_specs=placed,
        out_specs=(P("groups", "rows"), P("groups", None, "rows", None, None)),
        check_vma=False,
    )
```

```python
import jax
import jax.numpy as jnp
from jax import lax
from jax.experimental import pallas as pl
from jax.experimental.pallas import tpu as pltpu
from jax.sharding import PartitionSpec as P


def inverse_kernel(skew_ref, out_ref):
    extent = skew_ref.shape[-1]
    shape = skew_ref.shape
    row_at = lax.broadcasted_iota(jnp.int32, shape, 1)
    col_at = lax.broadcasted_iota(jnp.int32, shape, 2)
    skew = skew_ref[...]
    generator = skew - jnp.swapaxes(skew, 1, 2)
    out_ref[...] = jnp.where(row_at == col_at, 1.0, 0.0) + generator
    lane = lax.broadcasted_iota(jnp.int32, (shape[0], 1, extent), 2)

    def step(at, carry):
        work = out_ref[...]
        pivot_row = out_ref[:, pl.ds(at, 1), :]
        at_col = col_at == at
        pivot_col = jnp.sum(jnp.where(at_col, work, 0.0), axis=2, keepdims=True)
        pivot = jnp.sum(jnp.where(lane == at, pivot_row, 0.0), axis=2, keepdims=True)
        scale = 1.0 / pivot
        scaled_row = jnp.where(lane == at, 1.0, pivot_row) * scale
        cleared = jnp.where(at_col, 0.0, work)
        out_ref[...] = cleared - pivot_col * scaled_row
        out_ref[:, pl.ds(at, 1), :] = scaled_row
        return carry

    lax.fori_loop(0, extent, step, 0)


def cayley_inverse(skew_blocks):
    extent = skew_blocks.shape[-1]
    flat = skew_blocks.reshape(-1, extent, extent)
    out = pl.pallas_call(
        inverse_kernel,
        out_shape=jax.ShapeDtypeStruct(flat.shape, jnp.float32),
        in_specs=[pl.BlockSpec(memory_space=pltpu.VMEM)],
        out_specs=pl.BlockSpec(memory_space=pltpu.VMEM),
        cost_estimate=pl.CostEstimate(
            flops=50_000_000, bytes_accessed=2 * 4 * flat.size, transcendentals=0
        ),
        name="cayley_inverse",
    )(flat)
    return out.reshape(skew_blocks.shape)


def estimate(flops, *arrays):
    moved = sum(array.size * array.dtype.itemsize for array in arrays)
    return pl.CostEstimate(flops=flops, bytes_accessed=moved, transcendentals=0)


def pack(weight, half, cols):
    rows, width = weight.shape
    step = min(rows, 32)

    def body(in_ref, out_ref):
        for at in range(half):
            left = in_ref[:, at * cols : (at + 1) * cols]
            right = in_ref[:, (half + at) * cols : (half + at + 1) * cols]
            out_ref[at] = jnp.concatenate([left, right], axis=1)

    out = jax.ShapeDtypeStruct((half, rows, 2 * cols), weight.dtype)
    return pl.pallas_call(
        body,
        out_shape=out,
        grid=(rows // step,),
        in_specs=[pl.BlockSpec((step, width), lambda at: (at, 0))],
        out_specs=pl.BlockSpec((half, step, 2 * cols), lambda at: (0, at, 0)),
        cost_estimate=estimate(0, weight, out),
        name="pack",
    )(weight)


def dot(left, right, left_dim, right_dim):
    contract = (((left_dim,), (right_dim,)), ((), ()))
    return lax.dot_general(left, right, contract, preferred_element_type=jnp.float32)


def routes(places):
    count, digits = places.shape
    low = GROUP_BITS
    at = jnp.arange(digits, dtype=jnp.int32)
    hit = places[:, :, None] == at[None, None, :]
    slot_of = jnp.sum(jnp.where(hit, at[None, :, None], 0), axis=1)
    is_low = at[None, :] < low
    crosses = is_low != (slot_of < low)
    before = at[:, None] < at[None, :]
    same = (at[:, None] < low) == (at[None, :] < low)
    rank_cross = jnp.sum((crosses[:, :, None] & (before & same)[None]).astype(jnp.int32), axis=1)
    rank_stay = jnp.sum((~crosses[:, :, None] & (before & same)[None]).astype(jnp.int32), axis=1)
    inside = jnp.where(crosses, low - 1 - rank_cross, rank_stay)
    first = jnp.where(is_low, inside, at[None, :])
    second = jnp.where(is_low & ~crosses, inside, slot_of)
    second = jnp.where(~is_low & crosses, low - 1 - rank_cross, second)
    after = jnp.sum(jnp.where(hit, second[:, None, :], 0), axis=2)

    def spread(index, sources, targets):
        bits = jnp.right_shift(index[None, :, None], sources[:, None, :]) & 1
        return jnp.sum(jnp.left_shift(bits, targets[:, None, :]), axis=2)

    group = jnp.arange(1 << low, dtype=jnp.int32)
    natural = jnp.broadcast_to(at[None, :], (count, digits))
    take_first = spread(group, first[:, :low], natural[:, :low])
    take_last = spread(group, natural[:, :low], after[:, :low])
    tiles = jnp.arange((1 << digits) // TILE, dtype=jnp.int32) * TILE
    moves = spread(tiles, second, first)
    heads = (take_first[:, :, None] == group[None, None, :]).astype(jnp.bfloat16)
    tails = (take_last[:, :, None] == group[None, None, :]).astype(jnp.bfloat16)
    return heads, tails, moves


GROUP_BITS = 8
GROUP = 1 << GROUP_BITS
TILE = 8
STEPS = 8


def collect(moves_ref, base, source_ref, slot_ref):
    for pair in range(GROUP // (2 * TILE)):
        parts = []
        for half in range(2):
            start = pl.multiple_of(moves_ref[base + 2 * pair + half], TILE)
            parts.append(source_ref[pl.ds(start, TILE), :])
        rows = slice(2 * TILE * pair, 2 * TILE * (pair + 1))
        slot_ref[rows, :] = jnp.concatenate(parts, axis=0).astype(jnp.bfloat16)


def flipped(index, bit):
    return index + (1 - 2 * ((index // (1 << bit)) % 2)) * (1 << bit)


def greet(bits):
    me = lax.axis_index("rows")
    barrier = pltpu.get_barrier_semaphore()
    for bit in range(bits):
        pl.semaphore_signal(
            barrier, inc=1, device_id={"rows": flipped(me, bit)}, device_id_type=pl.DeviceIdType.MESH
        )
    pl.semaphore_wait(barrier, bits)
    return me


def bit_orders(devices):
    down = list(reversed(range(devices.bit_length() - 1)))
    return [down, down[:-3] + [down[-2], down[-3], down[-1]]]


def gather_blocks(arrays, devices):
    bits = devices.bit_length() - 1
    down = list(reversed(range(bits)))
    high, (far, near, core) = down[:-3], down[-3:]
    orders = [high + [far, near, core], high + [near, far, core], [near, far] + high + [core], [far, near] + high + [core]]
    count = len(arrays)
    streams = [(at, color) for color in range(4) for at in range(count)]

    def kernel(*refs):
        own_refs, out_refs = refs[:count], refs[count : 2 * count]
        send_sem, recv_sem, local_sem = refs[2 * count :]
        me = greet(bits)
        locals_ = []
        for at in range(count):
            local = pltpu.make_async_copy(own_refs[at], out_refs[at].at[me], local_sem.at[at])
            local.start()
            locals_.append(local)

        def part(at, color):
            rows, lanes = arrays[at].shape
            extent = rows if rows % 64 == 0 else lanes
            eighths = (0, 3, 6, 7, 8) if extent % 128 == 0 else (0, 2, 4, 6, 8)
            begin, end = (extent * eighths[color + at] // 8 for at in range(2))
            if extent == rows:
                return (pl.ds(begin, end - begin), slice(None))
            return (slice(None), pl.ds(begin, end - begin))

        def copy(stream, step, pattern):
            at, color = streams[stream]
            order = orders[color]
            block = me
            for level in range(step):
                if (pattern >> level) & 1:
                    block = flipped(block, order[level])
            piece = part(at, color)
            source = own_refs[at].at[piece] if pattern == 0 else out_refs[at].at[(block,) + piece]
            slot = pattern + (1 << step) - 1
            return pltpu.make_async_remote_copy(
                src_ref=source,
                dst_ref=out_refs[at].at[(block,) + piece],
                send_sem=send_sem.at[stream, slot],
                recv_sem=recv_sem.at[stream, slot],
                device_id={"rows": flipped(me, order[step])},
                device_id_type=pl.DeviceIdType.MESH,
            )

        copies = {}
        arrived = set()

        def arrive(stream, pattern):
            if pattern and (stream, pattern) not in arrived:
                arrived.add((stream, pattern))
                copies[stream, pattern].wait_recv()

        for step in range(bits):
            for pattern in range(1 << step):
                for stream in range(len(streams)):
                    arrive(stream, pattern)
                    made = copy(stream, step, pattern)
                    made.start()
                    copies[stream, pattern + (1 << step)] = made
        for pattern in range(1, devices):
            for stream in range(len(streams)):
                arrive(stream, pattern)
        for made in copies.values():
            made.wait_send()
        for local in locals_:
            local.wait()

    outs = tuple(jax.ShapeDtypeStruct((devices,) + own.shape, own.dtype) for own in arrays)
    anywhere = pl.BlockSpec(memory_space=pl.ANY)
    return pl.pallas_call(
        kernel,
        out_shape=outs,
        in_specs=[anywhere] * count,
        out_specs=(anywhere,) * count,
        scratch_shapes=[
            pltpu.SemaphoreType.DMA((4 * count, devices - 1)),
            pltpu.SemaphoreType.DMA((4 * count, devices - 1)),
            pltpu.SemaphoreType.DMA((count,)),
        ],
        compiler_params=pltpu.CompilerParams(collective_id=0, has_side_effects=True),
        cost_estimate=pl.CostEstimate(
            flops=0, bytes_accessed=32 * sum(2 * out.size for out in outs), transcendentals=0
        ),
        name="gather_blocks",
    )(*arrays)


def reduce_blocks(arrays, devices):
    _, rows, lanes = arrays[0].shape
    bits = devices.bit_length() - 1
    count = len(arrays)
    orders = [list(reversed(order)) for order in bit_orders(devices)]

    def kernel(*refs):
        in_refs = refs[:count]
        out_ref, acc, landed, send_sem, recv_sem = refs[count:]
        me = greet(bits)
        copies = {}

        def block_of(at, step, pattern, index):
            order = orders[at % 2]
            for level in range(step + 1, bits):
                if (pattern >> (level - step - 1)) & 1:
                    index = flipped(index, order[level])
            return index

        def send(at, step, pattern):
            other = flipped(me, orders[at % 2][step])
            if step == 0:
                source = in_refs[at].at[block_of(at, 0, pattern, other)]
            else:
                source = acc.at[at, (2 * pattern + 1) << (step - 1)]
            slot = (devices >> (step + 1)) + pattern - 1
            made = pltpu.make_async_remote_copy(
                src_ref=source,
                dst_ref=landed.at[at, slot],
                send_sem=send_sem.at[at, slot],
                recv_sem=recv_sem.at[at, slot],
                device_id={"rows": other},
                device_id_type=pl.DeviceIdType.MESH,
            )
            made.start()
            copies[at, step, pattern] = made

        def arrive(at, step, pattern):
            copies[at, step, pattern].wait_recv()
            slot = (devices >> (step + 1)) + pattern - 1
            if step == 0:
                kept = in_refs[at][block_of(at, 0, pattern, me)]
            else:
                kept = acc[at, (2 * pattern) << (step - 1)]
            total = kept.astype(jnp.float32) + landed[at, slot].astype(jnp.float32)
            if step == bits - 1:
                out_ref[at] = total
            else:
                acc[at, pattern << step] = total.astype(jnp.bfloat16)

        for pattern in [p for odd in (1, 0) for p in range(devices // 2) if p % 2 == odd]:
            for at in range(count):
                send(at, 0, pattern)
        for step in range(1, bits + 1):
            patterns = devices >> step
            for pattern in [p for odd in (1, 0) for p in range(patterns) if p % 2 == odd]:
                for at in range(count):
                    arrive(at, step - 1, pattern)
                    if step < bits and pattern % 2:
                        send(at, step, pattern // 2)
        for made in copies.values():
            made.wait_send()

    return pl.pallas_call(
        kernel,
        out_shape=jax.ShapeDtypeStruct((count, rows, lanes), jnp.float32),
        in_specs=[pl.BlockSpec(memory_space=pltpu.VMEM)] * count,
        out_specs=pl.BlockSpec(memory_space=pltpu.VMEM),
        scratch_shapes=[
            pltpu.VMEM((count, devices // 2, rows, lanes), jnp.bfloat16),
            pltpu.VMEM((count, devices - 1, rows, lanes), jnp.bfloat16),
            pltpu.SemaphoreType.DMA((count, devices - 1)),
            pltpu.SemaphoreType.DMA((count, devices - 1)),
        ],
        compiler_params=pltpu.CompilerParams(
            collective_id=1, has_side_effects=True, vmem_limit_bytes=32 << 20
        ),
        cost_estimate=pl.CostEstimate(flops=0, bytes_accessed=64 * arrays[0].size, transcendentals=0),
        name="reduce_blocks",
    )(*arrays)


def clamp(phase, wanted, at, last):
    return jnp.where(phase < wanted, 0, jnp.where(phase > wanted, last, at))


def rotate_tokens(all_tokens, rotation, heads, tails, moves, side, extent, mats):
    count, width = all_tokens.shape
    chunk = width // STEPS
    groups = chunk // GROUP
    tiles = GROUP // TILE
    all_tiles = width // TILE
    half_rows = width // 2
    half_chunk = half_rows // STEPS
    last = STEPS - 1

    def body(moves_ref, side_ref, tok_ref, rot_ref, heads_ref, tails_ref, top_ref, mid_ref, low_ref, za, *rest):
        mixed_refs, slot = rest[:mats], rest[mats]
        phase, at = pl.program_id(0), pl.program_id(1)

        block_row = lax.broadcasted_iota(jnp.int32, (GROUP, GROUP), 0) // extent
        block_col = lax.broadcasted_iota(jnp.int32, (GROUP, GROUP), 1) // extent
        same_block = block_row == block_col

        def turned(values, section, m):
            blocks = []
            first = (section * mats + m) * extent
            for g in range(groups):
                own = rot_ref[g * GROUP : (g + 1) * GROUP, first : first + extent]
                tiled = jnp.concatenate([own] * (GROUP // extent), axis=1)
                blocks.append(jnp.where(same_block, tiled, jnp.zeros_like(tiled)))
            return [dot(block, value, 0, 0).astype(jnp.bfloat16) for block, value in zip(blocks, values)]

        def stage(base, source, out_ref, perm, section, targets):
            for g in range(groups):
                collect(moves_ref, base + (at * groups + g) * tiles, source, slot.at[g])
            values = [dot(tails_ref[perm], slot[g], 1, 0).astype(jnp.bfloat16) for g in range(groups)]
            for g in range(groups):
                out_ref[g * GROUP : (g + 1) * GROUP, :] = values[g]
            for m, target in targets:
                mixed = turned(values, section, m)
                for g in range(groups):
                    target[pl.ds(at * chunk + g * GROUP, GROUP), :] = dot(heads_ref[perm + 1], mixed[g], 1, 0)

        @pl.when(phase == 0)
        def _():
            for g in range(groups):
                piece = tok_ref[:, g * GROUP : (g + 1) * GROUP]
                za[pl.ds(at * chunk + g * GROUP, GROUP), :] = dot(heads_ref[0], piece, 1, 1)

        @pl.when(phase == 1)
        def _():
            stage(0, za, top_ref, 0, 1, list(enumerate(mixed_refs)))

        for m in range(mats):

            @pl.when(phase == 2 + 2 * m)
            def _(m=m):
                stage(all_tiles, mixed_refs[m], mid_ref, 1, 0, [(m, za)])

            @pl.when(phase == 3 + 2 * m)
            def _():
                low_groups = half_chunk // GROUP
                for g in range(low_groups):
                    at_group = side_ref[0] * (half_rows // GROUP) + at * low_groups + g
                    collect(moves_ref, 2 * all_tiles + at_group * tiles, za, slot.at[g])
                for g in range(low_groups):
                    value = dot(tails_ref[2], slot[g], 1, 0)
                    low_ref[g * GROUP : (g + 1) * GROUP, :] = value.astype(jnp.bfloat16)

    outs = (
        jax.ShapeDtypeStruct((width, count), jnp.bfloat16),
        jax.ShapeDtypeStruct((width, mats * count), jnp.bfloat16),
        jax.ShapeDtypeStruct((half_rows, mats * count), jnp.bfloat16),
    )
    whole = lambda phase, at: (0, 0, 0)

    def rows_of(first):
        def place(phase, at):
            turn = (phase - first) // 2
            row = jnp.where(phase < first, 0, jnp.where((phase - first) % 2 == 0, at, last))
            return (row, jnp.where(phase < first, 0, turn))

        return place

    return pl.pallas_call(
        body,
        out_shape=outs,
        grid=(2 + 2 * mats, STEPS),
        in_specs=[
            pl.BlockSpec(memory_space=pltpu.SMEM),
            pl.BlockSpec(memory_space=pltpu.SMEM),
            pl.BlockSpec((count, chunk), lambda phase, at: (0, jnp.where(phase == 0, at, last))),
            pl.BlockSpec(
                (chunk, rotation.shape[1]),
                lambda phase, at: (jnp.where((phase == 1) | ((phase > 0) & (phase % 2 == 0)), at, jnp.where(phase == 0, 0, last)), 0),
            ),
            pl.BlockSpec((3, GROUP, GROUP), whole),
            pl.BlockSpec((3, GROUP, GROUP), whole),
        ],
        out_specs=(
            pl.BlockSpec((chunk, count), lambda phase, at: (clamp(phase, 1, at, last), 0)),
            pl.BlockSpec((chunk, count), rows_of(2)),
            pl.BlockSpec((half_chunk, count), rows_of(3)),
        ),
        scratch_shapes=[
            *[pltpu.VMEM((width, count), jnp.float32) for _ in range(1 + mats)],
            pltpu.VMEM((groups, GROUP, count), jnp.bfloat16),
        ],
        compiler_params=pltpu.CompilerParams(vmem_limit_bytes=56 << 20),
        cost_estimate=estimate(14 * 2 * width * GROUP * count, all_tokens, rotation, *outs),
        name="rotate_tokens",
    )(moves, side, all_tokens, rotation, heads, tails)


def merge_blocks(rotation, head, tail, extent, mats):
    width = rotation.shape[0]
    chunk = width // STEPS

    def body(rot_ref, head_ref, tail_ref, out_ref):
        m = pl.program_id(1)
        block_row = lax.broadcasted_iota(jnp.int32, (GROUP, GROUP), 0) // extent
        block_col = lax.broadcasted_iota(jnp.int32, (GROUP, GROUP), 1) // extent
        same_block = block_row == block_col
        merged = []
        for g in range(chunk // GROUP):
            both = rot_ref[g * GROUP : (g + 1) * GROUP, : mats * extent]
            own = jnp.where(m == 0, both[:, :extent], both[:, extent:])
            tiled = jnp.concatenate([own] * (GROUP // extent), axis=1)
            block = jnp.where(same_block, tiled, jnp.zeros_like(tiled))
            merged.append(dot(block, tail_ref[...], 1, 0).astype(jnp.bfloat16))
        for g, value in enumerate(merged):
            out_ref[g * GROUP : (g + 1) * GROUP, :] = dot(head_ref[...], value, 1, 0).astype(jnp.bfloat16)

    out = jax.ShapeDtypeStruct((mats, width, GROUP), jnp.bfloat16)
    whole = pl.BlockSpec((GROUP, GROUP), lambda at, m: (0, 0))
    return pl.pallas_call(
        body,
        out_shape=out,
        grid=(STEPS, mats),
        in_specs=[pl.BlockSpec((chunk, rotation.shape[1]), lambda at, m: (at, 0)), whole, whole],
        out_specs=pl.BlockSpec((None, chunk, GROUP), lambda at, m: (m, at, 0)),
        compiler_params=pltpu.CompilerParams(vmem_limit_bytes=16 << 20),
        cost_estimate=estimate(8 * width * GROUP * GROUP, rotation, out),
        name="merge_blocks",
    )(rotation, head, tail)


def block_terms(gate_cols, up_cols, gate_grad, up_grad, mid, top, merged, heads, tails, moves, side, extent, mats):
    half_rows, cols = gate_cols.shape
    width, count = top.shape
    chunk = width // STEPS
    groups = chunk // GROUP
    tiles = GROUP // TILE
    all_tiles = width // TILE
    half_chunk = half_rows // STEPS
    last = STEPS - 1

    def body(moves_ref, side_ref, gate_ref, up_ref, gate_grad_ref, up_grad_ref, mid_ref, top_ref, merged_ref, heads_ref, tails_ref, terms_0_ref, terms_1_ref, za, zb, slot, kept_0, kept_1):
        m, phase, at = pl.program_id(0), pl.program_id(1), pl.program_id(2)
        lane_mat = lax.broadcasted_iota(jnp.int32, (chunk, mats * extent), 1) // extent
        chunk_rows = pl.ds(pl.multiple_of(at * chunk, chunk), chunk)

        def emit(out_ref, kept, left_ref, tail):
            grams = [
                dot(left_ref[g * GROUP : (g + 1) * GROUP, :], slot[g], 1, 1).astype(jnp.bfloat16)
                for g in range(groups)
            ]
            terms = [dot(gram, tail, 1, 1) for gram in grams]
            parts = []
            for g in range(groups):
                for b in range(GROUP // extent):
                    pair = b // mats * mats * extent
                    piece = terms[g][b * extent : (b + 1) * extent, pair : pair + mats * extent]
                    parts.append(jnp.where(m == b % mats, piece, pltpu.roll(piece, extent, 1)))
            placed = jnp.concatenate(parts, axis=0)
            both = jnp.where(lane_mat == m, placed, kept[chunk_rows, :])
            kept[chunk_rows, :] = both
            out_ref[...] = both.astype(jnp.bfloat16)

        for own_mat, cols_ref, grad_ref in ((0, gate_ref, gate_grad_ref), (1, up_ref, up_grad_ref)):

            @pl.when((phase == 0) & (m == own_mat))
            def _(cols_ref=cols_ref, grad_ref=grad_ref):
                own = side_ref[0] * half_rows + at * half_chunk
                other = (1 - side_ref[0]) * half_rows + at * half_chunk
                za[pl.ds(pl.multiple_of(other, half_chunk), half_chunk), :] = jnp.zeros((half_chunk, count), jnp.float32)
                pulled = dot(cols_ref[...], grad_ref[...], 1, 1).astype(jnp.bfloat16)
                for g in range(half_chunk // GROUP):
                    piece = pulled[g * GROUP : (g + 1) * GROUP, :]
                    za[pl.ds(pl.multiple_of(own + g * GROUP, GROUP), GROUP), :] = dot(heads_ref[0], piece, 1, 0)

        @pl.when(phase == 1)
        def _():
            for g in range(groups):
                collect(moves_ref, (at * groups + g) * tiles, za, slot.at[g])
            emit(terms_0_ref, kept_0, mid_ref, tails_ref[0])
            for g in range(groups):
                merged = merged_ref[g * GROUP : (g + 1) * GROUP, :]
                zb[pl.ds(at * chunk + g * GROUP, GROUP), :] = dot(merged, slot[g], 1, 0)

        @pl.when(phase == 2)
        def _():
            for g in range(groups):
                collect(moves_ref, all_tiles + (at * groups + g) * tiles, zb, slot.at[g])
            emit(terms_1_ref, kept_1, top_ref, tails_ref[1])

    out = jax.ShapeDtypeStruct((width, mats * extent), jnp.bfloat16)
    whole = lambda m, phase, at: (0, 0, 0)
    return pl.pallas_call(
        body,
        out_shape=(out, out),
        grid=(mats, 3, STEPS),
        in_specs=[
            pl.BlockSpec(memory_space=pltpu.SMEM),
            pl.BlockSpec(memory_space=pltpu.SMEM),
            pl.BlockSpec((half_chunk, cols), lambda m, phase, at: (jnp.where(m == 0, clamp(phase, 0, at, last), last), 0)),
            pl.BlockSpec((half_chunk, cols), lambda m, phase, at: (jnp.where(m == 0, 0, clamp(phase, 0, at, last)), 0)),
            pl.BlockSpec((count, cols), lambda m, phase, at: (0, 0)),
            pl.BlockSpec((count, cols), lambda m, phase, at: (0, 0)),
            pl.BlockSpec((chunk, count), lambda m, phase, at: (clamp(phase, 1, at, last), m)),
            pl.BlockSpec((chunk, count), lambda m, phase, at: (clamp(phase, 2, at, last), 0)),
            pl.BlockSpec((None, chunk, GROUP), lambda m, phase, at: (m, clamp(phase, 1, at, last), 0)),
            pl.BlockSpec((1, GROUP, GROUP), whole),
            pl.BlockSpec((2, GROUP, GROUP), whole),
        ],
        out_specs=(
            pl.BlockSpec((chunk, mats * extent), lambda m, phase, at: (jnp.where(m == mats - 1, clamp(phase, 1, at, last), 0), 0)),
            pl.BlockSpec((chunk, mats * extent), lambda m, phase, at: (jnp.where(m == mats - 1, clamp(phase, 2, at, last), 0), 0)),
        ),
        scratch_shapes=[
            pltpu.VMEM((width, count), jnp.float32),
            pltpu.VMEM((width, count), jnp.float32),
            pltpu.VMEM((groups, GROUP, count), jnp.bfloat16),
            pltpu.VMEM((width, mats * extent), jnp.float32),
            pltpu.VMEM((width, mats * extent), jnp.float32),
        ],
        compiler_params=pltpu.CompilerParams(vmem_limit_bytes=56 << 20),
        cost_estimate=estimate(14 * 2 * width * GROUP * count, gate_cols, up_cols, mid, top, merged, out, out),
        name="block_terms",
    )(moves, side, gate_cols, up_cols, gate_grad, up_grad, mid, top, merged, heads, tails)


def places_of(bits, section_row):
    places = jnp.arange(section_row.shape[0], dtype=jnp.int32)
    found = bits[:, None] == section_row[None, :]
    return jnp.sum(jnp.where(found, places[None, :], 0), axis=1)


def shards(tokens, gate_weight, up_weight, skew_params, section_bits, upstream):
    mats, _, own_blocks, extent, _ = skew_params.shape
    own_rows = gate_weight.shape[0]
    own_cols = upstream.shape[1]
    devices = gate_weight.shape[1] // own_cols
    half = devices // 2
    half_rows = half * own_rows
    side = lax.axis_index("rows") // half
    groups = [list(range(half)), list(range(half, devices))]
    swap = [(at, (at + half) % devices) for at in range(devices)]

    def move(parts):
        moved = lax.all_to_all(
            parts, "rows", split_axis=0, concat_axis=0, axis_index_groups=groups, tiled=True
        )
        return moved.reshape(half_rows, 2 * own_cols)

    bits_0, bits_1 = section_bits[0], section_bits[1]
    natural = jnp.arange(bits_0.shape[0], dtype=jnp.int32)
    inverse_0 = places_of(natural, bits_0)
    one_to_zero = places_of(bits_0, bits_1)
    zero_to_one = places_of(bits_1, bits_0)
    heads, tails, moves = routes(jnp.stack([bits_1, one_to_zero, inverse_0, bits_0, zero_to_one]))
    side_at = jnp.reshape(side, (1,)).astype(jnp.int32)

    skew_params, gate_parts = lax.optimization_barrier((skew_params, pack(gate_weight, half, own_cols)))
    gate_cols = move(gate_parts)
    other_upstream = lax.ppermute(upstream, "rows", swap)
    inverse = cayley_inverse(skew_params)
    own_rotation = (2.0 * inverse - jnp.eye(extent, dtype=jnp.float32)).astype(jnp.bfloat16)
    packed = own_rotation.transpose(2, 3, 1, 0, 4).reshape(own_blocks * extent, -1)
    up_weight, packed = lax.optimization_barrier((up_weight, packed))
    packed, up_parts = lax.optimization_barrier((packed, pack(up_weight, half, own_cols)))
    all_tokens, rotation = gather_blocks((tokens, packed), devices)
    all_tokens, gate_cols, up_parts, other_upstream = lax.optimization_barrier(
        (all_tokens, gate_cols, up_parts, other_upstream)
    )
    up_cols = move(up_parts)
    all_tokens = all_tokens.reshape(-1, tokens.shape[1])
    rotation = rotation.reshape(devices * own_blocks * extent, -1)
    token_count = all_tokens.shape[0]
    top_tokens, mid, low = rotate_tokens(
        all_tokens, rotation, heads[:3], tails[:3], moves[:3].reshape(-1), side_at, extent, mats
    )
    rotation, low = lax.optimization_barrier((rotation, low))
    merged = merge_blocks(rotation, heads[4], tails[3], extent, mats)

    def project(at, columns):
        part = dot(low[:, at * token_count : (at + 1) * token_count], columns, 0, 0)
        return part + lax.ppermute(part.astype(jnp.bfloat16), "rows", swap).astype(jnp.float32)

    gate_pre = project(0, gate_cols)
    up_pre = project(1, up_cols)
    sigmoid_val = jax.nn.sigmoid(gate_pre)
    silu_val = gate_pre * sigmoid_val
    activation = (silu_val * up_pre).astype(jnp.bfloat16)
    activation = jnp.where(side == 0, activation[:, :own_cols], activation[:, own_cols:])
    first = jnp.where(side == 0, upstream, other_upstream)
    second = jnp.where(side == 0, other_upstream, upstream)
    cotangent = jnp.concatenate([first, second], axis=1).astype(jnp.float32)
    gate_grad = (cotangent * up_pre * sigmoid_val * (1.0 + gate_pre * (1.0 - sigmoid_val))).astype(
        jnp.bfloat16
    )
    up_grad = (cotangent * silu_val).astype(jnp.bfloat16)

    terms_0, terms_1 = block_terms(
        gate_cols, up_cols, gate_grad, up_grad, mid, top_tokens, merged, heads[3:4], tails[3:], moves[3:].reshape(-1), side_at, extent, mats
    )

    def ordered(summed):
        return summed.reshape(own_blocks, extent, mats, extent).transpose(2, 0, 1, 3)

    by_owner = (devices, own_blocks * extent, mats * extent)
    summed = reduce_blocks((terms_0.reshape(by_owner), terms_1.reshape(by_owner)), devices)
    factor_grad = jnp.stack([ordered(summed[0]), ordered(summed[1])], axis=1)

    left = jnp.einsum(
        "mskab,mskac->mskbc", inverse, factor_grad, precision=lax.Precision.HIGHEST
    )
    generator_grad = -2.0 * jnp.einsum(
        "mskbc,mskdc->mskbd", left, inverse, precision=lax.Precision.HIGHEST
    )
    skew_grad = generator_grad - jnp.swapaxes(generator_grad, -1, -2)
    return (activation, skew_grad)


def solution(mesh):
    placed = (
        P(("groups", "rows"), None),
        P("rows", None),
        P("rows", None),
        P(None, None, "rows", None, None),
        P(),
        P("groups", "rows"),
    )
    return jax.shard_map(
        shards,
        mesh=mesh,
        in_specs=placed,
        out_specs=(P("groups", "rows"), P("groups", None, "rows", None, None)),
        check_vma=False,
    )
```
